32 devices in a mesh: dp: 4 (over z), ctx: 4 (over y, core), tensor: 2 (over x).
Axes of the slice: x: 2, y: 2, z: 4, core: 2. Of those that a mesh axis runs over, the one named last changes fastest.
Arguments:
- inputs: bfloat16 [4, 1024, 2048], P('dp', 'ctx'), may hold values from -6 to 6
- segments: int32 [4, 1024], P('dp'), may hold values from 0 to 4, as said below
- first_gain: bfloat16 [2048], replicated, may hold values from 0.5 to 1.5
- first_shift: bfloat16 [2048], replicated, may hold values from -3 to 3
- in_weight: bfloat16 [2048, 3, 2048], P(None, None, 'tensor'), may hold values from -0.125 to 0.125
- in_bias: bfloat16 [2, 2048], P(None, 'tensor'), may hold values from -2 to 2
- out_weight: bfloat16 [2048, 2048], P(None, 'tensor'), may hold values from -1 to 1
- out_bias: bfloat16 [2048], replicated, may hold values from -2 to 2
- second_gain: bfloat16 [2048], replicated, may hold values from 0.5 to 1.5
- second_shift: bfloat16 [2048], replicated, may hold values from -3 to 3
- up_weight: bfloat16 [2048, 8192], P(None, 'tensor'), may hold values from -0.125 to 0.125
- up_bias: bfloat16 [8192], P('tensor'), may hold values from -3 to 3
- down_weight: bfloat16 [2048, 8192], P(None, 'tensor'), may hold values from -0.0625 to 0.0625
- down_bias: bfloat16 [2048], replicated, may hold values from -2 to 2
- cotangent: bfloat16 [4, 1024, 2048], P('dp', 'ctx'), may hold values from -6 to 6
Outputs:
- outputs: bfloat16 [4, 1024, 2048], P('dp', ('ctx', 'tensor'))
- input_grad: bfloat16 [4, 1024, 2048], P('dp', ('ctx', 'tensor'))
- first_gain_grad: float32 [2048], replicated
- first_shift_grad: float32 [2048], replicated
- in_weight_grad: float32 [2048, 3, 2048], P(('dp', 'ctx'), None, 'tensor')
- in_bias_grad: float32 [2, 2048], P(None, 'tensor')
- out_weight_grad: float32 [2048, 2048], P(('dp', 'ctx'), 'tensor')
- out_bias_grad: float32 [2048], replicated
- second_gain_grad: float32 [2048], replicated
- second_shift_grad: float32 [2048], replicated
- up_weight_grad: float32 [2048, 8192], P(('dp', 'ctx'), 'tensor')
- up_bias_grad: float32 [8192], P('tensor')
- down_weight_grad: float32 [2048, 8192], P(('dp', 'ctx'), 'tensor')
- down_bias_grad: float32 [2048], replicated
The draws below stay inside these ranges and needn't reach their ends.
Inputs may be any that keep to these rules, and one draw needn't show every extreme that they name: `segments`: along each sequence the numbers start at 0 and rise by one at each document boundary; every sequence holds exactly five documents.
All inputs are finite; a program needn't handle non-finite values.
Results may differ from the reference program's by a relative error of at most 0.019.
Values may be sent and summed in bfloat16 or wider, within the bound.
No kernel may reach another device: no remote copies, remote signals or barrier semaphores. Data moves between devices by JAX's collectives and lax.ppermute only.
A program may use at most 192 MiB of HBM per device.

```python
import math
import jax
import jax.numpy as jnp
from jax import lax

D = 2048
H = 16
HD = 128
FF = 8192
TOK_DEV = 256
LENGTH = 1024
SEQS = 4


def draw_segments(key, part):
    half = TOK_DEV // 2
    first_key, second_key, third_key, fourth_key = jax.random.split(jax.random.fold_in(key, 17), 4)
    head_end = jax.random.randint(first_key, (SEQS, 1), 2, half + 1)
    head_cut = jax.random.randint(second_key, (SEQS, 1), 1, head_end)
    tail_len = jax.random.randint(third_key, (SEQS, 1), 2, half + 1)
    tail_cut = jax.random.randint(fourth_key, (SEQS, 1), 1, tail_len)
    positions = jnp.arange(LENGTH, dtype=jnp.int32)[None, :]
    tail_start = LENGTH - tail_len
    result = (positions >= head_cut).astype(jnp.int32) + (positions >= head_end).astype(jnp.int32)
    result = result + (positions >= tail_start).astype(jnp.int32) + (positions >= tail_start + tail_cut).astype(jnp.int32)
    return result.astype(jnp.int32)


def strengthened(drawn, key, source, target, blocks, factor):
    owner, partner = [(jnp.arange(drawn.shape[dim]) // (drawn.shape[dim] // blocks)).reshape([-1 if axis == dim else 1 for axis in range(drawn.ndim)]) for dim in (source, target)]
    chosen = jax.random.permutation(key, blocks)[partner]
    strong = (owner == chosen) | (owner == (partner + blocks // 2) % blocks)
    return jnp.where(strong, factor * drawn, drawn)


def shard_levels(key, dims, shards, least, high):
    def one(dim, parts):
        steps = jax.random.uniform(jax.random.fold_in(jax.random.fold_in(key, 6), dim), (parts,), jnp.float32, least / len(shards), high / len(shards))
        return jnp.repeat(jnp.exp(steps), dims[dim] // parts).reshape((-1,) + (1,) * (len(dims) - dim - 1))

    loudness = one(*shards[0])
    for cut in shards[1:]:
        loudness = loudness * one(*cut)
    return loudness


def normal_values(own_key, shape, scale, bound, pieces=(), kind=jnp.bfloat16):
    values = scale * jax.random.normal(own_key, shape, jnp.float32)
    if pieces:
        values = values * shard_levels(own_key, shape, pieces, -0.22, 0.18)
    return jnp.clip(values, -bound, bound).astype(kind)


def heavy_noise(rng, dims, deviation, most, cuts, heavy, held_as=jnp.bfloat16):
    array = deviation * jax.random.normal(rng, dims, jnp.float32)
    if cuts:
        array = array * shard_levels(rng, dims, cuts, -0.22, 0.18)
    return jnp.clip(strengthened(array, jax.random.fold_in(rng, 3), *heavy), -most, most).astype(held_as)


def setup_inputs(seed: int = 0) -> dict:
    key_list = jax.random.split(jax.random.key(seed), 16)
    inputs = normal_values(key_list[0], (SEQS, LENGTH, D), 1.0, 6.0, ((0, 4), (1, 4)))
    segments = draw_segments(jax.random.fold_in(key_list[15], 71), 0)
    first_gain = jnp.clip(1.0 + 0.1 * jax.random.normal(key_list[2], (D,), jnp.float32), 0.5, 1.5).astype(jnp.bfloat16)
    first_shift = normal_values(key_list[3], (D,), 0.5, 3.0)
    in_weight = normal_values(key_list[4], (D, 3, D), D ** -0.5, 0.125, ((2, 2),))
    in_bias = normal_values(key_list[5], (2, D), 0.3, 2.0, ((1, 2),))
    out_weight = normal_values(key_list[6], (D, D), (D // 64) ** -0.5, 1.0, ((1, 2),))
    out_bias = normal_values(key_list[7], (D,), 0.3, 2.0)
    second_gain = jnp.clip(1.0 + 0.1 * jax.random.normal(key_list[8], (D,), jnp.float32), 0.5, 1.5).astype(jnp.bfloat16)
    second_shift = normal_values(key_list[9], (D,), 0.5, 3.0)
    up_weight = normal_values(key_list[10], (D, FF), D ** -0.5, 0.125, ((1, 2),))
    up_bias = normal_values(key_list[11], (FF,), 0.5, 3.0, ((0, 2),))
    down_weight = normal_values(key_list[12], (D, FF), FF ** -0.5, 0.0625, ((1, 2),))
    down_bias = normal_values(key_list[13], (D,), 0.3, 2.0)
    cotangent = heavy_noise(key_list[14], (SEQS, LENGTH, D), 1.0, 6.0, ((0, 4), (1, 4)), (1, 2, 4, 2.0))
    return {"inputs": inputs, "segments": segments, "first_gain": first_gain, "first_shift": first_shift, "in_weight": in_weight, "in_bias": in_bias, "out_weight": out_weight, "out_bias": out_bias, "second_gain": second_gain, "second_shift": second_shift, "up_weight": up_weight, "up_bias": up_bias, "down_weight": down_weight, "down_bias": down_bias, "cotangent": cotangent}


@jax.custom_vjp
def low(v):
    return lax.optimization_barrier(v.astype(jnp.bfloat16)).astype(jnp.float32)

@jax.custom_vjp
def low_back(v):
    return v

def low_keep(v):
    return (low(v), None)

def low_pass(kept, grad):
    return (grad,)

def back_keep(v):
    return (v, None)

def back_low(kept, grad):
    return (low(grad),)
low.defvjp(low_keep, low_pass)
low_back.defvjp(back_keep, back_low)
EPSILON = 1e-05
HIGHEST = lax.Precision.HIGHEST

def layer_norm(values, norm_gain, norm_shift):
    average = lax.optimization_barrier(jnp.mean(values, axis=-1, keepdims=True))
    centered = values - average
    spread = lax.optimization_barrier(jnp.mean(centered * centered, axis=-1, keepdims=True))
    return centered * lax.rsqrt(spread + EPSILON) * norm_gain + norm_shift

def attend(query, key, value, segment_row):
    length = query.shape[0]
    block = min(512, length)
    count = length // block
    positions = jnp.arange(length, dtype=jnp.int32)
    heads = jnp.arange(H).astype(jnp.float32)
    slopes = jnp.exp2(-8.0 * (heads + 1.0) / H)
    scale = 1.0 / math.sqrt(HD)

    def one_block(items):
        query_block, query_pos, query_seg = items
        raw = jnp.einsum('qhd,khd->hqk', query_block, key, precision=HIGHEST) * scale
        offset = (positions[None, :] - query_pos[:, None]).astype(jnp.float32)
        raw = low_back(raw + slopes[:, None, None] * offset[None])
        allowed = (positions[None, :] <= query_pos[:, None]) & (segment_row[None, :] == query_seg[:, None])
        masked = jnp.where(allowed[None], raw, -1e+30)
        top = lax.optimization_barrier(jnp.max(masked, axis=-1, keepdims=True))
        weights = jnp.exp(masked - top)
        probs = low(weights / lax.optimization_barrier(jnp.sum(weights, axis=-1, keepdims=True)))
        return jnp.einsum('hqk,khd->qhd', probs, value, precision=HIGHEST)
    items = (query.reshape(count, block, H, HD), positions.reshape(count, block), segment_row.reshape(count, block))
    mixed = lax.map(jax.checkpoint(one_block), items)
    return mixed.reshape(length, H, HD)

def forward(inputs, segment_row, params):
    first_gain, first_shift, in_weight, in_bias, out_weight, out_bias, second_gain, second_shift, up_weight, up_bias, down_weight, down_bias = params
    length = inputs.shape[0]
    normed_first = low(layer_norm(inputs, first_gain, first_shift))
    projected = jnp.einsum('td,dcf->tcf', normed_first, in_weight, precision=HIGHEST)
    query = low(low_back(projected[:, 0] + in_bias[0])).reshape(length, H, HD)
    key = low(low_back(projected[:, 1])).reshape(length, H, HD)
    value = low(low_back(projected[:, 2] + in_bias[1])).reshape(length, H, HD)
    mixed = low(low_back(attend(query, key, value, segment_row).reshape(length, D)))
    attention = low_back(jnp.dot(mixed, out_weight.T, precision=HIGHEST))
    middle = inputs + attention + out_bias
    normed_second = low(layer_norm(middle, second_gain, second_shift))
    upper = low_back(jnp.dot(normed_second, up_weight, precision=HIGHEST) + up_bias)
    active = low(jax.nn.gelu(upper, approximate=True))
    return middle + jnp.dot(active, down_weight.T, precision=HIGHEST) + down_bias

def reference(inputs, segments, first_gain, first_shift, in_weight, in_bias, out_weight, out_bias, second_gain, second_shift, up_weight, up_bias, down_weight, down_bias, cotangent):
    params = tuple((item.astype(jnp.float32) for item in (first_gain, first_shift, in_weight, in_bias, out_weight, out_bias, second_gain, second_shift, up_weight, up_bias, down_weight, down_bias)))

    def one_sequence(totals, items):
        sequence, segment_row, cotangent_row = items

        def apply_layer(values, weights):
            return forward(values, segment_row, weights)
        result, pullback = jax.vjp(apply_layer, sequence.astype(jnp.float32), params)
        grad_inputs, grad_params = pullback(cotangent_row.astype(jnp.float32))
        totals = jax.tree.map(lambda left, right: left + right, totals, grad_params)
        return (totals, (result.astype(jnp.bfloat16), grad_inputs.astype(jnp.bfloat16)))
    zeros = jax.tree.map(jnp.zeros_like, params)
    totals, (outputs, input_grad) = lax.scan(one_sequence, zeros, (inputs, segments, cotangent))
    return (outputs, input_grad, totals[0], totals[1], totals[2], totals[3], totals[4], totals[5], totals[6], totals[7], totals[8], totals[9], totals[10], totals[11])
```

```python
import functools
import math

import jax
import jax.numpy as jnp
from jax import lax
from jax.experimental import pallas as pl
from jax.experimental.pallas import tpu as pltpu
from jax.sharding import PartitionSpec as P

H = 16
HD = 128
EPSILON = 1e-05
MASKED = -1e30
MIB = 1 << 20
GELU_C = math.sqrt(2.0 / math.pi)
GELU_A = 0.044715

BF16 = jnp.bfloat16
F32 = jnp.float32


def params(limit):
    return pltpu.CompilerParams(vmem_limit_bytes=limit * MIB)


def cost(flops, nbytes, trans=0):
    return pl.CostEstimate(
        flops=int(flops), bytes_accessed=int(nbytes), transcendentals=int(trans)
    )


def xperm(values, axis, bit, wanted=None):
    pairs = [
        (i, i ^ bit) for i in range(lax.axis_size(axis)) if wanted is None or wanted(i)
    ]
    return lax.ppermute(values, axis, pairs)


def after(values, *deps):
    return lax.optimization_barrier((values,) + deps)[0]


def ctx_bits():
    n = lax.axis_size("ctx")
    return [1 << b for b in reversed(range(n.bit_length() - 1))]


def ctx_offsets():
    offsets = [0]
    for bit in ctx_bits():
        offsets = offsets + [o ^ bit for o in offsets]
    return offsets


def gather_ctx(block):
    blocks = [block]
    for bit in ctx_bits():
        blocks = blocks + [xperm(b, "ctx", bit) for b in blocks]
    return blocks


def gather_ctx_causal(block):
    blocks, offsets = [block], [0]
    for bit in ctx_bits():
        fresh = []
        for b, o in zip(blocks, offsets):
            fresh.append(
                xperm(b, "ctx", bit, lambda i, o=o, bit=bit: (i ^ o) < (i ^ bit))
            )
        blocks = blocks + fresh
        offsets = offsets + [o ^ bit for o in offsets]
    return blocks


def mm_kernel(*refs, n_pairs, trans):
    lefts, rights = refs[:n_pairs], refs[n_pairs : 2 * n_pairs]
    extras, out = refs[2 * n_pairs : -1], refs[-1]
    total = None
    for left, right in zip(lefts, rights):
        term = lax.dot_general(
            left[...],
            right[...],
            (((1,), (1 if trans else 0,)), ((), ())),
            preferred_element_type=F32,
        )
        total = term if total is None else total + term
    for extra in extras:
        total = total + extra[...].astype(F32)
    out[...] = total.astype(out.dtype)


def mm(lefts, rights, *, trans, start, size, tile, out_dtype, extras=()):
    rows = lefts[0].shape[0]
    tile = min(tile, size)
    first = start // tile
    specs, operands = [], []
    flops = nbytes = 0
    for left in lefts:
        specs.append(pl.BlockSpec(left.shape, lambda i: (0, 0)))
        operands.append(left)
        nbytes += left.size * 2
        flops += 2 * left.size * size
    for left, right in zip(lefts, rights):
        depth = left.shape[1]
        lead = None
        if isinstance(right, tuple):
            right, lead = right
        shape = (tile, depth) if trans else (depth, tile)
        place = (
            (lambda i, lead=lead: ((lead,) if lead is not None else ()) + (first + i, 0))
            if trans
            else (lambda i, lead=lead: ((lead,) if lead is not None else ()) + (0, first + i))
        )
        specs.append(pl.BlockSpec(((None,) if lead is not None else ()) + shape, place))
        operands.append(right)
        nbytes += depth * size * 2
    for extra in extras:
        specs.append(pl.BlockSpec((extra.shape[0], tile), lambda i: (0, first + i)))
        operands.append(extra)
        nbytes += extra.shape[0] * size * extra.dtype.itemsize
    nbytes += rows * size * jnp.dtype(out_dtype).itemsize
    return pl.pallas_call(
        functools.partial(mm_kernel, n_pairs=len(lefts), trans=trans),
        grid=(size // tile,),
        in_specs=specs,
        out_specs=pl.BlockSpec((rows, tile), lambda i: (0, i)),
        out_shape=jax.ShapeDtypeStruct((rows, size), out_dtype),
        compiler_params=params(40),
        cost_estimate=cost(flops, nbytes),
    )(*operands)


def kv_kernel(norm, weight, bias, out):
    total = jnp.dot(norm[...], weight[...], preferred_element_type=F32)
    out[...] = (total + bias[...]).astype(out.dtype)


def project_kv(norm, weight, bias, start, size, tile):
    rows, width = norm.shape
    tile = min(tile, size)
    first = start // tile
    return pl.pallas_call(
        kv_kernel,
        grid=(2, size // tile),
        in_specs=[
            pl.BlockSpec((rows, width), lambda c, i: (0, 0)),
            pl.BlockSpec((None, width, tile), lambda c, i: (c + 1, 0, first + i)),
            pl.BlockSpec((None, 1, tile), lambda c, i: (c, 0, first + i)),
        ],
        out_specs=pl.BlockSpec((None, rows, tile), lambda c, i: (c, 0, i)),
        out_shape=jax.ShapeDtypeStruct((2, rows, size), BF16),
        compiler_params=params(40),
        cost_estimate=cost(4 * rows * width * size, 4 * width * size),
    )(norm, weight, bias)


def up_kernel(norm, weight, bias, grad_active, active, grad_upper, bias_sum):
    upper = jnp.dot(norm[...], weight[...], preferred_element_type=F32) + bias[...]
    square = upper * upper
    wave = jnp.tanh(GELU_C * (upper + GELU_A * square * upper))
    half = 0.5 * (1.0 + wave)
    active[...] = (upper * half).astype(BF16)
    slope = half + 0.5 * upper * (1.0 - wave * wave) * (
        GELU_C * (1.0 + 3.0 * GELU_A * square)
    )
    grad = (grad_active[...] * slope).astype(BF16)
    grad_upper[...] = grad
    bias_sum[...] = jnp.sum(grad.astype(F32), axis=0, keepdims=True)


def up_and_gelu(norm, weight, bias, grad_active, start, size, tile):
    rows, width = norm.shape
    tile = min(tile, size)
    first = start // tile
    block = pl.BlockSpec((rows, tile), lambda i: (0, i))
    return pl.pallas_call(
        up_kernel,
        grid=(size // tile,),
        in_specs=[
            pl.BlockSpec((rows, width), lambda i: (0, 0)),
            pl.BlockSpec((width, tile), lambda i: (0, first + i)),
            pl.BlockSpec((1, tile), lambda i: (0, first + i)),
            pl.BlockSpec((rows, tile), lambda i: (0, first + i)),
        ],
        out_specs=[block, block, pl.BlockSpec((1, tile), lambda i: (0, i))],
        out_shape=[
            jax.ShapeDtypeStruct((rows, size), BF16),
            jax.ShapeDtypeStruct((rows, size), BF16),
            jax.ShapeDtypeStruct((1, size), F32),
        ],
        compiler_params=params(40),
        cost_estimate=cost(
            2 * rows * width * size, 2 * width * size + 8 * rows * size, rows * size
        ),
    )(norm, weight, bias, grad_active)


def weight_grad_kernel(place, left, *refs, offsets):
    rights, out = refs[:-1], refs[-1]
    total = None
    for right, offset in zip(rights, offsets):
        term = jnp.dot(
            left[place[0] ^ offset], right[...], preferred_element_type=F32
        )
        total = term if total is None else total + term
    out[...] = total.astype(out.dtype)


def weight_grad(place, left, rights, tile):
    rows = left.shape[1]
    tokens, size = rights[0].shape
    tile = min(tile, size)
    return pl.pallas_call(
        functools.partial(weight_grad_kernel, offsets=ctx_offsets()),
        grid_spec=pltpu.PrefetchScalarGridSpec(
            num_scalar_prefetch=1,
            grid=(size // tile,),
            in_specs=[pl.BlockSpec(left.shape, lambda i, place: (0, 0, 0))]
            + [pl.BlockSpec((tokens, tile), lambda i, place: (0, i)) for _ in rights],
            out_specs=pl.BlockSpec((rows, tile), lambda i, place: (0, i)),
        ),
        out_shape=jax.ShapeDtypeStruct((rows, size), BF16),
        compiler_params=params(40),
        cost_estimate=cost(
            2 * left.size * size, 2 * (left.size + len(rights) * tokens * size + rows * size)
        ),
    )(place, left, *rights)


def block_scores(place, slope, query, key, start_row, offset):
    rows = query.shape[0]
    raw = lax.dot_general(
        key, query, (((1,), (1,)), ((), ())), preferred_element_type=F32
    ) * (1.0 / math.sqrt(HD))
    shape = raw.shape
    key_pos = (place[0] ^ offset) * rows + lax.broadcasted_iota(jnp.int32, shape, 0)
    query_pos = place[0] * rows + lax.broadcasted_iota(jnp.int32, shape, 1)
    raw = raw + slope * (key_pos - query_pos).astype(F32)
    allowed = (key_pos <= query_pos) & (key_pos >= start_row)
    return raw, allowed


def forward_kernel(place, slopes, query, start, *refs, offsets, first_head):
    n = len(offsets)
    keyvals, (mixed, stats), (held,) = refs[:n], refs[n : n + 2], refs[n + 2 :]
    slope = slopes[first_head + pl.program_id(0)]
    top = None
    for k, offset in enumerate(offsets):
        raw, allowed = block_scores(
            place, slope, query[...], keyvals[k][0], start[...], offset
        )
        raw = jnp.where(allowed, raw, MASKED)
        held[k] = raw
        peak = jnp.max(raw, axis=0, keepdims=True)
        top = peak if top is None else jnp.maximum(top, peak)
    total = None
    for k in range(n):
        fresh = jnp.exp(held[k] - top)
        held[k] = fresh
        part = jnp.sum(fresh, axis=0, keepdims=True)
        total = part if total is None else total + part
    stats[...] = top + jnp.log(total)
    inverse = 1.0 / total
    result = None
    for k in range(n):
        probs = (held[k] * inverse).astype(BF16)
        term = lax.dot_general(
            probs, keyvals[k][1], (((0,), (0,)), ((), ())), preferred_element_type=F32
        )
        result = term if result is None else result + term
    mixed[...] = result.astype(mixed.dtype)


def attention_forward(place, slopes, query, start, keyvals, first_head, heads):
    rows = query.shape[0]
    n = len(keyvals)
    grid_spec = pltpu.PrefetchScalarGridSpec(
        num_scalar_prefetch=2,
        grid=(heads,),
        in_specs=[
            pl.BlockSpec((rows, HD), lambda h, *_: (0, first_head + h)),
            pl.BlockSpec((1, rows), lambda h, *_: (0, 0)),
        ]
        + [pl.BlockSpec((2, rows, HD), lambda h, *_: (0, 0, h))] * n,
        out_specs=[
            pl.BlockSpec((rows, HD), lambda h, *_: (0, h)),
            pl.BlockSpec((None, 1, rows), lambda h, *_: (h, 0, 0)),
        ],
        scratch_shapes=[pltpu.VMEM((n, rows, rows), F32)],
    )
    return pl.pallas_call(
        functools.partial(forward_kernel, offsets=ctx_offsets(), first_head=first_head),
        grid_spec=grid_spec,
        out_shape=[
            jax.ShapeDtypeStruct((rows, heads * HD), BF16),
            jax.ShapeDtypeStruct((heads, 1, rows), F32),
        ],
        compiler_params=params(40),
        cost_estimate=cost(
            4 * n * rows * rows * HD * heads,
            4 * n * rows * HD * heads,
            n * rows * rows * heads,
        ),
    )(place, slopes, query, start, *keyvals)


def backward_kernel(
    place, slopes, query, grad_mixed, start, stats, *refs, offsets, first_head
):
    n = len(offsets)
    keyvals = refs[:n]
    grad_query, near, far, probs_held, grads_held = refs[n:]
    slope = slopes[first_head + pl.program_id(0)]
    scale = 1.0 / math.sqrt(HD)
    delta = None
    for k, offset in enumerate(offsets):
        raw, allowed = block_scores(
            place, slope, query[...], keyvals[k][0], start[...], offset
        )
        probs = jnp.where(allowed, jnp.exp(raw - stats[...]), 0.0)
        grads = lax.dot_general(
            keyvals[k][1],
            grad_mixed[...],
            (((1,), (1,)), ((), ())),
            preferred_element_type=F32,
        )
        probs_held[k] = probs
        grads_held[k] = grads
        part = jnp.sum(probs * grads, axis=0, keepdims=True)
        delta = part if delta is None else delta + part
    total = None
    for k, offset in enumerate(offsets):
        probs = probs_held[k]
        grad_scores = (probs * (grads_held[k] - delta)).astype(BF16)
        term = lax.dot_general(
            grad_scores,
            keyvals[k][0],
            (((0,), (0,)), ((), ())),
            preferred_element_type=F32,
        )
        total = term if total is None else total + term
        key_grad = jnp.dot(grad_scores, query[...], preferred_element_type=F32) * scale
        value_grad = jnp.dot(
            probs.astype(BF16), grad_mixed[...], preferred_element_type=F32
        )
        target, slot = (near, k) if k < n - n // 2 else (far, k - (n - n // 2))
        target[0, slot] = key_grad.astype(target.dtype)
        target[1, slot] = value_grad.astype(target.dtype)
    grad_query[...] = (total * scale).astype(grad_query.dtype)


def attention_backward(
    place, slopes, query, grad_mixed, start, stats, keyvals, first_head, heads
):
    rows = query.shape[0]
    n = len(keyvals)
    n_far = n // 2
    n_near = n - n_far
    grid_spec = pltpu.PrefetchScalarGridSpec(
        num_scalar_prefetch=2,
        grid=(heads,),
        in_specs=[
            pl.BlockSpec((rows, HD), lambda h, *_: (0, first_head + h)),
            pl.BlockSpec((rows, HD), lambda h, *_: (0, first_head + h)),
            pl.BlockSpec((1, rows), lambda h, *_: (0, 0)),
            pl.BlockSpec((None, 1, rows), lambda h, *_: (h, 0, 0)),
        ]
        + [pl.BlockSpec((2, rows, HD), lambda h, *_: (0, 0, h))] * n,
        out_specs=[
            pl.BlockSpec((rows, HD), lambda h, *_: (0, h)),
            pl.BlockSpec((2, n_near, rows, HD), lambda h, *_: (0, 0, 0, h)),
            pl.BlockSpec((2, max(n_far, 1), rows, HD), lambda h, *_: (0, 0, 0, h)),
        ],
        scratch_shapes=[pltpu.VMEM((n, rows, rows), F32)] * 2,
    )
    return pl.pallas_call(
        functools.partial(backward_kernel, offsets=ctx_offsets(), first_head=first_head),
        grid_spec=grid_spec,
        out_shape=[
            jax.ShapeDtypeStruct((rows, heads * HD), BF16),
            jax.ShapeDtypeStruct((2, n_near, rows, heads * HD), BF16),
            jax.ShapeDtypeStruct((2, max(n_far, 1), rows, heads * HD), BF16),
        ],
        compiler_params=params(40),
        cost_estimate=cost(
            10 * n * rows * rows * HD * heads,
            8 * n * rows * HD * heads,
            n * rows * rows * heads,
        ),
    )(place, slopes, query, grad_mixed, start, stats, *keyvals)


def normalized(values):
    average = jnp.mean(values, axis=-1, keepdims=True)
    centered = values - average
    spread = jnp.mean(centered * centered, axis=-1, keepdims=True)
    inverse = lax.rsqrt(spread + EPSILON)
    return centered * inverse, inverse


def norm_backward(grad, unit, inverse, gain):
    scaled = grad * gain
    mean_scaled = jnp.mean(scaled, axis=-1, keepdims=True)
    mean_unit = jnp.mean(scaled * unit, axis=-1, keepdims=True)
    return inverse * (scaled - mean_scaled - unit * mean_unit)


def all_sum(values, axes):
    for axis in axes:
        bit = 1
        while bit < lax.axis_size(axis):
            values = values + xperm(values, axis, bit)
            bit *= 2
    return values


def spread_left(values):
    tokens, width = values.shape
    n_dp, n_ctx = lax.axis_size("dp"), lax.axis_size("ctx")
    grid = values.reshape(tokens, n_dp, n_ctx, width // (n_dp * n_ctx))
    parts = grid.transpose(2, 1, 3, 0).reshape(n_ctx, width // n_ctx, tokens)
    return lax.all_to_all(parts, "ctx", 0, 0, tiled=True)


def shards(
    inputs,
    segments,
    first_gain,
    first_shift,
    in_weight,
    in_bias,
    out_weight,
    out_bias,
    second_gain,
    second_shift,
    up_weight,
    up_bias,
    down_weight,
    down_bias,
    cotangent,
):
    rows = inputs.shape[1]
    width = inputs.shape[2]
    local_width = in_weight.shape[2]
    local_hidden = up_weight.shape[1]
    heads_here = local_width // HD
    n_tensor = lax.axis_size("tensor")
    n_ctx = lax.axis_size("ctx")
    share = rows // n_tensor
    tensor_place = lax.axis_index("tensor")
    context_place = lax.axis_index("ctx")
    place = context_place.astype(jnp.int32).reshape(1)
    share_start = tensor_place * share

    def mine(values):
        return lax.dynamic_slice_in_dim(values, share_start, share, 0)

    head_index = (tensor_place * heads_here).astype(F32) + jnp.arange(heads_here, dtype=F32)
    slopes = jnp.exp2(-8.0 * (head_index + 1.0) / H)
    query_seg = lax.dynamic_slice_in_dim(segments[0], context_place * rows, rows)
    doc_start = jnp.sum(
        (segments[0][:, None] < query_seg[None, :]).astype(jnp.int32), axis=0, keepdims=True
    )

    gain_one, shift_one = first_gain.astype(F32), first_shift.astype(F32)
    gain_two, shift_two = second_gain.astype(F32), second_shift.astype(F32)
    weight_in = in_weight.transpose(1, 0, 2)
    bias_pair = in_bias.astype(F32)
    cot_low = cotangent[0]

    half_width = local_width // 2
    pair_place = context_place & 1
    out_half = lax.dynamic_slice_in_dim(out_weight, pair_place * half_width, half_width, 1)
    out_halves = [xperm(out_half, "tensor", k) for k in range(1, n_tensor)]

    residual = inputs[0]
    unit_one, _ = normalized(residual.astype(F32))
    normed_first = (unit_one * gain_one + shift_one).astype(BF16)

    groups = 2 if heads_here % 2 == 0 else 1
    group_heads = heads_here // groups
    group_width = group_heads * HD
    kv_bias = jnp.stack([jnp.zeros_like(bias_pair[1]), bias_pair[1]])[:, None, :]
    own = [
        project_kv(normed_first, weight_in, kv_bias, g * group_width, group_width, 512)
        for g in range(groups)
    ]
    keyvals = [gather_ctx_causal(block) for block in own]
    query = mm(
        [normed_first], [(weight_in, 0)], trans=False, start=0, size=local_width, tile=512,
        out_dtype=BF16, extras=(bias_pair[0:1],),
    )
    grad_active = mm(
        [cot_low], [down_weight], trans=False, start=0, size=local_hidden, tile=512, out_dtype=F32,
    )
    out_others = [
        (half, xperm(half, "ctx", 1)) for half in out_halves
    ]
    keyvals, grad_active = lax.optimization_barrier((keyvals, grad_active))

    mixed_parts, stats = [], []
    mixed_others = [[] for _ in range(1, n_tensor)]
    for g in range(groups):
        part, stat = attention_forward(
            place, slopes, query, doc_start, keyvals[g], g * group_heads, group_heads
        )
        mixed_parts.append(part)
        stats.append(stat)
        for k in range(1, n_tensor):
            mixed_others[k - 1].append(xperm(part, "tensor", k))
    mixed = jnp.concatenate(mixed_parts, axis=1) if groups > 1 else mixed_parts[0]
    lefts, rights = [mixed], [out_weight]
    for parts, (half, other_half) in zip(mixed_others, out_others):
        whole = jnp.concatenate(parts, axis=1) if groups > 1 else parts[0]
        lefts.append(lax.dynamic_slice_in_dim(whole, pair_place * half_width, half_width, 1))
        rights.append(half)
        lefts.append(lax.dynamic_slice_in_dim(whole, (1 - pair_place) * half_width, half_width, 1))
        rights.append(other_half)
    middle = mm(
        lefts, rights, trans=True, start=0, size=width, tile=512, out_dtype=F32,
        extras=(residual, out_bias.astype(F32)[None]),
    )
    unit_two, inverse_two = normalized(middle)
    normed_second = (unit_two * gain_two + shift_two).astype(BF16)

    left_down = spread_left(cot_low)
    left_in = spread_left(normed_first)
    left_up = spread_left(normed_second)

    chunks = 2
    chunk = local_hidden // chunks
    actives, grad_uppers, up_bias_parts = [], [], []
    up_bias_row = up_bias.astype(F32)[None]
    for i in range(chunks):
        active, grad_upper, bias_part = up_and_gelu(
            normed_second, up_weight, up_bias_row, grad_active, i * chunk, chunk, 512
        )
        actives.append(active)
        grad_uppers.append(grad_upper)
        up_bias_parts.append(bias_part)

    def reduced(left, right, tile=512):
        whole = weight_grad(place, left, gather_ctx(right), tile)
        return lax.psum_scatter(whole, "dp", scatter_dimension=0, tiled=True)

    down_parts = [reduced(left_down, active) for active in actives]
    up_parts = [reduced(left_up, grad) for grad in grad_uppers]

    grad_hidden = jnp.concatenate(grad_uppers, axis=1)
    halves = 2
    grad_normed = []
    for i in range(halves):
        part = mm(
            [grad_hidden], [up_weight], trans=True, start=i * (width // halves),
            size=width // halves, tile=256, out_dtype=BF16,
        )
        total = part.astype(F32)
        for k in range(1, n_tensor):
            total = total + xperm(part, "tensor", k).astype(F32)
        grad_normed.append(total)
    grad_normed = jnp.concatenate(grad_normed, axis=1)
    cot = cot_low.astype(F32)
    grad_middle = cot + norm_backward(grad_normed, unit_two, inverse_two, gain_two)
    grad_middle_low = grad_middle.astype(BF16)
    grad_mixed = mm(
        [grad_middle_low], [out_weight], trans=False, start=0, size=local_width, tile=512,
        out_dtype=BF16,
    )
    left_out = spread_left(grad_middle_low)
    out_part = reduced(left_out, mixed)

    active_late = after(jnp.concatenate(actives, axis=1), grad_mixed)
    feed = mm(
        [active_late], [down_weight], trans=True, start=0, size=width, tile=256, out_dtype=BF16
    )

    def tensor_scatter(values):
        total = mine(values).astype(F32)
        for k in range(1, n_tensor):
            piece = lax.dynamic_slice_in_dim(values, (tensor_place ^ k) * share, share, 0)
            total = total + xperm(piece, "tensor", k).astype(F32)
        return total

    outputs = (mine(middle) + tensor_scatter(feed) + down_bias.astype(F32)).astype(BF16)

    grad_queries, grad_keys, grad_values = [], [], []
    for g in range(groups):
        grad_query, near, far = attention_backward(
            place, slopes, query, grad_mixed, doc_start, stats[g], keyvals[g],
            g * group_heads, group_heads,
        )
        grad_queries.append(grad_query)
        blocks = [near[:, k] for k in range(near.shape[1])]
        if n_ctx > 1:
            received = xperm(far, "ctx", 1)
            blocks = [
                (block.astype(F32) + received[:, k].astype(F32))
                for k, block in enumerate(blocks)
            ]
            bits = ctx_bits()[:-1]
            for bit in reversed(bits):
                half = len(blocks) // 2
                blocks = [
                    block
                    + xperm(sent.astype(BF16), "ctx", bit, lambda i, bit=bit: i > i ^ bit).astype(F32)
                    for block, sent in zip(blocks[:half], blocks[half:])
                ]
        final = blocks[0].astype(BF16)
        grad_keys.append(final[0])
        grad_values.append(final[1])
    grad_projected = [
        jnp.concatenate(parts, axis=1) if groups > 1 else parts[0]
        for parts in (grad_queries, grad_keys, grad_values)
    ]
    in_parts = [reduced(left_in, grad) for grad in grad_projected]
    grad_first = mm(
        grad_projected, [(weight_in, c) for c in range(3)], trans=True, start=0, size=width,
        tile=512, out_dtype=BF16,
    )
    grad_first_share = tensor_scatter(grad_first)
    unit_share, inverse_share = normalized(mine(residual).astype(F32))
    grad_from_first = norm_backward(grad_first_share, unit_share, inverse_share, gain_one)
    grad_middle_share = mine(grad_middle)
    input_grad = (grad_middle_share + grad_from_first).astype(BF16)

    def over_tokens(values):
        return jnp.sum(values, axis=0)

    grad_normed_share, unit_two_share = mine(grad_normed), mine(unit_two)
    early = jnp.stack(
        [
            over_tokens(grad_normed_share * unit_two_share),
            over_tokens(grad_normed_share),
            over_tokens(grad_middle_share),
            over_tokens(mine(cot)),
        ]
    )
    early = all_sum(early, ("tensor",))
    up_bias_row_sum = jnp.concatenate(up_bias_parts, axis=1).reshape(-1, local_width)
    early_rows = early.reshape(-1, local_width)
    early_all = all_sum(jnp.concatenate([early_rows, up_bias_row_sum]), ("ctx", "dp"))
    early = early_all[: early_rows.shape[0]].reshape(4, width)
    up_bias_grad = early_all[early_rows.shape[0] :].reshape(-1)
    late = jnp.stack(
        [over_tokens(grad_first_share * unit_share), over_tokens(grad_first_share)]
    )
    late = all_sum(late, ("tensor",)).reshape(-1, local_width)
    bias_terms = jnp.stack(
        [
            over_tokens(grad_projected[0].astype(F32)),
            over_tokens(grad_projected[2].astype(F32)),
        ]
    )
    late_all = all_sum(jnp.concatenate([late, bias_terms]), ("ctx", "dp"))
    late = late_all[: late.shape[0]].reshape(2, width)
    in_bias_grad = late_all[-2:]

    in_weight_grad = jnp.stack([part.astype(F32) for part in in_parts]).transpose(1, 0, 2)
    down_weight_grad = jnp.concatenate([part.astype(F32) for part in down_parts], axis=1)
    up_weight_grad = jnp.concatenate([part.astype(F32) for part in up_parts], axis=1)
    return (
        outputs[None],
        input_grad[None],
        late[0],
        late[1],
        in_weight_grad,
        in_bias_grad,
        out_part.astype(F32),
        early[2],
        early[0],
        early[1],
        up_weight_grad,
        up_bias_grad,
        down_weight_grad,
        early[3],
    )


def solution(mesh):
    return jax.shard_map(
        shards,
        mesh=mesh,
        in_specs=(
            P("dp", "ctx", None),
            P("dp", None),
            P(),
            P(),
            P(None, None, "tensor"),
            P(None, "tensor"),
            P(None, "tensor"),
            P(),
            P(),
            P(),
            P(None, "tensor"),
            P("tensor"),
            P(None, "tensor"),
            P(),
            P("dp", "ctx", None),
        ),
        out_specs=(
            P("dp", ("ctx", "tensor"), None),
            P("dp", ("ctx", "tensor"), None),
            P(),
            P(),
            P(("dp", "ctx"), None, "tensor"),
            P(None, "tensor"),
            P(("dp", "ctx"), "tensor"),
            P(),
            P(),
            P(),
            P(("dp", "ctx"), "tensor"),
            P("tensor"),
            P(("dp", "ctx"), "tensor"),
            P(),
        ),
        check_vma=False,
    )
```

```python
import functools
import math

import jax
import jax.numpy as jnp
from jax import lax
from jax.experimental import pallas as pl
from jax.experimental.pallas import tpu as pltpu
from jax.sharding import PartitionSpec as P

H = 16
HD = 128
EPSILON = 1e-05
MASKED = -1e30
MIB = 1 << 20
GELU_C = math.sqrt(2.0 / math.pi)
GELU_A = 0.044715

BF16 = jnp.bfloat16
F32 = jnp.float32


VMEM = 56


def params(limit):
    return pltpu.CompilerParams(vmem_limit_bytes=limit * MIB)


def load(level=0):
    if not level:
        return None
    return pl.CostEstimate(flops=10 ** (8 + 2 * level), bytes_accessed=10**7, transcendentals=0)


def xperm(values, axis, bit, wanted=None):
    pairs = [
        (i, i ^ bit) for i in range(lax.axis_size(axis)) if wanted is None or wanted(i)
    ]
    return lax.ppermute(values, axis, pairs)


def after(values, *deps):
    return lax.optimization_barrier((values,) + deps)[0]


def ctx_bits():
    n = lax.axis_size("ctx")
    return [1 << b for b in reversed(range(n.bit_length() - 1))]


def ctx_offsets():
    offsets = [0]
    for bit in ctx_bits():
        offsets = offsets + [o ^ bit for o in offsets]
    return offsets


def gather_ctx(block, gates=()):
    blocks = [block]
    for hop, bit in enumerate(ctx_bits()):
        held_back = 0 < hop <= len(gates)
        sent = lax.optimization_barrier((blocks, gates[hop - 1]))[0] if held_back else blocks
        blocks = blocks + [xperm(b, "ctx", bit) for b in sent]
    return blocks


def gather_ctx_causal(block, gate):
    blocks, offsets = [block], [0]
    for bit in ctx_bits():
        fresh = []
        for b, o in zip(blocks, offsets):
            b = after(b, gate) if o else b
            fresh.append(
                xperm(b, "ctx", bit, lambda i, o=o, bit=bit: (i ^ o) < (i ^ bit))
            )
        blocks = blocks + fresh
        offsets = offsets + [o ^ bit for o in offsets]
    return blocks


def mm_kernel(*refs, n_pairs, trans):
    lefts, rights = refs[:n_pairs], refs[n_pairs : 2 * n_pairs]
    extras, out = refs[2 * n_pairs : -1], refs[-1]
    total = None
    for left, right in zip(lefts, rights):
        term = lax.dot_general(
            left[...],
            right[...],
            (((1,), (1 if trans else 0,)), ((), ())),
            preferred_element_type=F32,
        )
        total = term if total is None else total + term
    for extra in extras:
        row = extra[0:1, :] if extra.shape[0] == 2 else extra[...]
        total = total + row.astype(F32)
    out[...] = total.astype(out.dtype)


def mm(lefts, rights, *, trans, start, size, tile, out_dtype, extras=(), heavy=0):
    lefts = [left if isinstance(left, tuple) else (left, 0, left.shape[1]) for left in lefts]
    rows = lefts[0][0].shape[0]
    tile = math.gcd(tile, size)
    first = start // tile
    specs, operands = [], []
    for left, column, depth in lefts:
        specs.append(pl.BlockSpec((rows, depth), lambda i, column=column: (0, column)))
        operands.append(left)
    for (left, column, depth), right in zip(lefts, rights):
        lead, part = None, 0
        if isinstance(right, tuple):
            right, lead, part = right
        shape = (tile, depth) if trans else (depth, tile)

        def place(i, lead=lead, part=part):
            where = (first + i, part) if trans else (part, first + i)
            return where if lead is None else (lead,) + where

        specs.append(pl.BlockSpec(((None,) if lead is not None else ()) + shape, place))
        operands.append(right)
    for extra in extras:
        specs.append(pl.BlockSpec((extra.shape[0], tile), lambda i: (0, first + i)))
        operands.append(extra)
    return pl.pallas_call(
        functools.partial(mm_kernel, n_pairs=len(lefts), trans=trans),
        grid=(size // tile,),
        in_specs=specs,
        out_specs=pl.BlockSpec((rows, tile), lambda i: (0, i)),
        out_shape=jax.ShapeDtypeStruct((rows, size), out_dtype),
        compiler_params=params(VMEM),
        cost_estimate=load(heavy),
    )(*operands)


def kv_kernel(values, pair, weight, bias, norm, *outs):
    @pl.when(pl.program_id(0) == 0)
    def _():
        unit, _ = normalized(values[...].astype(F32))
        norm[...] = (unit * pair[0:1, :] + pair[1:2, :]).astype(BF16)

    shifted = bias[1:2, :].astype(F32) * pl.program_id(0).astype(F32)
    total = jnp.dot(norm[...], weight[...], preferred_element_type=F32) + shifted
    size = outs[0].shape[1]
    for k, out in enumerate(outs):
        out[...] = total[:, k * size : (k + 1) * size].astype(out.dtype)


def project_kv(values, pair, weight, bias, groups):
    rows, width = values.shape
    columns = weight.shape[2]
    size = columns // groups
    whole = pl.BlockSpec((rows, width), lambda c: (0, 0))
    return pl.pallas_call(
        kv_kernel,
        grid=(2,),
        in_specs=[
            whole,
            pl.BlockSpec((2, width), lambda c: (0, 0)),
            pl.BlockSpec((None, width, columns), lambda c: (c + 1, 0, 0)),
            pl.BlockSpec((2, columns), lambda c: (0, 0)),
        ],
        out_specs=[whole]
        + [pl.BlockSpec((None, rows, size), lambda c: (c, 0, 0))] * groups,
        out_shape=[jax.ShapeDtypeStruct((rows, width), BF16)]
        + [jax.ShapeDtypeStruct((2, rows, size), BF16)] * groups,
        compiler_params=params(VMEM),
        cost_estimate=load(),
    )(values, pair, weight, bias)


def normalized(values):
    average = jnp.mean(values, axis=-1, keepdims=True)
    centered = values - average
    spread = jnp.mean(centered * centered, axis=-1, keepdims=True)
    inverse = lax.rsqrt(spread + EPSILON)
    return centered * inverse, inverse


def up_block(norm, weight, bias, grad_active, active, grad_upper, bias_sum):
    upper = jnp.dot(norm[...], weight[...], preferred_element_type=F32) + bias[...]
    square = upper * upper
    wave = jnp.tanh(GELU_C * (upper + GELU_A * square * upper))
    half = 0.5 * (1.0 + wave)
    active[...] = (upper * half).astype(BF16)
    slope = half + 0.5 * upper * (1.0 - wave * wave) * (
        GELU_C * (1.0 + 3.0 * GELU_A * square)
    )
    grad = (grad_active[...] * slope).astype(BF16)
    grad_upper[...] = grad
    bias_sum[...] = jnp.sum(grad.astype(F32), axis=0, keepdims=True)


def up_kernel(norm, weight, bias, grad_active, *refs):
    up_block(norm, weight, bias, grad_active, *refs[-3:])


def first_up_kernel(*refs, n_terms):
    values, vectors = refs[:2]
    terms, (weight, bias, grad_active) = refs[2 : 2 + n_terms], refs[2 + n_terms : 5 + n_terms]
    middle, norm, active, grad_upper, bias_sum = refs[5 + n_terms :]

    @pl.when(pl.program_id(0) == 0)
    def _():
        total = terms[0][...].astype(F32)
        for term in terms[1:]:
            total = total + term[...].astype(F32)
        middle[...] = values[...].astype(F32) + total + vectors[0:1, :]
        unit, _ = normalized(middle[...])
        norm[...] = (unit * vectors[1:2, :] + vectors[2:3, :]).astype(BF16)

    up_block(norm, weight, bias, grad_active, active, grad_upper, bias_sum)


def up_specs(width, rows, tile, first, out_first=0):
    ins = [
        pl.BlockSpec((width, tile), lambda i: (0, first + i)),
        pl.BlockSpec((1, tile), lambda i: (0, first + i)),
        pl.BlockSpec((rows, tile), lambda i: (0, first + i)),
    ]
    outs = [
        pl.BlockSpec((rows, tile), lambda i: (0, i)),
        pl.BlockSpec((rows, tile), lambda i: (0, out_first + i)),
        pl.BlockSpec((1, tile), lambda i: (0, i)),
    ]
    return ins, outs


def up_shapes(rows, size, local):
    return [
        jax.ShapeDtypeStruct((rows, size), BF16),
        jax.ShapeDtypeStruct((rows, local), BF16),
        jax.ShapeDtypeStruct((1, size), F32),
    ]


def first_up(values, vectors, terms, weight, bias, grad_active, size, local, tile):
    rows, width = values.shape
    whole = pl.BlockSpec((rows, width), lambda i: (0, 0))
    ins, outs = up_specs(width, rows, tile, 0)
    return pl.pallas_call(
        functools.partial(first_up_kernel, n_terms=len(terms)),
        grid=(size // tile,),
        in_specs=[whole, pl.BlockSpec((3, width), lambda i: (0, 0))] + [whole] * len(terms) + ins,
        out_specs=[whole, whole] + outs,
        out_shape=[
            jax.ShapeDtypeStruct((rows, width), F32),
            jax.ShapeDtypeStruct((rows, width), BF16),
        ]
        + up_shapes(rows, size, local),
        compiler_params=params(VMEM),
        cost_estimate=load(),
    )(values, vectors, *terms, weight, bias, grad_active)


def more_up(norm, weight, bias, grad_active, start, size, tile, held=None):
    rows, width = norm.shape
    ins, outs = up_specs(width, rows, tile, start // tile, 0 if held is None else start // tile)
    in_specs = [pl.BlockSpec((rows, width), lambda i: (0, 0))] + ins
    operands = [norm, weight, bias, grad_active]
    if held is not None:
        in_specs.append(pl.BlockSpec(memory_space=pl.ANY))
        operands.append(held)
    return pl.pallas_call(
        up_kernel,
        grid=(size // tile,),
        in_specs=in_specs,
        out_specs=outs,
        out_shape=up_shapes(rows, size, size if held is None else held.shape[1]),
        input_output_aliases={} if held is None else {4: 1},
        compiler_params=params(VMEM),
        cost_estimate=load(),
    )(*operands)


def weight_grad_kernel(*refs, blocks, n):
    out, step, first = refs[-1], pl.program_id(0), 0

    def summed(lefts, rights):
        total = None
        for left, right in zip(lefts, rights):
            term = jnp.dot(left[...], right[...], preferred_element_type=F32)
            total = term if total is None else total + term
        out[...] = total.astype(out.dtype)

    for part, count in enumerate(blocks):
        lefts = refs[2 * n * part : 2 * n * part + n]
        rights = refs[2 * n * part + n : 2 * n * (part + 1)]
        if len(blocks) == 1:
            summed(lefts, rights)
        else:
            pl.when((step >= first) & (step < first + count))(
                functools.partial(summed, lefts, rights)
            )
        first += count


def weight_grad(parts, rows, tile):
    n = len(parts[0][0])
    tokens = parts[0][0][0].shape[1]
    for _, _, rights in parts:
        tile = math.gcd(tile, rights[0].shape[1])
    blocks = [rights[0].shape[1] // tile for _, _, rights in parts]
    specs, operands, first = [], [], 0
    for (lefts, row, rights), count in zip(parts, blocks):

        def place(i, first=first, count=count):
            return (0, jnp.clip(i - first, 0, count - 1))

        specs += [pl.BlockSpec((rows, tokens), lambda i, row=row: (row, 0))] * n
        specs += [pl.BlockSpec((tokens, tile), place)] * n
        operands += list(lefts) + list(rights)
        first += count
    return pl.pallas_call(
        functools.partial(weight_grad_kernel, blocks=blocks, n=n),
        grid=(first,),
        in_specs=specs,
        out_specs=pl.BlockSpec((rows, tile), lambda i: (0, i)),
        out_shape=jax.ShapeDtypeStruct((rows, first * tile), BF16),
        compiler_params=params(VMEM),
        cost_estimate=load(),
    )(*operands)


def widen_kernel(values, first, other):
    @pl.when(pl.program_id(0) == 0)
    def _():
        first[...] = values[...].astype(F32)

    @pl.when(pl.program_id(0) > 0)
    def _():
        other[...] = values[...].astype(F32)


def widen_joint(values, tile):
    rows, size = values.shape
    blocks = size // tile
    return pl.pallas_call(
        widen_kernel,
        grid=(blocks,),
        in_specs=[pl.BlockSpec((rows, tile), lambda i: (0, i))],
        out_specs=[
            pl.BlockSpec((rows, tile), lambda i: (0, 0)),
            pl.BlockSpec((None, rows, tile), lambda i: (jnp.maximum(i - 1, 0), 0, 0)),
        ],
        out_shape=[
            jax.ShapeDtypeStruct((rows, tile), F32),
            jax.ShapeDtypeStruct((blocks - 1, rows, tile), F32),
        ],
        compiler_params=params(VMEM),
        cost_estimate=load(),
    )(values)


def block_scores(place, slope, query, key, start_row, offset):
    rows = query.shape[0]
    raw = lax.dot_general(
        key, query, (((1,), (1,)), ((), ())), preferred_element_type=F32
    ) * (1.0 / math.sqrt(HD))
    shape = raw.shape
    key_pos = (place[0] ^ offset) * rows + lax.broadcasted_iota(jnp.int32, shape, 0)
    query_pos = place[0] * rows + lax.broadcasted_iota(jnp.int32, shape, 1)
    raw = raw + slope * (key_pos - query_pos).astype(F32)
    allowed = (key_pos <= query_pos) & (key_pos >= start_row)
    return raw, allowed


def forward_kernel(place, slopes, query, start, *refs, offsets, first_head):
    n = len(offsets)
    keyvals, (mixed, stats, held) = refs[:n], refs[-3:]
    slope = slopes[first_head + pl.program_id(0)]
    top = None
    for k, offset in enumerate(offsets):
        raw, allowed = block_scores(
            place, slope, query[...], keyvals[k][0], start[...], offset
        )
        raw = jnp.where(allowed, raw, MASKED)
        held[k] = raw
        peak = jnp.max(raw, axis=0, keepdims=True)
        top = peak if top is None else jnp.maximum(top, peak)
    total = None
    for k in range(n):
        fresh = jnp.exp(held[k] - top)
        held[k] = fresh
        part = jnp.sum(fresh, axis=0, keepdims=True)
        total = part if total is None else total + part
    stats[...] = top + jnp.log(total)
    inverse = 1.0 / total
    result = None
    for k in range(n):
        probs = (held[k] * inverse).astype(BF16)
        term = lax.dot_general(
            probs, keyvals[k][1], (((0,), (0,)), ((), ())), preferred_element_type=F32
        )
        result = term if result is None else result + term
    mixed[...] = result.astype(mixed.dtype)


def attention_forward(place, slopes, query, start, keyvals, first_head, heads, held=None):
    rows, columns = query.shape
    extra = [] if held is None else [held]
    n = len(keyvals)
    grid_spec = pltpu.PrefetchScalarGridSpec(
        num_scalar_prefetch=2,
        grid=(heads,),
        in_specs=[
            pl.BlockSpec((rows, HD), lambda h, *_: (0, first_head + h)),
            pl.BlockSpec((1, rows), lambda h, *_: (0, 0)),
        ]
        + [pl.BlockSpec((2, rows, HD), lambda h, *_: (0, 0, h))] * n
        + [pl.BlockSpec(memory_space=pl.ANY)] * len(extra),
        out_specs=[
            pl.BlockSpec((rows, HD), lambda h, *_: (0, first_head + h)),
            pl.BlockSpec((None, 1, rows), lambda h, *_: (h, 0, 0)),
        ],
        scratch_shapes=[pltpu.VMEM((n, rows, rows), F32)],
    )
    return pl.pallas_call(
        functools.partial(forward_kernel, offsets=ctx_offsets(), first_head=first_head),
        grid_spec=grid_spec,
        out_shape=[
            jax.ShapeDtypeStruct((rows, columns), BF16),
            jax.ShapeDtypeStruct((heads, 1, rows), F32),
        ],
        input_output_aliases={4 + n: 0} if extra else {},
        compiler_params=params(VMEM),
        cost_estimate=load(),
    )(place, slopes, query, start, *keyvals, *extra)


def backward_kernel(
    place, slopes, query, grad_mixed, start, stats, *refs, offsets, first_head
):
    n = len(offsets)
    keyvals = refs[:n]
    grad_query, near, far, probs_held, grads_held = refs[-5:]
    slope = slopes[first_head + pl.program_id(0)]
    scale = 1.0 / math.sqrt(HD)
    delta = None
    for k, offset in enumerate(offsets):
        raw, allowed = block_scores(
            place, slope, query[...], keyvals[k][0], start[...], offset
        )
        probs = jnp.where(allowed, jnp.exp(raw - stats[...]), 0.0)
        grads = lax.dot_general(
            keyvals[k][1],
            grad_mixed[...],
            (((1,), (1,)), ((), ())),
            preferred_element_type=F32,
        )
        probs_held[k] = probs
        grads_held[k] = grads
        part = jnp.sum(probs * grads, axis=0, keepdims=True)
        delta = part if delta is None else delta + part
    total = None
    for k, offset in enumerate(offsets):
        probs = probs_held[k]
        grad_scores = (probs * (grads_held[k] - delta)).astype(BF16)
        term = lax.dot_general(
            grad_scores,
            keyvals[k][0],
            (((0,), (0,)), ((), ())),
            preferred_element_type=F32,
        )
        total = term if total is None else total + term
        key_grad = jnp.dot(grad_scores, query[...], preferred_element_type=F32) * scale
        value_grad = jnp.dot(
            probs.astype(BF16), grad_mixed[...], preferred_element_type=F32
        )
        target, slot = (near, k) if k < n - n // 2 else (far, k - (n - n // 2))
        target[0, slot] = key_grad.astype(target.dtype)
        target[1, slot] = value_grad.astype(target.dtype)
    grad_query[...] = (total * scale).astype(grad_query.dtype)


def attention_backward(
    place, slopes, query, grad_mixed, start, stats, keyvals, first_head, heads, held=None,
    heavy=0,
):
    rows, columns = query.shape
    extra = [] if held is None else [held]
    n = len(keyvals)
    n_far = n // 2
    n_near = n - n_far
    grid_spec = pltpu.PrefetchScalarGridSpec(
        num_scalar_prefetch=2,
        grid=(heads,),
        in_specs=[
            pl.BlockSpec((rows, HD), lambda h, *_: (0, first_head + h)),
            pl.BlockSpec((rows, HD), lambda h, *_: (0, first_head + h)),
            pl.BlockSpec((1, rows), lambda h, *_: (0, 0)),
            pl.BlockSpec((None, 1, rows), lambda h, *_: (h, 0, 0)),
        ]
        + [pl.BlockSpec((2, rows, HD), lambda h, *_: (0, 0, h))] * n
        + [pl.BlockSpec(memory_space=pl.ANY)] * len(extra),
        out_specs=[
            pl.BlockSpec((rows, HD), lambda h, *_: (0, first_head + h)),
            pl.BlockSpec((2, n_near, rows, HD), lambda h, *_: (0, 0, 0, h)),
            pl.BlockSpec((2, max(n_far, 1), rows, HD), lambda h, *_: (0, 0, 0, h)),
        ],
        scratch_shapes=[pltpu.VMEM((n, rows, rows), F32)] * 2,
    )
    return pl.pallas_call(
        functools.partial(backward_kernel, offsets=ctx_offsets(), first_head=first_head),
        grid_spec=grid_spec,
        out_shape=[
            jax.ShapeDtypeStruct((rows, columns), BF16),
            jax.ShapeDtypeStruct((2, n_near, rows, heads * HD), BF16),
            jax.ShapeDtypeStruct((2, max(n_far, 1), rows, heads * HD), BF16),
        ],
        input_output_aliases={6 + n: 0} if extra else {},
        compiler_params=params(VMEM),
        cost_estimate=load(heavy),
    )(place, slopes, query, grad_mixed, start, stats, *keyvals, *extra)


def norm_backward(grad, unit, inverse, gain):
    scaled = grad * gain
    mean_scaled = jnp.mean(scaled, axis=-1, keepdims=True)
    mean_unit = jnp.mean(scaled * unit, axis=-1, keepdims=True)
    return inverse * (scaled - mean_scaled - unit * mean_unit)


def all_sum(values, axes):
    for axis in axes:
        bit = 1
        while bit < lax.axis_size(axis):
            values = values + xperm(values, axis, bit)
            bit *= 2
    return values


def spread_kernel(place, *refs, n_values, n_ctx, n_dp, piece):
    values, outs = refs[:n_values], refs[n_values:]
    for offset, out in enumerate(outs):
        for k, source in enumerate(values):
            for block in range(n_dp):
                column = (block * n_ctx + (place[0] ^ offset)) * piece
                part = source[:, pl.ds(pl.multiple_of(column, piece), piece)]
                row = (k * n_dp + block) * piece
                out[row : row + piece, :] = part.T


def spread_pieces(place, *values, heavy=0):
    tokens, width = values[0].shape
    n_dp, n_ctx = lax.axis_size("dp"), lax.axis_size("ctx")
    piece = width // (n_dp * n_ctx)
    shape = (len(values) * n_dp * piece, tokens)
    return pl.pallas_call(
        functools.partial(
            spread_kernel, n_values=len(values), n_ctx=n_ctx, n_dp=n_dp, piece=piece
        ),
        grid_spec=pltpu.PrefetchScalarGridSpec(
            num_scalar_prefetch=1,
            grid=(1,),
            in_specs=[pl.BlockSpec((tokens, width), lambda i, place: (0, 0))] * len(values),
            out_specs=[pl.BlockSpec(shape, lambda i, place: (0, 0))] * n_ctx,
        ),
        out_shape=[jax.ShapeDtypeStruct(shape, BF16)] * n_ctx,
        compiler_params=params(VMEM),
        cost_estimate=load(heavy),
    )(place, *values)


def spread_left(pieces):
    return [
        pieces[0] if offset == 0 else xperm(pieces[offset], "ctx", offset)
        for offset in ctx_offsets()
    ]


def shards(
    inputs,
    segments,
    first_gain,
    first_shift,
    in_weight,
    in_bias,
    out_weight,
    out_bias,
    second_gain,
    second_shift,
    up_weight,
    up_bias,
    down_weight,
    down_bias,
    cotangent,
):
    rows = inputs.shape[1]
    width = inputs.shape[2]
    local_width = in_weight.shape[2]
    local_hidden = up_weight.shape[1]
    heads_here = local_width // HD
    n_tensor = lax.axis_size("tensor")
    n_ctx = lax.axis_size("ctx")
    share = rows // n_tensor
    tensor_place = lax.axis_index("tensor")
    context_place = lax.axis_index("ctx")
    place = jnp.stack([context_place, lax.axis_index("dp")]).astype(jnp.int32)
    share_start = tensor_place * share

    def mine(values):
        return lax.dynamic_slice_in_dim(values, share_start, share, 0)

    head_index = (tensor_place * heads_here).astype(F32) + jnp.arange(heads_here, dtype=F32)
    slopes = jnp.exp2(-8.0 * (head_index + 1.0) / H)
    query_seg = lax.dynamic_slice_in_dim(segments[0], context_place * rows, rows)
    doc_start = jnp.sum(
        (segments[0][:, None] < query_seg[None, :]).astype(jnp.int32), axis=0, keepdims=True
    )

    gain_one, shift_one = first_gain.astype(F32), first_shift.astype(F32)
    gain_two, shift_two = second_gain.astype(F32), second_shift.astype(F32)
    second_vectors = jnp.stack([out_bias, second_gain, second_shift]).astype(F32)
    weight_in = in_weight.transpose(1, 0, 2)
    first_pair = jnp.stack([first_gain, first_shift]).astype(F32)
    cot_low = cotangent[0]

    order = []

    def then(values):
        values = after(values, order[-1]) if order else values
        return values

    def ran(values):
        order.append(jax.tree.leaves(values)[0])
        return values

    order = []

    def then(values):
        return after(values, order[-1]) if order else values

    def ran(values):
        order.append(jax.tree.leaves(values)[0])
        return values

    residual = inputs[0]
    groups = 2 if heads_here % 2 == 0 else 1
    group_heads = heads_here // groups
    group_width = group_heads * HD
    normed_first, *own = ran(
        project_kv(residual, first_pair, weight_in, in_bias, groups)
    )
    query = ran(
        mm(
            [then(normed_first)], [(weight_in, 0, 0)], trans=False, start=0, size=local_width,
            tile=1024, out_dtype=BF16, extras=(in_bias,), heavy=1,
        )
    )
    early_pieces = ran(spread_pieces(place, then(cot_low), normed_first, heavy=1))
    mixed, stats, keyvals = None, [], []
    for g in range(groups):
        keyvals.append(gather_ctx_causal(own[g], query if g == 0 else order[-1]))
        mixed, stat = ran(
            attention_forward(
                place, slopes, then(query), doc_start, keyvals[g], g * group_heads, group_heads,
                mixed,
            )
        )
        stats.append(stat)

    early_left = spread_left(lax.optimization_barrier((early_pieces, stats[0]))[0])

    def exchanged(part):
        return [part] + [xperm(part, "tensor", k) for k in range(1, n_tensor)]

    attention = exchanged(
        ran(
            mm(
                [then(mixed)], [out_weight], trans=True, start=0, size=width, tile=1024,
                out_dtype=BF16,
            )
        )
    )
    grad_active = ran(
        mm(
            [then(cot_low)], [down_weight], trans=False, start=0, size=local_hidden, tile=1024,
            out_dtype=F32,
        )
    )
    mixed_all = gather_ctx(mixed, [order[-1]])

    tile = local_hidden // 8
    half_hidden = local_hidden // 2
    up_bias_row = up_bias.astype(F32)[None]
    middle, normed_second, active_near, grad_near, bias_near = ran(
        first_up(
            residual, second_vectors, [after(then(attention[0]), early_left)] + attention[1:],
            up_weight, up_bias_row, grad_active, half_hidden, half_hidden, tile,
        )
    )
    active_far, grad_far, bias_far = ran(
        more_up(
            after(then(normed_second), mixed_all), up_weight, up_bias_row, grad_active,
            half_hidden, half_hidden, 2 * tile,
        )
    )

    def reduce_over_dp(parts, *deps):
        lefts, row, rights = parts[0]
        head = after(then(lefts[0]), *deps)
        whole = ran(
            weight_grad([([head] + lefts[1:], row, rights)] + parts[1:], width // n_ctx, 1024)
        )
        return lax.psum_scatter(whole, "dp", scatter_dimension=0, tiled=True)

    def grad_normed_part(side):
        part = ran(
            mm(
                [then(grad_near), grad_far], [(up_weight, None, 0), (up_weight, None, 1)],
                trans=True, start=side * (width // 2), size=width // 2, tile=512,
                out_dtype=BF16,
            )
        )
        return exchanged(part)

    normed_terms = [grad_normed_part(0), grad_normed_part(1)]
    near_rights = gather_ctx(active_near, [order[-1]])
    up_pieces = ran(spread_pieces(place, then(normed_second), heavy=1))
    down_parts = [reduce_over_dp([(early_left, 0, near_rights)])]
    near_sent = after(grad_near, order[-1])

    feed = ran(
        mm(
            [then(active_near), active_far],
            [(down_weight, None, 0), (down_weight, None, 1)], trans=True,
            start=0, size=width, tile=512, out_dtype=BF16, heavy=2,
        )
    )

    def tensor_scatter(values):
        total = mine(values).astype(F32)
        for k in range(1, n_tensor):
            piece = lax.dynamic_slice_in_dim(values, (tensor_place ^ k) * share, share, 0)
            total = total + xperm(piece, "tensor", k).astype(F32)
        return total

    feed_gate = order[-1]
    up_left = spread_left(up_pieces)

    def added(terms):
        total = after(terms[0], order[-1]).astype(F32)
        for term in terms[1:]:
            total = total + term.astype(F32)
        return total

    grad_normed = jnp.concatenate([added(terms) for terms in normed_terms], axis=1)
    unit_two, inverse_two = normalized(middle)
    cot = after(cot_low, order[-1]).astype(F32)
    grad_middle = cot + norm_backward(grad_normed, unit_two, inverse_two, gain_two)
    grad_middle_low = grad_middle.astype(BF16)
    grad_mixed = ran(
        mm(
            [then(grad_middle_low)], [out_weight], trans=False, start=0,
            size=local_width, tile=1024, out_dtype=BF16,
        )
    )
    down_parts.append(
        reduce_over_dp([(early_left, 0, gather_ctx(active_far, [feed_gate]))], up_left)
    )
    far_sent = after(grad_far, order[-1])
    grad_query, kv_near, kv_far = None, [], []
    for g in range(groups):
        grad_query, near, far = ran(
            attention_backward(
                place, slopes, then(query), grad_mixed, doc_start, stats[g], keyvals[g],
                g * group_heads, group_heads, grad_query, heavy=2 if g == 0 else 0,
            )
        )
        kv_near.append(near)
        kv_far.append(far)
    kv_received = [xperm(far, "ctx", 1) if n_ctx > 1 else None for far in kv_far]
    kv_near = after(kv_near, order[-1])

    near_all = gather_ctx(near_sent, [order[-1]])
    far_all = gather_ctx(far_sent, [order[-1]])
    up_part = reduce_over_dp([(up_left, 0, near_all), (up_left, 0, far_all)])
    up_gate = order[-1]
    late_pieces = ran(spread_pieces(place, then(grad_middle_low), heavy=2))
    late_left = spread_left(late_pieces)
    outputs = (mine(middle) + tensor_scatter(feed) + down_bias.astype(F32)).astype(BF16)

    grad_keys, grad_values = [], []
    for near, received in zip(kv_near, kv_received):
        blocks = [near[:, k] for k in range(near.shape[1])]
        if n_ctx > 1:
            blocks = [
                (block.astype(F32) + received[:, k].astype(F32))
                for k, block in enumerate(blocks)
            ]
            bits = ctx_bits()[:-1]
            for bit in reversed(bits):
                half = len(blocks) // 2
                got = [
                    xperm(sent.astype(BF16), "ctx", bit, lambda i, bit=bit: i > i ^ bit)
                    for sent in blocks[half:]
                ]
                blocks = [
                    after(block, order[-1]) + term.astype(F32)
                    for block, term in zip(blocks[:half], got)
                ]
        final = blocks[0].astype(BF16)
        grad_keys.append(final[0])
        grad_values.append(final[1])
    grad_keyvals = jnp.concatenate(grad_keys + grad_values, axis=1)
    gated = after(then(grad_keyvals), late_left)
    grad_first = ran(
        mm(
            [(grad_query, 0, local_width)] + [(gated, c, local_width) for c in range(2)],
            [(weight_in, c, 0) for c in range(3)], trans=True, start=0, size=width,
            tile=512, out_dtype=BF16, heavy=1,
        )
    )
    query_all = gather_ctx(after(grad_query, up_gate), [order[-1]])
    keyvals_all = gather_ctx(grad_keyvals, [order[-1]])
    joint_part = reduce_over_dp(
        [(late_left, 0, mixed_all), (early_left, 1, query_all), (early_left, 1, keyvals_all)],
        outputs,
    )
    grad_first_share = tensor_scatter(grad_first)
    unit_share, inverse_share = normalized(mine(inputs[0]).astype(F32))
    grad_from_first = norm_backward(grad_first_share, unit_share, inverse_share, gain_one)
    grad_middle_share = mine(grad_middle)
    input_grad = (grad_middle_share + grad_from_first).astype(BF16)

    def over_tokens(values):
        return jnp.sum(values, axis=0)

    grad_normed_share, unit_two_share = mine(grad_normed), mine(unit_two)
    sums = jnp.concatenate(
        [
            over_tokens(values).reshape(-1, local_width)
            for values in (
                grad_normed_share * unit_two_share,
                grad_normed_share,
                grad_middle_share,
                mine(cot),
                grad_first_share * unit_share,
                grad_first_share,
            )
        ]
    )
    count = sums.shape[0]
    sums = all_sum(sums, ("tensor",))
    sums = jnp.concatenate(
        [
            sums,
            over_tokens(grad_query.astype(F32))[None],
            over_tokens(grad_keyvals[:, local_width:].astype(F32))[None],
            jnp.concatenate([bias_near, bias_far], axis=1).reshape(-1, local_width),
        ]
    )
    sums = all_sum(sums, ("ctx", "dp"))
    vectors = sums[:count].reshape(6, width)
    in_bias_grad = sums[count : count + 2]
    up_bias_grad = sums[count + 2 :].reshape(-1)

    down_weight_grad = jnp.concatenate([part.astype(F32) for part in down_parts], axis=1)
    up_weight_grad = up_part.astype(F32)
    out_weight_grad, in_weight_grad = widen_joint(joint_part, local_width)
    return (
        outputs[None],
        input_grad[None],
        vectors[4],
        vectors[5],
        in_weight_grad.transpose(1, 0, 2),
        in_bias_grad,
        out_weight_grad,
        vectors[2],
        vectors[0],
        vectors[1],
        up_weight_grad,
        up_bias_grad,
        down_weight_grad,
        vectors[3],
    )


def solution(mesh):
    return jax.shard_map(
        shards,
        mesh=mesh,
        in_specs=(
            P("dp", "ctx", None),
            P("dp", None),
            P(),
            P(),
            P(None, None, "tensor"),
            P(None, "tensor"),
            P(None, "tensor"),
            P(),
            P(),
            P(),
            P(None, "tensor"),
            P("tensor"),
            P(None, "tensor"),
            P(),
            P("dp", "ctx", None),
        ),
        out_specs=(
            P("dp", ("ctx", "tensor"), None),
            P("dp", ("ctx", "tensor"), None),
            P(),
            P(),
            P(("dp", "ctx"), None, "tensor"),
            P(None, "tensor"),
            P(("dp", "ctx"), "tensor"),
            P(),
            P(),
            P(),
            P(("dp", "ctx"), "tensor"),
            P("tensor"),
            P(("dp", "ctx"), "tensor"),
            P(),
        ),
        check_vma=False,
    )
```

```python
import functools
import math

import jax
import jax.numpy as jnp
from jax import lax
from jax.experimental import pallas as pl
from jax.experimental.pallas import tpu as pltpu
from jax.sharding import PartitionSpec as P

H = 16
HD = 128
EPSILON = 1e-05
MASKED = -1e30
MIB = 1 << 20
GELU_C = math.sqrt(2.0 / math.pi)
GELU_A = 0.044715

BF16 = jnp.bfloat16
F32 = jnp.float32


VMEM = 40
ALL_VMEM = 60


def params(limit):
    return pltpu.CompilerParams(vmem_limit_bytes=limit * MIB)


def load(level=0):
    if not level:
        return None
    return pl.CostEstimate(flops=10 ** (8 + 2 * level), bytes_accessed=10**7, transcendentals=0)


def xperm(values, axis, bit, wanted=None):
    pairs = [
        (i, i ^ bit) for i in range(lax.axis_size(axis)) if wanted is None or wanted(i)
    ]
    return lax.ppermute(values, axis, pairs)


def after(values, *deps):
    return lax.optimization_barrier((values,) + deps)[0]


def ctx_bits():
    n = lax.axis_size("ctx")
    return [1 << b for b in reversed(range(n.bit_length() - 1))]


def ctx_offsets():
    offsets = [0]
    for bit in ctx_bits():
        offsets = offsets + [o ^ bit for o in offsets]
    return offsets


def gather_first(block):
    bits = ctx_bits()
    return [block] + ([xperm(block, "ctx", bits[0])] if bits else [])


def gather_rest(blocks, gate):
    blocks = lax.optimization_barrier((blocks, gate))[0]
    for bit in ctx_bits()[1:]:
        blocks = blocks + [xperm(b, "ctx", bit) for b in blocks]
    return blocks


def gather_ctx(block, gate):
    return gather_rest(gather_first(block), gate)


def gather_ctx_causal(block, gate, first_gate=None):
    blocks, offsets = [block], [0]
    for bit in ctx_bits():
        fresh = []
        for b, o in zip(blocks, offsets):
            if o:
                b = after(b, gate)
            elif first_gate is not None and bit > 1:
                b = after(b, first_gate)
            fresh.append(
                xperm(b, "ctx", bit, lambda i, o=o, bit=bit: (i ^ o) < (i ^ bit))
            )
        blocks = blocks + fresh
        offsets = offsets + [o ^ bit for o in offsets]
    return blocks


def mm_kernel(*refs, n_pairs, trans):
    lefts, rights = refs[:n_pairs], refs[n_pairs : 2 * n_pairs]
    extras, out = refs[2 * n_pairs : -1], refs[-1]
    total = None
    for left, right in zip(lefts, rights):
        term = lax.dot_general(
            left[...],
            right[...],
            (((1,), (1 if trans else 0,)), ((), ())),
            preferred_element_type=F32,
        )
        total = term if total is None else total + term
    for extra in extras:
        row = extra[0:1, :] if extra.shape[0] == 2 else extra[...]
        total = total + row.astype(F32)
    out[...] = total.astype(out.dtype)


def mm(lefts, rights, *, trans, start, size, tile, out_dtype, extras=(), heavy=0):
    lefts = [left if isinstance(left, tuple) else (left, 0, left.shape[1]) for left in lefts]
    rows = lefts[0][0].shape[0]
    tile = math.gcd(tile, size)
    first = start // tile
    specs, operands = [], []
    for left, column, depth in lefts:
        specs.append(pl.BlockSpec((rows, depth), lambda i, column=column: (0, column)))
        operands.append(left)
    for (left, column, depth), right in zip(lefts, rights):
        lead, part = None, 0
        if isinstance(right, tuple):
            right, lead, part = right
        shape = (tile, depth) if trans else (depth, tile)

        def place(i, lead=lead, part=part):
            where = (first + i, part) if trans else (part, first + i)
            return where if lead is None else (lead,) + where

        specs.append(pl.BlockSpec(((None,) if lead is not None else ()) + shape, place))
        operands.append(right)
    for extra in extras:
        specs.append(pl.BlockSpec((extra.shape[0], tile), lambda i: (0, first + i)))
        operands.append(extra)
    return pl.pallas_call(
        functools.partial(mm_kernel, n_pairs=len(lefts), trans=trans),
        grid=(size // tile,),
        in_specs=specs,
        out_specs=pl.BlockSpec((rows, tile), lambda i: (0, i)),
        out_shape=jax.ShapeDtypeStruct((rows, size), out_dtype),
        compiler_params=params(VMEM),
        cost_estimate=load(heavy),
    )(*operands)


def kv_kernel(values, gain, shift, weight, bias, norm, *outs):
    @pl.when(pl.program_id(0) == 0)
    def _():
        unit, _ = normalized(values[...].astype(F32))
        scale, offset = gain[...].astype(F32), shift[...].astype(F32)
        norm[...] = (unit * scale[None, :] + offset[None, :]).astype(BF16)

    shifted = bias[1:2, :].astype(F32) * pl.program_id(0).astype(F32)
    total = jnp.dot(norm[...], weight[...], preferred_element_type=F32) + shifted
    size = outs[0].shape[1]
    for k, out in enumerate(outs):
        out[...] = total[:, k * size : (k + 1) * size].astype(out.dtype)


def project_kv(values, gain, shift, weight, bias, groups):
    rows, width = values.shape
    columns = weight.shape[2]
    size = columns // groups
    whole = pl.BlockSpec((rows, width), lambda c: (0, 0))
    return pl.pallas_call(
        kv_kernel,
        grid=(2,),
        in_specs=[
            whole,
            pl.BlockSpec((width,), lambda c: (0,)),
            pl.BlockSpec((width,), lambda c: (0,)),
            pl.BlockSpec((None, width, columns), lambda c: (c + 1, 0, 0)),
            pl.BlockSpec((2, columns), lambda c: (0, 0)),
        ],
        out_specs=[whole]
        + [pl.BlockSpec((None, rows, size), lambda c: (c, 0, 0))] * groups,
        out_shape=[jax.ShapeDtypeStruct((rows, width), BF16)]
        + [jax.ShapeDtypeStruct((2, rows, size), BF16)] * groups,
        compiler_params=params(ALL_VMEM),
        cost_estimate=load(),
    )(values, gain, shift, weight, bias)


def normalized(values):
    average = jnp.mean(values, axis=-1, keepdims=True)
    centered = values - average
    spread = jnp.mean(centered * centered, axis=-1, keepdims=True)
    inverse = lax.rsqrt(spread + EPSILON)
    return centered * inverse, inverse


def up_block(norm, weight, bias, grad_active, active, grad_upper, bias_sum):
    upper = jnp.dot(norm[...], weight[...], preferred_element_type=F32) + bias[...]
    square = upper * upper
    wave = jnp.tanh(GELU_C * (upper + GELU_A * square * upper))
    half = 0.5 * (1.0 + wave)
    active[...] = (upper * half).astype(BF16)
    slope = half + 0.5 * upper * (1.0 - wave * wave) * (
        GELU_C * (1.0 + 3.0 * GELU_A * square)
    )
    grad = (grad_active[...] * slope).astype(BF16)
    grad_upper[...] = grad
    bias_sum[...] = jnp.sum(grad.astype(F32), axis=0, keepdims=True)


def up_kernel(norm, weight, bias, grad_active, *refs):
    up_block(norm, weight, bias, grad_active, *refs[-3:])


def first_up_kernel(*refs, n_terms):
    values, vectors = refs[:2]
    terms, (weight, bias, grad_active) = refs[2 : 2 + n_terms], refs[2 + n_terms : 5 + n_terms]
    middle, norm, active, grad_upper, bias_sum = refs[5 + n_terms :]

    @pl.when(pl.program_id(0) == 0)
    def _():
        total = terms[0][...].astype(F32)
        for term in terms[1:]:
            total = total + term[...].astype(F32)
        middle[...] = values[...].astype(F32) + total + vectors[0:1, :]
        unit, _ = normalized(middle[...])
        norm[...] = (unit * vectors[1:2, :] + vectors[2:3, :]).astype(BF16)

    up_block(norm, weight, bias, grad_active, active, grad_upper, bias_sum)


def up_specs(width, rows, tile, first, out_first=0):
    ins = [
        pl.BlockSpec((width, tile), lambda i: (0, first + i)),
        pl.BlockSpec((1, tile), lambda i: (0, first + i)),
        pl.BlockSpec((rows, tile), lambda i: (0, first + i)),
    ]
    outs = [
        pl.BlockSpec((rows, tile), lambda i: (0, i)),
        pl.BlockSpec((rows, tile), lambda i: (0, out_first + i)),
        pl.BlockSpec((1, tile), lambda i: (0, i)),
    ]
    return ins, outs


def up_shapes(rows, size, local):
    return [
        jax.ShapeDtypeStruct((rows, size), BF16),
        jax.ShapeDtypeStruct((rows, local), BF16),
        jax.ShapeDtypeStruct((1, size), F32),
    ]


def first_up(values, vectors, terms, weight, bias, grad_active, size, local, tile):
    rows, width = values.shape
    whole = pl.BlockSpec((rows, width), lambda i: (0, 0))
    ins, outs = up_specs(width, rows, tile, 0)
    return pl.pallas_call(
        functools.partial(first_up_kernel, n_terms=len(terms)),
        grid=(size // tile,),
        in_specs=[whole, pl.BlockSpec((3, width), lambda i: (0, 0))] + [whole] * len(terms) + ins,
        out_specs=[whole, whole] + outs,
        out_shape=[
            jax.ShapeDtypeStruct((rows, width), F32),
            jax.ShapeDtypeStruct((rows, width), BF16),
        ]
        + up_shapes(rows, size, local),
        compiler_params=params(VMEM),
        cost_estimate=load(),
    )(values, vectors, *terms, weight, bias, grad_active)


def more_up(norm, weight, bias, grad_active, start, size, tile, held=None, heavy=0):
    rows, width = norm.shape
    ins, outs = up_specs(width, rows, tile, start // tile, 0 if held is None else start // tile)
    in_specs = [pl.BlockSpec((rows, width), lambda i: (0, 0))] + ins
    operands = [norm, weight, bias, grad_active]
    if held is not None:
        in_specs.append(pl.BlockSpec(memory_space=pl.ANY))
        operands.append(held)
    return pl.pallas_call(
        up_kernel,
        grid=(size // tile,),
        in_specs=in_specs,
        out_specs=outs,
        out_shape=up_shapes(rows, size, size if held is None else held.shape[1]),
        input_output_aliases={} if held is None else {4: 1},
        compiler_params=params(VMEM),
        cost_estimate=load(heavy),
    )(*operands)


def weight_grad_kernel(*refs, blocks, n):
    out, step, first = refs[-1], pl.program_id(0), 0

    def summed(lefts, rights):
        total = None
        for left, right in zip(lefts, rights):
            term = jnp.dot(left[...], right[...], preferred_element_type=F32)
            total = term if total is None else total + term
        out[...] = total.astype(out.dtype)

    for part, count in enumerate(blocks):
        lefts = refs[2 * n * part : 2 * n * part + n]
        rights = refs[2 * n * part + n : 2 * n * (part + 1)]
        if len(blocks) == 1:
            summed(lefts, rights)
        else:
            pl.when((step >= first) & (step < first + count))(
                functools.partial(summed, lefts, rights)
            )
        first += count


def weight_grad(parts, rows, tile):
    n = len(parts[0][0])
    tokens = parts[0][0][0].shape[1]
    for _, _, rights in parts:
        tile = math.gcd(tile, rights[0].shape[1])
    blocks = [rights[0].shape[1] // tile for _, _, rights in parts]
    specs, operands, first = [], [], 0
    for (lefts, row, rights), count in zip(parts, blocks):

        def place(i, first=first, count=count):
            return (0, jnp.clip(i - first, 0, count - 1))

        specs += [pl.BlockSpec((rows, tokens), lambda i, row=row: (row, 0))] * n
        specs += [pl.BlockSpec((tokens, tile), place)] * n
        operands += list(lefts) + list(rights)
        first += count
    return pl.pallas_call(
        functools.partial(weight_grad_kernel, blocks=blocks, n=n),
        grid=(first,),
        in_specs=specs,
        out_specs=pl.BlockSpec((rows, tile), lambda i: (0, i)),
        out_shape=jax.ShapeDtypeStruct((rows, first * tile), BF16),
        compiler_params=params(ALL_VMEM),
        cost_estimate=load(),
    )(*operands)


def widen_kernel(values, first, other):
    @pl.when(pl.program_id(0) == 0)
    def _():
        first[...] = values[...].astype(F32)

    @pl.when(pl.program_id(0) > 0)
    def _():
        other[...] = values[...].astype(F32)


def widen_joint(values, tile):
    rows, size = values.shape
    blocks = size // tile
    return pl.pallas_call(
        widen_kernel,
        grid=(blocks,),
        in_specs=[pl.BlockSpec((rows, tile), lambda i: (0, i))],
        out_specs=[
            pl.BlockSpec((rows, tile), lambda i: (0, 0)),
            pl.BlockSpec((None, rows, tile), lambda i: (jnp.maximum(i - 1, 0), 0, 0)),
        ],
        out_shape=[
            jax.ShapeDtypeStruct((rows, tile), F32),
            jax.ShapeDtypeStruct((blocks - 1, rows, tile), F32),
        ],
        compiler_params=params(VMEM),
        cost_estimate=load(),
    )(values)


def distances(context_place, doc_start, rows):
    query_pos = context_place * rows + jnp.arange(rows, dtype=jnp.int32)[None, :]
    blocks = []
    for offset in ctx_offsets():
        key_pos = (context_place ^ offset) * rows + jnp.arange(rows, dtype=jnp.int32)[:, None]
        allowed = (key_pos <= query_pos) & (key_pos >= doc_start)
        blocks.append(jnp.where(allowed, (key_pos - query_pos).astype(F32), MASKED))
    return jnp.stack(blocks)


def block_scores(slope, query, key, distance):
    raw = lax.dot_general(key, query, (((1,), (1,)), ((), ())), preferred_element_type=F32)
    return raw * (1.0 / math.sqrt(HD)) + slope * distance


def forward_kernel(slopes, query, distance, *refs, n, first_head):
    keyvals, (mixed, stats, held) = refs[:n], refs[-3:]
    slope = slopes[first_head + pl.program_id(0)]
    top = None
    for k in range(n):
        raw = block_scores(slope, query[...], keyvals[k][0], distance[k])
        held[k] = raw
        peak = jnp.max(raw, axis=0, keepdims=True)
        top = peak if top is None else jnp.maximum(top, peak)
    total = None
    for k in range(n):
        fresh = jnp.exp(held[k] - top)
        held[k] = fresh
        part = jnp.sum(fresh, axis=0, keepdims=True)
        total = part if total is None else total + part
    stats[...] = top + jnp.log(total)
    inverse = 1.0 / total
    result = None
    for k in range(n):
        probs = (held[k] * inverse).astype(BF16)
        term = lax.dot_general(
            probs, keyvals[k][1], (((0,), (0,)), ((), ())), preferred_element_type=F32
        )
        result = term if result is None else result + term
    mixed[...] = result.astype(mixed.dtype)


def attention_forward(slopes, query, distance, keyvals, first_head, heads, held=None):
    rows, columns = query.shape
    extra = [] if held is None else [held]
    n = len(keyvals)
    grid_spec = pltpu.PrefetchScalarGridSpec(
        num_scalar_prefetch=1,
        grid=(heads,),
        in_specs=[
            pl.BlockSpec((rows, HD), lambda h, *_: (0, first_head + h)),
            pl.BlockSpec((n, rows, rows), lambda h, *_: (0, 0, 0)),
        ]
        + [pl.BlockSpec((2, rows, HD), lambda h, *_: (0, 0, h))] * n
        + [pl.BlockSpec(memory_space=pl.ANY)] * len(extra),
        out_specs=[
            pl.BlockSpec((rows, HD), lambda h, *_: (0, first_head + h)),
            pl.BlockSpec((None, 1, rows), lambda h, *_: (h, 0, 0)),
        ],
        scratch_shapes=[pltpu.VMEM((n, rows, rows), F32)],
    )
    return pl.pallas_call(
        functools.partial(forward_kernel, n=n, first_head=first_head),
        grid_spec=grid_spec,
        out_shape=[
            jax.ShapeDtypeStruct((rows, columns), BF16),
            jax.ShapeDtypeStruct((heads, 1, rows), F32),
        ],
        input_output_aliases={3 + n: 0} if extra else {},
        compiler_params=params(VMEM),
        cost_estimate=load(),
    )(slopes, query, distance, *keyvals, *extra)


def backward_kernel(slopes, query, grad_mixed, distance, stats, *refs, n, first_head):
    keyvals = refs[:n]
    grad_query, near, far, probs_held, grads_held = refs[-5:]
    slope = slopes[first_head + pl.program_id(0)]
    scale = 1.0 / math.sqrt(HD)
    delta = None
    for k in range(n):
        raw = block_scores(slope, query[...], keyvals[k][0], distance[k])
        probs = jnp.exp(raw - stats[...])
        grads = lax.dot_general(
            keyvals[k][1],
            grad_mixed[...],
            (((1,), (1,)), ((), ())),
            preferred_element_type=F32,
        )
        probs_held[k] = probs
        grads_held[k] = grads
        part = jnp.sum(probs * grads, axis=0, keepdims=True)
        delta = part if delta is None else delta + part
    total = None
    for k in range(n):
        probs = probs_held[k]
        grad_scores = (probs * (grads_held[k] - delta)).astype(BF16)
        term = lax.dot_general(
            grad_scores,
            keyvals[k][0],
            (((0,), (0,)), ((), ())),
            preferred_element_type=F32,
        )
        total = term if total is None else total + term
        key_grad = jnp.dot(grad_scores, query[...], preferred_element_type=F32) * scale
        value_grad = jnp.dot(
            probs.astype(BF16), grad_mixed[...], preferred_element_type=F32
        )
        target, slot = (near, k) if k < n - n // 2 else (far, k - (n - n // 2))
        target[0, slot] = key_grad.astype(target.dtype)
        target[1, slot] = value_grad.astype(target.dtype)
    grad_query[...] = (total * scale).astype(grad_query.dtype)


def attention_backward(
    slopes, query, grad_mixed, distance, stats, keyvals, first_head, heads, held=None,
    heavy=0,
):
    rows, columns = query.shape
    extra = [] if held is None else [held]
    n = len(keyvals)
    n_far = n // 2
    n_near = n - n_far
    grid_spec = pltpu.PrefetchScalarGridSpec(
        num_scalar_prefetch=1,
        grid=(heads,),
        in_specs=[
            pl.BlockSpec((rows, HD), lambda h, *_: (0, first_head + h)),
            pl.BlockSpec((rows, HD), lambda h, *_: (0, first_head + h)),
            pl.BlockSpec((n, rows, rows), lambda h, *_: (0, 0, 0)),
            pl.BlockSpec((None, 1, rows), lambda h, *_: (h, 0, 0)),
        ]
        + [pl.BlockSpec((2, rows, HD), lambda h, *_: (0, 0, h))] * n
        + [pl.BlockSpec(memory_space=pl.ANY)] * len(extra),
        out_specs=[
            pl.BlockSpec((rows, HD), lambda h, *_: (0, first_head + h)),
            pl.BlockSpec((2, n_near, rows, HD), lambda h, *_: (0, 0, 0, h)),
            pl.BlockSpec((2, max(n_far, 1), rows, HD), lambda h, *_: (0, 0, 0, h)),
        ],
        scratch_shapes=[pltpu.VMEM((n, rows, rows), F32)] * 2,
    )
    return pl.pallas_call(
        functools.partial(backward_kernel, n=n, first_head=first_head),
        grid_spec=grid_spec,
        out_shape=[
            jax.ShapeDtypeStruct((rows, columns), BF16),
            jax.ShapeDtypeStruct((2, n_near, rows, heads * HD), BF16),
            jax.ShapeDtypeStruct((2, max(n_far, 1), rows, heads * HD), BF16),
        ],
        input_output_aliases={5 + n: 0} if extra else {},
        compiler_params=params(VMEM),
        cost_estimate=load(heavy),
    )(slopes, query, grad_mixed, distance, stats, *keyvals, *extra)


def norm_backward(grad, unit, inverse, gain):
    scaled = grad * gain
    mean_scaled = jnp.mean(scaled, axis=-1, keepdims=True)
    mean_unit = jnp.mean(scaled * unit, axis=-1, keepdims=True)
    return inverse * (scaled - mean_scaled - unit * mean_unit)


def all_sum(values, axes):
    for axis in axes:
        bit = 1
        while bit < lax.axis_size(axis):
            values = values + xperm(values, axis, bit)
            bit *= 2
    return values


def spread_kernel(place, *refs, n_values, n_ctx, n_dp, piece):
    values, outs = refs[:n_values], refs[n_values:]
    for offset, out in enumerate(outs):
        for k, source in enumerate(values):
            for block in range(n_dp):
                column = (block * n_ctx + (place[0] ^ offset)) * piece
                part = source[:, pl.ds(pl.multiple_of(column, piece), piece)]
                row = (k * n_dp + block) * piece
                out[row : row + piece, :] = part.T


def spread_pieces(place, *values, heavy=0):
    tokens, width = values[0].shape
    n_dp, n_ctx = lax.axis_size("dp"), lax.axis_size("ctx")
    piece = width // (n_dp * n_ctx)
    shape = (len(values) * n_dp * piece, tokens)
    return pl.pallas_call(
        functools.partial(
            spread_kernel, n_values=len(values), n_ctx=n_ctx, n_dp=n_dp, piece=piece
        ),
        grid_spec=pltpu.PrefetchScalarGridSpec(
            num_scalar_prefetch=1,
            grid=(1,),
            in_specs=[pl.BlockSpec((tokens, width), lambda i, place: (0, 0))] * len(values),
            out_specs=[pl.BlockSpec(shape, lambda i, place: (0, 0))] * n_ctx,
        ),
        out_shape=[jax.ShapeDtypeStruct(shape, BF16)] * n_ctx,
        compiler_params=params(VMEM),
        cost_estimate=load(heavy),
    )(place, *values)


def spread_left(pieces):
    return [
        pieces[0] if offset == 0 else xperm(pieces[offset], "ctx", offset)
        for offset in ctx_offsets()
    ]


def shards(
    inputs,
    segments,
    first_gain,
    first_shift,
    in_weight,
    in_bias,
    out_weight,
    out_bias,
    second_gain,
    second_shift,
    up_weight,
    up_bias,
    down_weight,
    down_bias,
    cotangent,
):
    rows = inputs.shape[1]
    width = inputs.shape[2]
    local_width = in_weight.shape[2]
    local_hidden = up_weight.shape[1]
    heads_here = local_width // HD
    n_tensor = lax.axis_size("tensor")
    n_ctx = lax.axis_size("ctx")
    share = rows // n_tensor
    tensor_place = lax.axis_index("tensor")
    context_place = lax.axis_index("ctx")
    place = jnp.stack([context_place, lax.axis_index("dp")]).astype(jnp.int32)
    share_start = tensor_place * share

    def mine(values):
        return lax.dynamic_slice_in_dim(values, share_start, share, 0)

    head_index = (tensor_place * heads_here).astype(F32) + jnp.arange(heads_here, dtype=F32)
    slopes = jnp.exp2(-8.0 * (head_index + 1.0) / H)
    query_seg = lax.dynamic_slice_in_dim(segments[0], context_place * rows, rows)
    doc_start = jnp.sum(
        (segments[0][:, None] < query_seg[None, :]).astype(jnp.int32), axis=0, keepdims=True
    )

    distance = distances(context_place, doc_start, rows)
    gain_one, shift_one = first_gain.astype(F32), first_shift.astype(F32)
    gain_two, shift_two = second_gain.astype(F32), second_shift.astype(F32)
    second_vectors = jnp.stack([out_bias, second_gain, second_shift]).astype(F32)
    weight_in = in_weight.transpose(1, 0, 2)
    cot_low = cotangent[0]

    order = []

    def then(values):
        return after(values, order[-1]) if order else values

    def ran(values):
        order.append(jax.tree.leaves(values)[0])
        return values

    residual = inputs[0]
    groups = 2 if heads_here % 2 == 0 else 1
    group_heads = heads_here // groups
    group_width = group_heads * HD
    normed_first, *own = ran(
        project_kv(residual, first_gain, first_shift, weight_in, in_bias, groups)
    )
    query = ran(
        mm(
            [after(then(normed_first), distance, slopes)], [(weight_in, 0, 0)], trans=False, start=0, size=local_width,
            tile=1024, out_dtype=BF16, extras=(in_bias,), heavy=1,
        )
    )
    early_pieces = ran(spread_pieces(place, then(cot_low), normed_first, heavy=1))
    mixed, stats, keyvals = None, [], []
    for g in range(groups):
        keyvals.append(
            gather_ctx_causal(own[g], query if g == 0 else order[-1], query if g else None)
        )
        mixed, stat = ran(
            attention_forward(
                slopes, then(query), distance, keyvals[g], g * group_heads, group_heads, mixed,
            )
        )
        stats.append(stat)

    def exchanged(part):
        return [part] + [xperm(part, "tensor", k) for k in range(1, n_tensor)]

    attention = exchanged(
        ran(
            mm(
                [then(mixed)], [out_weight], trans=True, start=0, size=width, tile=1024,
                out_dtype=BF16,
            )
        )
    )
    out_gate = order[-1]
    early_left = spread_left(lax.optimization_barrier((early_pieces, out_gate))[0])
    mixed_sent = after(mixed, out_gate)
    grad_active = ran(
        mm(
            [then(cot_low)], [down_weight], trans=False, start=0,
            size=local_hidden, tile=1024, out_dtype=F32, heavy=2,
        )
    )

    tile = local_hidden // 8
    half_hidden = local_hidden // 2
    up_bias_row = up_bias.astype(F32)[None]
    middle, normed_second, active_near, grad_near, bias_near = ran(
        first_up(
            residual, second_vectors, [then(attention[0])] + attention[1:],
            up_weight, up_bias_row, grad_active, half_hidden, half_hidden, tile,
        )
    )
    mixed_seen = gather_first(mixed_sent)
    active_far, grad_far, bias_far = ran(
        more_up(
            after(then(normed_second), early_left), up_weight, up_bias_row, grad_active,
            half_hidden, half_hidden, 2 * tile, heavy=2,
        )
    )

    def reduce_over_dp(parts, *deps):
        lefts, row, rights = parts[0]
        head = after(then(lefts[0]), *deps)
        whole = ran(
            weight_grad([([head] + lefts[1:], row, rights)] + parts[1:], width // n_ctx, 1024)
        )
        return lax.psum_scatter(whole, "dp", scatter_dimension=0, tiled=True)

    def grad_normed_part(side):
        part = ran(
            mm(
                [after(then(grad_near), mixed_seen), grad_far],
                [(up_weight, None, 0), (up_weight, None, 1)],
                trans=True, start=side * (width // 2), size=width // 2, tile=512,
                out_dtype=BF16,
            )
        )
        return exchanged(part)

    normed_terms = [grad_normed_part(0), grad_normed_part(1)]
    near_rights = gather_ctx(active_near, order[-1])
    up_pieces = ran(spread_pieces(place, then(normed_second), heavy=1))
    down_parts = [reduce_over_dp([(early_left, 0, near_rights)])]
    near_sent = after(grad_near, order[-1])

    feed = ran(
        mm(
            [then(active_near), active_far],
            [(down_weight, None, 0), (down_weight, None, 1)], trans=True,
            start=0, size=width, tile=512, out_dtype=BF16, heavy=2,
        )
    )

    def tensor_scatter(values):
        total = mine(values).astype(F32)
        for k in range(1, n_tensor):
            piece = lax.dynamic_slice_in_dim(values, (tensor_place ^ k) * share, share, 0)
            total = total + xperm(piece, "tensor", k).astype(F32)
        return total

    feed_gate = order[-1]
    up_left = spread_left(up_pieces)

    def added(terms):
        total = after(terms[0], order[-1]).astype(F32)
        for term in terms[1:]:
            total = total + term.astype(F32)
        return total

    grad_normed = jnp.concatenate([added(terms) for terms in normed_terms], axis=1)
    unit_two, inverse_two = normalized(middle)
    cot = after(cot_low, order[-1]).astype(F32)
    grad_middle = cot + norm_backward(grad_normed, unit_two, inverse_two, gain_two)
    grad_middle_low = grad_middle.astype(BF16)
    grad_mixed = ran(
        mm(
            [then(grad_middle_low)], [out_weight], trans=False, start=0,
            size=local_width, tile=1024, out_dtype=BF16, heavy=1,
        )
    )
    down_parts.append(
        reduce_over_dp([(early_left, 0, gather_ctx(active_far, feed_gate))], up_left)
    )
    far_sent = after(grad_far, order[-1])
    mixed_all = gather_rest(mixed_seen, order[-1])
    grad_query, kv_near, kv_far = None, [], []
    for g in range(groups):
        grad_query, near, far = ran(
            attention_backward(
                slopes, after(then(query), mixed_all if g else []), grad_mixed, distance, stats[g],
                keyvals[g],
                g * group_heads, group_heads, grad_query, heavy=2 if g == 0 else 0,
            )
        )
        kv_near.append(near)
        kv_far.append(far)
    kv_received = [xperm(far, "ctx", 1) if n_ctx > 1 else None for far in kv_far]
    kv_near = after(kv_near, order[-1])

    near_all = gather_ctx(near_sent, order[-1])
    partial = []
    for near, received in zip(kv_near, kv_received):
        blocks = [near[:, k].astype(F32) for k in range(near.shape[1])]
        if n_ctx > 1:
            blocks = [block + received[:, k].astype(F32) for k, block in enumerate(blocks)]
        partial.append(blocks)
    sent = [block.astype(BF16) for blocks in partial for block in blocks[len(blocks) // 2 :]]
    far_all = gather_ctx(far_sent, sent)
    up_part = reduce_over_dp([(up_left, 0, near_all), (up_left, 0, far_all)])
    up_gate = order[-1]
    late_pieces = ran(spread_pieces(place, then(grad_middle_low), heavy=2))
    late_left = spread_left(late_pieces)
    outputs = (mine(middle) + tensor_scatter(feed) + down_bias.astype(F32)).astype(BF16)

    grad_keys, grad_values = [], []
    for g, blocks in enumerate(partial):
        send_gate = up_gate if g else []
        for bit in reversed(ctx_bits()[:-1]):
            half = len(blocks) // 2
            got = [
                xperm(
                    after(block.astype(BF16), send_gate), "ctx", bit, lambda i, bit=bit: i > i ^ bit
                )
                for block in blocks[half:]
            ]
            blocks = [
                after(block, order[-1]) + term.astype(F32)
                for block, term in zip(blocks[:half], got)
            ]
        final = blocks[0].astype(BF16)
        grad_keys.append(final[0])
        grad_values.append(final[1])
    grad_keyvals = jnp.concatenate(grad_keys + grad_values, axis=1)
    gated = after(then(grad_keyvals), late_left)
    grad_first = ran(
        mm(
            [(grad_query, 0, local_width)] + [(gated, c, local_width) for c in range(2)],
            [(weight_in, c, 0) for c in range(3)], trans=True, start=0, size=width,
            tile=512, out_dtype=BF16, heavy=1,
        )
    )
    query_all = gather_ctx(after(grad_query, up_gate), order[-1])
    keyvals_all = gather_ctx(grad_keyvals, order[-1])
    joint_part = reduce_over_dp(
        [(late_left, 0, mixed_all), (early_left, 1, query_all), (early_left, 1, keyvals_all)],
        outputs,
    )
    grad_first_share = tensor_scatter(grad_first)
    unit_share, inverse_share = normalized(mine(inputs[0]).astype(F32))
    grad_from_first = norm_backward(grad_first_share, unit_share, inverse_share, gain_one)
    grad_middle_share = mine(grad_middle)
    input_grad = (grad_middle_share + grad_from_first).astype(BF16)

    def over_tokens(values):
        return jnp.sum(values, axis=0)

    grad_normed_share, unit_two_share = mine(grad_normed), mine(unit_two)
    sums = jnp.concatenate(
        [
            over_tokens(values).reshape(-1, local_width)
            for values in (
                grad_normed_share * unit_two_share,
                grad_normed_share,
                grad_middle_share,
                mine(cot),
                grad_first_share * unit_share,
                grad_first_share,
            )
        ]
    )
    count = sums.shape[0]
    sums = all_sum(sums, ("tensor",))
    sums = jnp.concatenate(
        [
            sums,
            over_tokens(grad_query.astype(F32))[None],
            over_tokens(grad_keyvals[:, local_width:].astype(F32))[None],
            jnp.concatenate([bias_near, bias_far], axis=1).reshape(-1, local_width),
        ]
    )
    sums = all_sum(sums, ("ctx", "dp"))
    vectors = sums[:count].reshape(6, width)
    in_bias_grad = sums[count : count + 2]
    up_bias_grad = sums[count + 2 :].reshape(-1)

    down_weight_grad = jnp.concatenate([part.astype(F32) for part in down_parts], axis=1)
    up_weight_grad = up_part.astype(F32)
    out_weight_grad, in_weight_grad = widen_joint(joint_part, local_width)
    return (
        outputs[None],
        input_grad[None],
        vectors[4],
        vectors[5],
        in_weight_grad.transpose(1, 0, 2),
        in_bias_grad,
        out_weight_grad,
        vectors[2],
        vectors[0],
        vectors[1],
        up_weight_grad,
        up_bias_grad,
        down_weight_grad,
        vectors[3],
    )


def solution(mesh):
    return jax.shard_map(
        shards,
        mesh=mesh,
        in_specs=(
            P("dp", "ctx", None),
            P("dp", None),
            P(),
            P(),
            P(None, None, "tensor"),
            P(None, "tensor"),
            P(None, "tensor"),
            P(),
            P(),
            P(),
            P(None, "tensor"),
            P("tensor"),
            P(None, "tensor"),
            P(),
            P("dp", "ctx", None),
        ),
        out_specs=(
            P("dp", ("ctx", "tensor"), None),
            P("dp", ("ctx", "tensor"), None),
            P(),
            P(),
            P(("dp", "ctx"), None, "tensor"),
            P(None, "tensor"),
            P(("dp", "ctx"), "tensor"),
            P(),
            P(),
            P(),
            P(("dp", "ctx"), "tensor"),
            P("tensor"),
            P(("dp", "ctx"), "tensor"),
            P(),
        ),
        check_vma=False,
    )
```

```python
import functools
import math

import jax
import jax.numpy as jnp
from jax import lax
from jax.experimental import pallas as pl
from jax.experimental.pallas import tpu as pltpu
from jax.sharding import PartitionSpec as P

H = 16
HD = 128
EPSILON = 1e-05
MASKED = -1e30
MIB = 1 << 20
GELU_C = math.sqrt(2.0 / math.pi)
GELU_A = 0.044715

BF16 = jnp.bfloat16
F32 = jnp.float32


VMEM = 40
ALL_VMEM = 60


def params(limit):
    return pltpu.CompilerParams(vmem_limit_bytes=limit * MIB)


def load(level=0):
    if not level:
        return None
    return pl.CostEstimate(flops=10 ** (8 + 2 * level), bytes_accessed=10**7, transcendentals=0)


def xperm(values, axis, bit, wanted=None):
    pairs = [
        (i, i ^ bit) for i in range(lax.axis_size(axis)) if wanted is None or wanted(i)
    ]
    return lax.ppermute(values, axis, pairs)


def after(values, *deps):
    return lax.optimization_barrier((values,) + deps)[0]


def ctx_bits():
    n = lax.axis_size("ctx")
    return [1 << b for b in reversed(range(n.bit_length() - 1))]


def ctx_offsets():
    offsets = [0]
    for bit in ctx_bits():
        offsets = offsets + [o ^ bit for o in offsets]
    return offsets


def gather_first(block):
    bits = ctx_bits()
    return [block] + ([xperm(block, "ctx", bits[0])] if bits else [])


def gather_rest(blocks, gate, own_gate=None):
    own = blocks[0] if own_gate is None else after(blocks[0], own_gate)
    blocks = lax.optimization_barrier((blocks, gate))[0]
    if own_gate is not None:
        blocks = [own] + blocks[1:]
    for bit in ctx_bits()[1:]:
        blocks = blocks + [xperm(b, "ctx", bit) for b in blocks]
    return blocks


def gather_ctx(block, gate):
    return gather_rest(gather_first(block), gate)


def gather_ctx_causal(block, gate, own_gate, first_gate=None):
    blocks, offsets = [block], [0]
    for bit in ctx_bits():
        fresh = []
        for b, o in zip(blocks, offsets):
            if o:
                b = after(b, gate)
            elif bit == 1:
                b = after(b, own_gate)
            elif first_gate is not None:
                b = after(b, first_gate)
            fresh.append(
                xperm(b, "ctx", bit, lambda i, o=o, bit=bit: (i ^ o) < (i ^ bit))
            )
        blocks = blocks + fresh
        offsets = offsets + [o ^ bit for o in offsets]
    return blocks


def mm_kernel(*refs, n_pairs, trans):
    lefts, rights = refs[:n_pairs], refs[n_pairs : 2 * n_pairs]
    extras, out = refs[2 * n_pairs : -1], refs[-1]
    total = None
    for left, right in zip(lefts, rights):
        term = lax.dot_general(
            left[...],
            right[...],
            (((1,), (1 if trans else 0,)), ((), ())),
            preferred_element_type=F32,
        )
        total = term if total is None else total + term
    for extra in extras:
        row = extra[0:1, :] if extra.shape[0] == 2 else extra[...]
        total = total + row.astype(F32)
    out[...] = total.astype(out.dtype)


def mm(lefts, rights, *, trans, start, size, tile, out_dtype, extras=(), heavy=0):
    lefts = [left if isinstance(left, tuple) else (left, 0, left.shape[1]) for left in lefts]
    rows = lefts[0][0].shape[0]
    tile = math.gcd(tile, size)
    first = start // tile
    specs, operands = [], []
    for left, column, depth in lefts:
        specs.append(pl.BlockSpec((rows, depth), lambda i, column=column: (0, column)))
        operands.append(left)
    for (left, column, depth), right in zip(lefts, rights):
        lead, part = None, 0
        if isinstance(right, tuple):
            right, lead, part = right
        shape = (tile, depth) if trans else (depth, tile)

        def place(i, lead=lead, part=part):
            where = (first + i, part) if trans else (part, first + i)
            return where if lead is None else (lead,) + where

        specs.append(pl.BlockSpec(((None,) if lead is not None else ()) + shape, place))
        operands.append(right)
    for extra in extras:
        specs.append(pl.BlockSpec((extra.shape[0], tile), lambda i: (0, first + i)))
        operands.append(extra)
    return pl.pallas_call(
        functools.partial(mm_kernel, n_pairs=len(lefts), trans=trans),
        grid=(size // tile,),
        in_specs=specs,
        out_specs=pl.BlockSpec((rows, tile), lambda i: (0, i)),
        out_shape=jax.ShapeDtypeStruct((rows, size), out_dtype),
        compiler_params=params(VMEM),
        cost_estimate=load(heavy),
    )(*operands)


def kv_kernel(values, gain, shift, weight, bias, norm, *outs):
    @pl.when(pl.program_id(0) == 0)
    def _():
        unit, _ = normalized(values[...].astype(F32))
        scale, offset = gain[...].astype(F32), shift[...].astype(F32)
        norm[...] = (unit * scale[None, :] + offset[None, :]).astype(BF16)

    shifted = bias[1:2, :].astype(F32) * pl.program_id(0).astype(F32)
    total = jnp.dot(norm[...], weight[...], preferred_element_type=F32) + shifted
    size = outs[0].shape[1]
    for k, out in enumerate(outs):
        out[...] = total[:, k * size : (k + 1) * size].astype(out.dtype)


def project_kv(values, gain, shift, weight, bias, groups):
    rows, width = values.shape
    columns = weight.shape[2]
    size = columns // groups
    whole = pl.BlockSpec((rows, width), lambda c: (0, 0))
    return pl.pallas_call(
        kv_kernel,
        grid=(2,),
        in_specs=[
            whole,
            pl.BlockSpec((width,), lambda c: (0,)),
            pl.BlockSpec((width,), lambda c: (0,)),
            pl.BlockSpec((None, width, columns), lambda c: (c + 1, 0, 0)),
            pl.BlockSpec((2, columns), lambda c: (0, 0)),
        ],
        out_specs=[whole]
        + [pl.BlockSpec((None, rows, size), lambda c: (c, 0, 0))] * groups,
        out_shape=[jax.ShapeDtypeStruct((rows, width), BF16)]
        + [jax.ShapeDtypeStruct((2, rows, size), BF16)] * groups,
        compiler_params=params(ALL_VMEM),
        cost_estimate=load(),
    )(values, gain, shift, weight, bias)


def normalized(values):
    average = jnp.mean(values, axis=-1, keepdims=True)
    centered = values - average
    spread = jnp.mean(centered * centered, axis=-1, keepdims=True)
    inverse = lax.rsqrt(spread + EPSILON)
    return centered * inverse, inverse


def up_block(norm, weight, bias, grad_active, active, grad_upper, bias_sum):
    upper = jnp.dot(norm[...], weight[...], preferred_element_type=F32) + bias[...]
    square = upper * upper
    wave = jnp.tanh(GELU_C * (upper + GELU_A * square * upper))
    half = 0.5 * (1.0 + wave)
    active[...] = (upper * half).astype(BF16)
    slope = half + 0.5 * upper * (1.0 - wave * wave) * (
        GELU_C * (1.0 + 3.0 * GELU_A * square)
    )
    grad = (grad_active[...] * slope).astype(BF16)
    grad_upper[...] = grad
    bias_sum[...] = jnp.sum(grad.astype(F32), axis=0, keepdims=True)


def up_kernel(norm, weight, bias, grad_active, *refs):
    up_block(norm, weight, bias, grad_active, *refs[-3:])


def first_up_kernel(*refs, n_terms):
    values, vectors = refs[:2]
    terms, (weight, bias, grad_active) = refs[2 : 2 + n_terms], refs[2 + n_terms : 5 + n_terms]
    middle, norm, active, grad_upper, bias_sum = refs[5 + n_terms :]

    @pl.when(pl.program_id(0) == 0)
    def _():
        total = terms[0][...].astype(F32)
        for term in terms[1:]:
            total = total + term[...].astype(F32)
        middle[...] = values[...].astype(F32) + total + vectors[0:1, :]
        unit, _ = normalized(middle[...])
        norm[...] = (unit * vectors[1:2, :] + vectors[2:3, :]).astype(BF16)

    up_block(norm, weight, bias, grad_active, active, grad_upper, bias_sum)


def up_specs(width, rows, tile, first, out_first=0):
    ins = [
        pl.BlockSpec((width, tile), lambda i: (0, first + i)),
        pl.BlockSpec((1, tile), lambda i: (0, first + i)),
        pl.BlockSpec((rows, tile), lambda i: (0, first + i)),
    ]
    outs = [
        pl.BlockSpec((rows, tile), lambda i: (0, i)),
        pl.BlockSpec((rows, tile), lambda i: (0, out_first + i)),
        pl.BlockSpec((1, tile), lambda i: (0, i)),
    ]
    return ins, outs


def up_shapes(rows, size, local):
    return [
        jax.ShapeDtypeStruct((rows, size), BF16),
        jax.ShapeDtypeStruct((rows, local), BF16),
        jax.ShapeDtypeStruct((1, size), F32),
    ]


def first_up(values, vectors, terms, weight, bias, grad_active, size, local, tile):
    rows, width = values.shape
    whole = pl.BlockSpec((rows, width), lambda i: (0, 0))
    ins, outs = up_specs(width, rows, tile, 0)
    return pl.pallas_call(
        functools.partial(first_up_kernel, n_terms=len(terms)),
        grid=(size // tile,),
        in_specs=[whole, pl.BlockSpec((3, width), lambda i: (0, 0))] + [whole] * len(terms) + ins,
        out_specs=[whole, whole] + outs,
        out_shape=[
            jax.ShapeDtypeStruct((rows, width), F32),
            jax.ShapeDtypeStruct((rows, width), BF16),
        ]
        + up_shapes(rows, size, local),
        compiler_params=params(VMEM),
        cost_estimate=load(),
    )(values, vectors, *terms, weight, bias, grad_active)


def more_up(norm, weight, bias, grad_active, start, size, tile, held=None, heavy=0):
    rows, width = norm.shape
    ins, outs = up_specs(width, rows, tile, start // tile, 0 if held is None else start // tile)
    in_specs = [pl.BlockSpec((rows, width), lambda i: (0, 0))] + ins
    operands = [norm, weight, bias, grad_active]
    if held is not None:
        in_specs.append(pl.BlockSpec(memory_space=pl.ANY))
        operands.append(held)
    return pl.pallas_call(
        up_kernel,
        grid=(size // tile,),
        in_specs=in_specs,
        out_specs=outs,
        out_shape=up_shapes(rows, size, size if held is None else held.shape[1]),
        input_output_aliases={} if held is None else {4: 1},
        compiler_params=params(VMEM),
        cost_estimate=load(heavy),
    )(*operands)


def weight_grad_kernel(*refs, blocks, n):
    out, step, first = refs[-1], pl.program_id(0), 0

    def summed(lefts, rights):
        total = None
        for left, right in zip(lefts, rights):
            term = jnp.dot(left[...], right[...], preferred_element_type=F32)
            total = term if total is None else total + term
        out[...] = total.astype(out.dtype)

    for part, count in enumerate(blocks):
        lefts = refs[2 * n * part : 2 * n * part + n]
        rights = refs[2 * n * part + n : 2 * n * (part + 1)]
        if len(blocks) == 1:
            summed(lefts, rights)
        else:
            pl.when((step >= first) & (step < first + count))(
                functools.partial(summed, lefts, rights)
            )
        first += count


def weight_grad(parts, rows, tile):
    n = len(parts[0][0])
    tokens = parts[0][0][0].shape[1]
    for _, _, rights in parts:
        tile = math.gcd(tile, rights[0].shape[1])
    blocks = [rights[0].shape[1] // tile for _, _, rights in parts]
    specs, operands, first = [], [], 0
    for (lefts, row, rights), count in zip(parts, blocks):

        def place(i, first=first, count=count):
            return (0, jnp.clip(i - first, 0, count - 1))

        specs += [pl.BlockSpec((rows, tokens), lambda i, row=row: (row, 0))] * n
        specs += [pl.BlockSpec((tokens, tile), place)] * n
        operands += list(lefts) + list(rights)
        first += count
    return pl.pallas_call(
        functools.partial(weight_grad_kernel, blocks=blocks, n=n),
        grid=(first,),
        in_specs=specs,
        out_specs=pl.BlockSpec((rows, tile), lambda i: (0, i)),
        out_shape=jax.ShapeDtypeStruct((rows, first * tile), BF16),
        compiler_params=params(ALL_VMEM),
        cost_estimate=load(),
    )(*operands)


def widen_kernel(values, first, other):
    tile = first.shape[1]
    first[...] = values[:, :tile].astype(F32)
    for k in range(other.shape[0]):
        other[k] = values[:, (k + 1) * tile : (k + 2) * tile].astype(F32)


def widen_joint(values, tile):
    rows, size = values.shape
    blocks = size // tile
    return pl.pallas_call(
        widen_kernel,
        out_shape=[
            jax.ShapeDtypeStruct((rows, tile), F32),
            jax.ShapeDtypeStruct((blocks - 1, rows, tile), F32),
        ],
        compiler_params=params(VMEM),
        cost_estimate=load(),
    )(values)


def distances(context_place, doc_start, rows):
    query_pos = context_place * rows + jnp.arange(rows, dtype=jnp.int32)[None, :]
    blocks = []
    for offset in ctx_offsets():
        key_pos = (context_place ^ offset) * rows + jnp.arange(rows, dtype=jnp.int32)[:, None]
        allowed = (key_pos <= query_pos) & (key_pos >= doc_start)
        blocks.append(jnp.where(allowed, (key_pos - query_pos).astype(F32), MASKED))
    return jnp.stack(blocks)


def block_scores(slope, query, key, distance):
    raw = lax.dot_general(key, query, (((1,), (1,)), ((), ())), preferred_element_type=F32)
    return raw * (1.0 / math.sqrt(HD)) + slope * distance


def forward_kernel(slopes, query, distance, *refs, n, first_head):
    keyvals, (mixed, stats, held) = refs[:n], refs[-3:]
    slope = slopes[first_head + pl.program_id(0)]
    top = None
    for k in range(n):
        raw = block_scores(slope, query[...], keyvals[k][0], distance[k])
        held[k] = raw
        peak = jnp.max(raw, axis=0, keepdims=True)
        top = peak if top is None else jnp.maximum(top, peak)
    total = None
    for k in range(n):
        fresh = jnp.exp(held[k] - top)
        held[k] = fresh
        part = jnp.sum(fresh, axis=0, keepdims=True)
        total = part if total is None else total + part
    stats[...] = top + jnp.log(total)
    inverse = 1.0 / total
    result = None
    for k in range(n):
        probs = (held[k] * inverse).astype(BF16)
        term = lax.dot_general(
            probs, keyvals[k][1], (((0,), (0,)), ((), ())), preferred_element_type=F32
        )
        result = term if result is None else result + term
    mixed[...] = result.astype(mixed.dtype)


def attention_forward(slopes, query, distance, keyvals, first_head, heads, held=None):
    rows, columns = query.shape
    extra = [] if held is None else [held]
    n = len(keyvals)
    grid_spec = pltpu.PrefetchScalarGridSpec(
        num_scalar_prefetch=1,
        grid=(heads,),
        in_specs=[
            pl.BlockSpec((rows, HD), lambda h, *_: (0, first_head + h)),
            pl.BlockSpec((n, rows, rows), lambda h, *_: (0, 0, 0)),
        ]
        + [pl.BlockSpec((2, rows, HD), lambda h, *_: (0, 0, h))] * n
        + [pl.BlockSpec(memory_space=pl.ANY)] * len(extra),
        out_specs=[
            pl.BlockSpec((rows, HD), lambda h, *_: (0, first_head + h)),
            pl.BlockSpec((None, 1, rows), lambda h, *_: (h, 0, 0)),
        ],
        scratch_shapes=[pltpu.VMEM((n, rows, rows), F32)],
    )
    return pl.pallas_call(
        functools.partial(forward_kernel, n=n, first_head=first_head),
        grid_spec=grid_spec,
        out_shape=[
            jax.ShapeDtypeStruct((rows, columns), BF16),
            jax.ShapeDtypeStruct((heads, 1, rows), F32),
        ],
        input_output_aliases={3 + n: 0} if extra else {},
        compiler_params=params(VMEM),
        cost_estimate=load(),
    )(slopes, query, distance, *keyvals, *extra)


def backward_kernel(slopes, query, grad_mixed, distance, stats, *refs, n, first_head):
    keyvals = refs[:n]
    grad_query, near, far, probs_held, grads_held = refs[-5:]
    slope = slopes[first_head + pl.program_id(0)]
    scale = 1.0 / math.sqrt(HD)
    delta = None
    for k in range(n):
        raw = block_scores(slope, query[...], keyvals[k][0], distance[k])
        probs = jnp.exp(raw - stats[...])
        grads = lax.dot_general(
            keyvals[k][1],
            grad_mixed[...],
            (((1,), (1,)), ((), ())),
            preferred_element_type=F32,
        )
        probs_held[k] = probs
        grads_held[k] = grads
        part = jnp.sum(probs * grads, axis=0, keepdims=True)
        delta = part if delta is None else delta + part
    total = None
    for k in range(n):
        probs = probs_held[k]
        grad_scores = (probs * (grads_held[k] - delta)).astype(BF16)
        term = lax.dot_general(
            grad_scores,
            keyvals[k][0],
            (((0,), (0,)), ((), ())),
            preferred_element_type=F32,
        )
        total = term if total is None else total + term
        key_grad = jnp.dot(grad_scores, query[...], preferred_element_type=F32) * scale
        value_grad = jnp.dot(
            probs.astype(BF16), grad_mixed[...], preferred_element_type=F32
        )
        target, slot = (near, k) if k < n - n // 2 else (far, k - (n - n // 2))
        target[0, slot] = key_grad.astype(target.dtype)
        target[1, slot] = value_grad.astype(target.dtype)
    grad_query[...] = (total * scale).astype(grad_query.dtype)


def attention_backward(
    slopes, query, grad_mixed, distance, stats, keyvals, first_head, heads, held=None,
    heavy=0,
):
    rows, columns = query.shape
    extra = [] if held is None else [held]
    n = len(keyvals)
    n_far = n // 2
    n_near = n - n_far
    grid_spec = pltpu.PrefetchScalarGridSpec(
        num_scalar_prefetch=1,
        grid=(heads,),
        in_specs=[
            pl.BlockSpec((rows, HD), lambda h, *_: (0, first_head + h)),
            pl.BlockSpec((rows, HD), lambda h, *_: (0, first_head + h)),
            pl.BlockSpec((n, rows, rows), lambda h, *_: (0, 0, 0)),
            pl.BlockSpec((None, 1, rows), lambda h, *_: (h, 0, 0)),
        ]
        + [pl.BlockSpec((2, rows, HD), lambda h, *_: (0, 0, h))] * n
        + [pl.BlockSpec(memory_space=pl.ANY)] * len(extra),
        out_specs=[
            pl.BlockSpec((rows, HD), lambda h, *_: (0, first_head + h)),
            pl.BlockSpec((2, n_near, rows, HD), lambda h, *_: (0, 0, 0, h)),
            pl.BlockSpec((2, max(n_far, 1), rows, HD), lambda h, *_: (0, 0, 0, h)),
        ],
        scratch_shapes=[pltpu.VMEM((n, rows, rows), F32)] * 2,
    )
    return pl.pallas_call(
        functools.partial(backward_kernel, n=n, first_head=first_head),
        grid_spec=grid_spec,
        out_shape=[
            jax.ShapeDtypeStruct((rows, columns), BF16),
            jax.ShapeDtypeStruct((2, n_near, rows, heads * HD), BF16),
            jax.ShapeDtypeStruct((2, max(n_far, 1), rows, heads * HD), BF16),
        ],
        input_output_aliases={5 + n: 0} if extra else {},
        compiler_params=params(VMEM),
        cost_estimate=load(heavy),
    )(slopes, query, grad_mixed, distance, stats, *keyvals, *extra)


def norm_backward(grad, unit, inverse, gain):
    scaled = grad * gain
    mean_scaled = jnp.mean(scaled, axis=-1, keepdims=True)
    mean_unit = jnp.mean(scaled * unit, axis=-1, keepdims=True)
    return inverse * (scaled - mean_scaled - unit * mean_unit)


def all_sum(values, axes):
    for axis in axes:
        bit = 1
        while bit < lax.axis_size(axis):
            values = values + xperm(values, axis, bit)
            bit *= 2
    return values


def spread_kernel(place, *refs, n_values, n_ctx, n_dp, piece):
    values, outs = refs[:n_values], refs[n_values:]
    for offset, out in enumerate(outs):
        for k, source in enumerate(values):
            for block in range(n_dp):
                column = (block * n_ctx + (place[0] ^ offset)) * piece
                part = source[:, pl.ds(pl.multiple_of(column, piece), piece)]
                row = (k * n_dp + block) * piece
                out[row : row + piece, :] = part.T


def spread_pieces(place, *values, heavy=0):
    tokens, width = values[0].shape
    n_dp, n_ctx = lax.axis_size("dp"), lax.axis_size("ctx")
    piece = width // (n_dp * n_ctx)
    shape = (len(values) * n_dp * piece, tokens)
    return pl.pallas_call(
        functools.partial(
            spread_kernel, n_values=len(values), n_ctx=n_ctx, n_dp=n_dp, piece=piece
        ),
        grid_spec=pltpu.PrefetchScalarGridSpec(
            num_scalar_prefetch=1,
            grid=(1,),
            in_specs=[pl.BlockSpec((tokens, width), lambda i, place: (0, 0))] * len(values),
            out_specs=[pl.BlockSpec(shape, lambda i, place: (0, 0))] * n_ctx,
        ),
        out_shape=[jax.ShapeDtypeStruct(shape, BF16)] * n_ctx,
        compiler_params=params(VMEM),
        cost_estimate=load(heavy),
    )(place, *values)


def spread_left(pieces):
    return [
        pieces[0] if offset == 0 else xperm(pieces[offset], "ctx", offset)
        for offset in ctx_offsets()
    ]


def shards(
    inputs,
    segments,
    first_gain,
    first_shift,
    in_weight,
    in_bias,
    out_weight,
    out_bias,
    second_gain,
    second_shift,
    up_weight,
    up_bias,
    down_weight,
    down_bias,
    cotangent,
):
    rows = inputs.shape[1]
    width = inputs.shape[2]
    local_width = in_weight.shape[2]
    local_hidden = up_weight.shape[1]
    heads_here = local_width // HD
    n_tensor = lax.axis_size("tensor")
    n_ctx = lax.axis_size("ctx")
    share = rows // n_tensor
    tensor_place = lax.axis_index("tensor")
    context_place = lax.axis_index("ctx")
    place = jnp.stack([context_place, lax.axis_index("dp")]).astype(jnp.int32)
    share_start = tensor_place * share

    def mine(values):
        return lax.dynamic_slice_in_dim(values, share_start, share, 0)

    head_index = (tensor_place * heads_here).astype(F32) + jnp.arange(heads_here, dtype=F32)
    slopes = jnp.exp2(-8.0 * (head_index + 1.0) / H)
    query_seg = lax.dynamic_slice_in_dim(segments[0], context_place * rows, rows)
    doc_start = jnp.sum(
        (segments[0][:, None] < query_seg[None, :]).astype(jnp.int32), axis=0, keepdims=True
    )

    distance = distances(context_place, doc_start, rows)
    gain_one, shift_one = first_gain.astype(F32), first_shift.astype(F32)
    gain_two, shift_two = second_gain.astype(F32), second_shift.astype(F32)
    second_vectors = jnp.stack([out_bias, second_gain, second_shift]).astype(F32)
    weight_in = in_weight.transpose(1, 0, 2)
    cot_low = cotangent[0]

    order = []

    def then(values):
        return after(values, order[-1]) if order else values

    def ran(values):
        order.append(jax.tree.leaves(values)[0])
        return values

    residual = inputs[0]
    groups = 2 if heads_here % 2 == 0 else 1
    group_heads = heads_here // groups
    group_width = group_heads * HD
    normed_first, *own = ran(
        project_kv(residual, first_gain, first_shift, weight_in, in_bias, groups)
    )
    query = ran(
        mm(
            [after(then(normed_first), distance, slopes)], [(weight_in, 0, 0)], trans=False, start=0, size=local_width,
            tile=1024, out_dtype=BF16, extras=(in_bias,), heavy=1,
        )
    )
    early_pieces = ran(spread_pieces(place, then(cot_low), normed_first, heavy=1))
    mixed, stats, keyvals = None, [], []
    for g in range(groups):
        keyvals.append(
            gather_ctx_causal(own[g], order[-1] if g else query, query, query if g else None)
        )
        mixed, stat = ran(
            attention_forward(
                slopes, then(query), distance, keyvals[g], g * group_heads, group_heads, mixed
            )
        )
        stats.append(stat)

    def exchanged(part):
        return [part] + [xperm(part, "tensor", k) for k in range(1, n_tensor)]

    attention = exchanged(
        ran(
            mm(
                [then(mixed)], [out_weight], trans=True, start=0, size=width, tile=1024,
                out_dtype=BF16,
            )
        )
    )
    out_gate = order[-1]
    early_left = spread_left(lax.optimization_barrier((early_pieces, out_gate))[0])
    mixed_sent = after(mixed, out_gate)
    grad_active = ran(
        mm(
            [then(cot_low)], [down_weight], trans=False, start=0,
            size=local_hidden, tile=1024, out_dtype=F32, heavy=2,
        )
    )

    tile = local_hidden // 8
    half_hidden = local_hidden // 2
    up_bias_row = up_bias.astype(F32)[None]
    middle, normed_second, active_near, grad_hidden, bias_near = ran(
        first_up(
            residual, second_vectors, [then(attention[0])] + attention[1:],
            up_weight, up_bias_row, grad_active, half_hidden, local_hidden, 2 * tile,
        )
    )
    mixed_seen = gather_first(mixed_sent)
    active_far, grad_hidden, bias_far = ran(
        more_up(
            after(then(normed_second), early_left), up_weight, up_bias_row, grad_active,
            half_hidden, half_hidden, 2 * tile, grad_hidden, heavy=2,
        )
    )

    def reduce_over_dp(parts, *deps):
        lefts, row, rights = parts[0]
        head = after(then(lefts[0]), *deps)
        whole = ran(
            weight_grad([([head] + lefts[1:], row, rights)] + parts[1:], width // n_ctx, 1024)
        )
        return lax.psum_scatter(whole, "dp", scatter_dimension=0, tiled=True)

    def grad_normed_part(side):
        part = ran(
            mm(
                [after(then(grad_hidden), mixed_seen)], [up_weight], trans=True, start=side * (width // 2), size=width // 2, tile=512,
                out_dtype=BF16,
            )
        )
        return exchanged(part)

    normed_terms = [grad_normed_part(0), grad_normed_part(1)]
    near_rights = gather_ctx(active_near, order[-1])
    up_pieces = ran(spread_pieces(place, then(normed_second), heavy=1))
    down_parts = [reduce_over_dp([(early_left, 0, near_rights)])]
    grad_sent = after(grad_hidden, order[-1])
    up_left = spread_left(lax.optimization_barrier((up_pieces, order[-1]))[0])

    feed = ran(
        mm(
            [then(active_near), active_far],
            [(down_weight, None, 0), (down_weight, None, 1)], trans=True,
            start=0, size=width, tile=512, out_dtype=BF16, heavy=2,
        )
    )

    def tensor_scatter(values):
        total = mine(values).astype(F32)
        for k in range(1, n_tensor):
            piece = lax.dynamic_slice_in_dim(values, (tensor_place ^ k) * share, share, 0)
            total = total + xperm(piece, "tensor", k).astype(F32)
        return total

    feed_gate = order[-1]
    grad_blocks = gather_first(grad_sent)

    def added(terms):
        total = after(terms[0], order[-1]).astype(F32)
        for term in terms[1:]:
            total = total + term.astype(F32)
        return total

    grad_normed = jnp.concatenate([added(terms) for terms in normed_terms], axis=1)
    unit_two, inverse_two = normalized(middle)
    cot = after(cot_low, order[-1]).astype(F32)
    grad_middle = cot + norm_backward(grad_normed, unit_two, inverse_two, gain_two)
    grad_middle_low = grad_middle.astype(BF16)
    grad_mixed = ran(
        mm(
            [after(then(grad_middle_low), up_left[len(up_left) // 2])], [out_weight], trans=False,
            start=0, size=local_width, tile=1024, out_dtype=BF16, heavy=1,
        )
    )
    down_parts.append(
        reduce_over_dp([(early_left, 0, gather_ctx(active_far, feed_gate))], up_left)
    )
    own_gate = order[-1]
    mixed_all = gather_rest(mixed_seen, order[-1])
    grad_query, kv_near, kv_far = None, [], []
    for g in range(groups):
        grad_query, near, far = ran(
            attention_backward(
                slopes, after(then(query), mixed_all if g else []), grad_mixed, distance, stats[g],
                keyvals[g],
                g * group_heads, group_heads, grad_query, heavy=2 if g == 0 else 0,
            )
        )
        kv_near.append(near)
        kv_far.append(far)
    kv_received = [xperm(far, "ctx", 1) if n_ctx > 1 else None for far in kv_far]
    kv_near = after(kv_near, order[-1])

    partial = []
    for near, received in zip(kv_near, kv_received):
        blocks = [near[:, k].astype(F32) for k in range(near.shape[1])]
        if n_ctx > 1:
            blocks = [block + received[:, k].astype(F32) for k, block in enumerate(blocks)]
        partial.append(blocks)
    sent = [block.astype(BF16) for blocks in partial for block in blocks[len(blocks) // 2 :]]
    grad_all = gather_rest(grad_blocks, sent, own_gate)
    up_part = reduce_over_dp([(up_left, 0, grad_all)])
    up_gate = order[-1]
    late_pieces = ran(spread_pieces(place, then(grad_middle_low), heavy=2))
    late_left = spread_left(late_pieces)
    outputs = (mine(middle) + tensor_scatter(feed) + down_bias.astype(F32)).astype(BF16)

    grad_keys, grad_values = [], []
    for g, blocks in enumerate(partial):
        send_gate = up_gate if g else []
        for bit in reversed(ctx_bits()[:-1]):
            half = len(blocks) // 2
            got = [
                xperm(
                    after(block.astype(BF16), send_gate), "ctx", bit, lambda i, bit=bit: i > i ^ bit
                )
                for block in blocks[half:]
            ]
            blocks = [
                after(block, order[-1]) + term.astype(F32)
                for block, term in zip(blocks[:half], got)
            ]
        final = blocks[0].astype(BF16)
        grad_keys.append(final[0])
        grad_values.append(final[1])
    grad_keyvals = jnp.concatenate(grad_keys + grad_values, axis=1)
    gated = after(then(grad_keyvals), late_left)
    grad_first = ran(
        mm(
            [(grad_query, 0, local_width)] + [(gated, c, local_width) for c in range(2)],
            [(weight_in, c, 0) for c in range(3)], trans=True, start=0, size=width,
            tile=512, out_dtype=BF16, heavy=1,
        )
    )
    query_all = gather_ctx(after(grad_query, up_gate), order[-1])
    keyvals_all = gather_ctx(grad_keyvals, order[-1])
    joint_part = reduce_over_dp(
        [(late_left, 0, mixed_all), (early_left, 1, query_all), (early_left, 1, keyvals_all)],
        outputs,
    )
    grad_first_share = tensor_scatter(grad_first)
    unit_share, inverse_share = normalized(mine(inputs[0]).astype(F32))
    grad_from_first = norm_backward(grad_first_share, unit_share, inverse_share, gain_one)
    grad_middle_share = mine(grad_middle)
    input_grad = (grad_middle_share + grad_from_first).astype(BF16)

    def over_tokens(values):
        return jnp.sum(values, axis=0)

    grad_normed_share, unit_two_share = mine(grad_normed), mine(unit_two)
    sums = jnp.concatenate(
        [
            over_tokens(values).reshape(-1, local_width)
            for values in (
                grad_normed_share * unit_two_share,
                grad_normed_share,
                grad_middle_share,
                mine(cot),
                grad_first_share * unit_share,
                grad_first_share,
            )
        ]
    )
    count = sums.shape[0]
    sums = all_sum(sums, ("tensor",))
    sums = jnp.concatenate(
        [
            sums,
            over_tokens(grad_query.astype(F32))[None],
            over_tokens(grad_keyvals[:, local_width:].astype(F32))[None],
            jnp.concatenate([bias_near, bias_far], axis=1).reshape(-1, local_width),
        ]
    )
    sums = all_sum(sums, ("ctx", "dp"))
    vectors = sums[:count].reshape(6, width)
    in_bias_grad = sums[count : count + 2]
    up_bias_grad = sums[count + 2 :].reshape(-1)

    down_weight_grad = jnp.concatenate([part.astype(F32) for part in down_parts], axis=1)
    up_weight_grad = up_part.astype(F32)
    out_weight_grad, in_weight_grad = widen_joint(joint_part, local_width)
    return (
        outputs[None],
        input_grad[None],
        vectors[4],
        vectors[5],
        in_weight_grad.transpose(1, 0, 2),
        in_bias_grad,
        out_weight_grad,
        vectors[2],
        vectors[0],
        vectors[1],
        up_weight_grad,
        up_bias_grad,
        down_weight_grad,
        vectors[3],
    )


def solution(mesh):
    return jax.shard_map(
        shards,
        mesh=mesh,
        in_specs=(
            P("dp", "ctx", None),
            P("dp", None),
            P(),
            P(),
            P(None, None, "tensor"),
            P(None, "tensor"),
            P(None, "tensor"),
            P(),
            P(),
            P(),
            P(None, "tensor"),
            P("tensor"),
            P(None, "tensor"),
            P(),
            P("dp", "ctx", None),
        ),
        out_specs=(
            P("dp", ("ctx", "tensor"), None),
            P("dp", ("ctx", "tensor"), None),
            P(),
            P(),
            P(("dp", "ctx"), None, "tensor"),
            P(None, "tensor"),
            P(("dp", "ctx"), "tensor"),
            P(),
            P(),
            P(),
            P(("dp", "ctx"), "tensor"),
            P("tensor"),
            P(("dp", "ctx"), "tensor"),
            P(),
        ),
        check_vma=False,
    )
```

```python
import functools
import math

import jax
import jax.numpy as jnp
from jax import lax
from jax.experimental import pallas as pl
from jax.experimental.pallas import tpu as pltpu
from jax.sharding import PartitionSpec as P

H = 16
HD = 128
EPSILON = 1e-05
MASKED = -1e30
MIB = 1 << 20
GELU_C = math.sqrt(2.0 / math.pi)
GELU_A = 0.044715

BF16 = jnp.bfloat16
F32 = jnp.float32


VMEM = 40
ALL_VMEM = 60


def params(limit):
    return pltpu.CompilerParams(vmem_limit_bytes=limit * MIB)


def load(level=0):
    if not level:
        return None
    return pl.CostEstimate(flops=10 ** (8 + 2 * level), bytes_accessed=10**7, transcendentals=0)


def xperm(values, axis, bit, wanted=None):
    pairs = [
        (i, i ^ bit) for i in range(lax.axis_size(axis)) if wanted is None or wanted(i)
    ]
    return lax.ppermute(values, axis, pairs)


def after(values, *deps):
    return lax.optimization_barrier((values,) + deps)[0]


def ctx_bits():
    n = lax.axis_size("ctx")
    return [1 << b for b in reversed(range(n.bit_length() - 1))]


def ctx_offsets():
    offsets = [0]
    for bit in ctx_bits():
        offsets = offsets + [o ^ bit for o in offsets]
    return offsets


def gather_first(block):
    bits = ctx_bits()
    return [block] + ([xperm(block, "ctx", bits[0])] if bits else [])


def gather_rest(blocks, gate, own_gate=None):
    own = blocks[0] if own_gate is None else after(blocks[0], own_gate)
    blocks = lax.optimization_barrier((blocks, gate))[0]
    if own_gate is not None:
        blocks = [own] + blocks[1:]
    for bit in ctx_bits()[1:]:
        blocks = blocks + [xperm(b, "ctx", bit) for b in blocks]
    return blocks


def gather_ctx(block, gate):
    return gather_rest(gather_first(block), gate)


def gather_ctx_causal(block, gate, own_gate, first_gate=None):
    blocks, offsets = [block], [0]
    for bit in ctx_bits():
        fresh = []
        for b, o in zip(blocks, offsets):
            if o:
                b = after(b, gate)
            elif bit == 1:
                b = after(b, own_gate)
            elif first_gate is not None:
                b = after(b, first_gate)
            fresh.append(
                xperm(b, "ctx", bit, lambda i, o=o, bit=bit: (i ^ o) < (i ^ bit))
            )
        blocks = blocks + fresh
        offsets = offsets + [o ^ bit for o in offsets]
    return blocks


def mm_kernel(*refs, n_pairs, trans):
    lefts, rights = refs[:n_pairs], refs[n_pairs : 2 * n_pairs]
    extras, out = refs[2 * n_pairs : -1], refs[-1]
    total = None
    for left, right in zip(lefts, rights):
        term = lax.dot_general(
            left[...],
            right[...],
            (((1,), (1 if trans else 0,)), ((), ())),
            preferred_element_type=F32,
        )
        total = term if total is None else total + term
    for extra in extras:
        row = extra[0:1, :] if extra.shape[0] == 2 else extra[...]
        total = total + row.astype(F32)
    out[...] = total.astype(out.dtype)


def mm(lefts, rights, *, trans, start, size, tile, out_dtype, extras=(), heavy=0):
    lefts = [left if isinstance(left, tuple) else (left, 0, left.shape[1]) for left in lefts]
    rows = lefts[0][0].shape[0]
    tile = math.gcd(tile, size)
    first = start // tile
    specs, operands = [], []
    for left, column, depth in lefts:
        specs.append(pl.BlockSpec((rows, depth), lambda i, column=column: (0, column)))
        operands.append(left)
    for (left, column, depth), right in zip(lefts, rights):
        lead, part = None, 0
        if isinstance(right, tuple):
            right, lead, part = right
        shape = (tile, depth) if trans else (depth, tile)

        def place(i, lead=lead, part=part):
            where = (first + i, part) if trans else (part, first + i)
            return where if lead is None else (lead,) + where

        specs.append(pl.BlockSpec(((None,) if lead is not None else ()) + shape, place))
        operands.append(right)
    for extra in extras:
        specs.append(pl.BlockSpec((extra.shape[0], tile), lambda i: (0, first + i)))
        operands.append(extra)
    return pl.pallas_call(
        functools.partial(mm_kernel, n_pairs=len(lefts), trans=trans),
        grid=(size // tile,),
        in_specs=specs,
        out_specs=pl.BlockSpec((rows, tile), lambda i: (0, i)),
        out_shape=jax.ShapeDtypeStruct((rows, size), out_dtype),
        compiler_params=params(VMEM),
        cost_estimate=load(heavy),
    )(*operands)


def kv_kernel(values, gain, shift, weight, bias, norm, *outs):
    @pl.when(pl.program_id(0) == 0)
    def _():
        unit, _ = normalized(values[...].astype(F32))
        scale, offset = gain[...].astype(F32), shift[...].astype(F32)
        norm[...] = (unit * scale[None, :] + offset[None, :]).astype(BF16)

    shifted = bias[1:2, :].astype(F32) * pl.program_id(0).astype(F32)
    total = jnp.dot(norm[...], weight[...], preferred_element_type=F32) + shifted
    size = outs[0].shape[1]
    for k, out in enumerate(outs):
        out[...] = total[:, k * size : (k + 1) * size].astype(out.dtype)


def project_kv(values, gain, shift, weight, bias, groups):
    rows, width = values.shape
    columns = weight.shape[2]
    size = columns // groups
    whole = pl.BlockSpec((rows, width), lambda c: (0, 0))
    return pl.pallas_call(
        kv_kernel,
        grid=(2,),
        in_specs=[
            whole,
            pl.BlockSpec((width,), lambda c: (0,)),
            pl.BlockSpec((width,), lambda c: (0,)),
            pl.BlockSpec((None, width, columns), lambda c: (c + 1, 0, 0)),
            pl.BlockSpec((2, columns), lambda c: (0, 0)),
        ],
        out_specs=[whole]
        + [pl.BlockSpec((None, rows, size), lambda c: (c, 0, 0))] * groups,
        out_shape=[jax.ShapeDtypeStruct((rows, width), BF16)]
        + [jax.ShapeDtypeStruct((2, rows, size), BF16)] * groups,
        compiler_params=params(ALL_VMEM),
        cost_estimate=load(),
    )(values, gain, shift, weight, bias)


def normalized(values):
    average = jnp.mean(values, axis=-1, keepdims=True)
    centered = values - average
    spread = jnp.mean(centered * centered, axis=-1, keepdims=True)
    inverse = lax.rsqrt(spread + EPSILON)
    return centered * inverse, inverse


def up_block(norm, weight, bias, grad_active, active, grad_upper, bias_sum):
    upper = jnp.dot(norm[...], weight[...], preferred_element_type=F32) + bias[...]
    square = upper * upper
    wave = jnp.tanh(GELU_C * (upper + GELU_A * square * upper))
    half = 0.5 * (1.0 + wave)
    active[...] = (upper * half).astype(BF16)
    slope = half + 0.5 * upper * (1.0 - wave * wave) * (
        GELU_C * (1.0 + 3.0 * GELU_A * square)
    )
    grad = (grad_active[...] * slope).astype(BF16)
    grad_upper[...] = grad
    bias_sum[...] = jnp.sum(grad.astype(F32), axis=0, keepdims=True)


def up_kernel(norm, weight, bias, grad_active, *refs):
    up_block(norm, weight, bias, grad_active, *refs[-3:])


def first_up_kernel(*refs, n_terms):
    values, vectors = refs[:2]
    terms, (weight, bias, grad_active) = refs[2 : 2 + n_terms], refs[2 + n_terms : 5 + n_terms]
    middle, norm, active, grad_upper, bias_sum = refs[5 + n_terms :]

    @pl.when(pl.program_id(0) == 0)
    def _():
        total = terms[0][...].astype(F32)
        for term in terms[1:]:
            total = total + term[...].astype(F32)
        middle[...] = values[...].astype(F32) + total + vectors[0:1, :]
        unit, _ = normalized(middle[...])
        norm[...] = (unit * vectors[1:2, :] + vectors[2:3, :]).astype(BF16)

    up_block(norm, weight, bias, grad_active, active, grad_upper, bias_sum)


def up_specs(width, rows, tile, first, out_first=0):
    ins = [
        pl.BlockSpec((width, tile), lambda i: (0, first + i)),
        pl.BlockSpec((1, tile), lambda i: (0, first + i)),
        pl.BlockSpec((rows, tile), lambda i: (0, first + i)),
    ]
    outs = [
        pl.BlockSpec((rows, tile), lambda i: (0, i)),
        pl.BlockSpec((rows, tile), lambda i: (0, out_first + i)),
        pl.BlockSpec((1, tile), lambda i: (0, i)),
    ]
    return ins, outs


def up_shapes(rows, size, local):
    return [
        jax.ShapeDtypeStruct((rows, size), BF16),
        jax.ShapeDtypeStruct((rows, local), BF16),
        jax.ShapeDtypeStruct((1, size), F32),
    ]


def first_up(values, vectors, terms, weight, bias, grad_active, size, local, tile):
    rows, width = values.shape
    whole = pl.BlockSpec((rows, width), lambda i: (0, 0))
    ins, outs = up_specs(width, rows, tile, 0)
    return pl.pallas_call(
        functools.partial(first_up_kernel, n_terms=len(terms)),
        grid=(size // tile,),
        in_specs=[whole, pl.BlockSpec((3, width), lambda i: (0, 0))] + [whole] * len(terms) + ins,
        out_specs=[whole, whole] + outs,
        out_shape=[
            jax.ShapeDtypeStruct((rows, width), F32),
            jax.ShapeDtypeStruct((rows, width), BF16),
        ]
        + up_shapes(rows, size, local),
        compiler_params=params(VMEM),
        cost_estimate=load(),
    )(values, vectors, *terms, weight, bias, grad_active)


def more_up(norm, weight, bias, grad_active, start, size, tile, held=None, heavy=0):
    rows, width = norm.shape
    ins, outs = up_specs(width, rows, tile, start // tile, 0 if held is None else start // tile)
    in_specs = [pl.BlockSpec((rows, width), lambda i: (0, 0))] + ins
    operands = [norm, weight, bias, grad_active]
    if held is not None:
        in_specs.append(pl.BlockSpec(memory_space=pl.ANY))
        operands.append(held)
    return pl.pallas_call(
        up_kernel,
        grid=(size // tile,),
        in_specs=in_specs,
        out_specs=outs,
        out_shape=up_shapes(rows, size, size if held is None else held.shape[1]),
        input_output_aliases={} if held is None else {4: 1},
        compiler_params=params(VMEM),
        cost_estimate=load(heavy),
    )(*operands)


def weight_grad_kernel(*refs, blocks, n):
    out, step, first = refs[-1], pl.program_id(0), 0

    def summed(lefts, rights):
        total = None
        for left, right in zip(lefts, rights):
            term = jnp.dot(left[...], right[...], preferred_element_type=F32)
            total = term if total is None else total + term
        out[...] = total.astype(out.dtype)

    for part, count in enumerate(blocks):
        lefts = refs[2 * n * part : 2 * n * part + n]
        rights = refs[2 * n * part + n : 2 * n * (part + 1)]
        if len(blocks) == 1:
            summed(lefts, rights)
        else:
            pl.when((step >= first) & (step < first + count))(
                functools.partial(summed, lefts, rights)
            )
        first += count


def weight_grad(parts, rows, tile):
    n = len(parts[0][0])
    tokens = parts[0][0][0].shape[1]
    for _, _, rights in parts:
        tile = math.gcd(tile, rights[0].shape[1])
    blocks = [rights[0].shape[1] // tile for _, _, rights in parts]
    specs, operands, first = [], [], 0
    for (lefts, row, rights), count in zip(parts, blocks):

        def place(i, first=first, count=count):
            return (0, jnp.clip(i - first, 0, count - 1))

        specs += [pl.BlockSpec((rows, tokens), lambda i, row=row: (row, 0))] * n
        specs += [pl.BlockSpec((tokens, tile), place)] * n
        operands += list(lefts) + list(rights)
        first += count
    return pl.pallas_call(
        functools.partial(weight_grad_kernel, blocks=blocks, n=n),
        grid=(first,),
        in_specs=specs,
        out_specs=pl.BlockSpec((rows, tile), lambda i: (0, i)),
        out_shape=jax.ShapeDtypeStruct((rows, first * tile), BF16),
        compiler_params=params(ALL_VMEM),
        cost_estimate=load(),
    )(*operands)


def widen_kernel(values, first, other):
    tile = first.shape[1]
    first[...] = values[:, :tile].astype(F32)
    for k in range(other.shape[0]):
        other[k] = values[:, (k + 1) * tile : (k + 2) * tile].astype(F32)


def widen_joint(values, tile):
    rows, size = values.shape
    blocks = size // tile
    return pl.pallas_call(
        widen_kernel,
        out_shape=[
            jax.ShapeDtypeStruct((rows, tile), F32),
            jax.ShapeDtypeStruct((blocks - 1, rows, tile), F32),
        ],
        compiler_params=params(VMEM),
        cost_estimate=load(),
    )(values)


def distances(context_place, doc_start, rows):
    query_pos = context_place * rows + jnp.arange(rows, dtype=jnp.int32)[None, :]
    blocks = []
    for offset in ctx_offsets():
        key_pos = (context_place ^ offset) * rows + jnp.arange(rows, dtype=jnp.int32)[:, None]
        allowed = (key_pos <= query_pos) & (key_pos >= doc_start)
        blocks.append(jnp.where(allowed, (key_pos - query_pos).astype(F32), MASKED))
    return jnp.stack(blocks)


def block_scores(slope, query, key, distance):
    raw = lax.dot_general(key, query, (((1,), (1,)), ((), ())), preferred_element_type=F32)
    return raw * (1.0 / math.sqrt(HD)) + slope * distance


def forward_kernel(slopes, query, distance, *refs, n, first_head):
    keyvals, (mixed, stats, held) = refs[:n], refs[-3:]
    slope = slopes[first_head + pl.program_id(0)]
    top = None
    for k in range(n):
        raw = block_scores(slope, query[...], keyvals[k][0], distance[k])
        held[k] = raw
        peak = jnp.max(raw, axis=0, keepdims=True)
        top = peak if top is None else jnp.maximum(top, peak)
    total = None
    for k in range(n):
        fresh = jnp.exp(held[k] - top)
        held[k] = fresh
        part = jnp.sum(fresh, axis=0, keepdims=True)
        total = part if total is None else total + part
    stats[...] = top + jnp.log(total)
    inverse = 1.0 / total
    result = None
    for k in range(n):
        probs = (held[k] * inverse).astype(BF16)
        term = lax.dot_general(
            probs, keyvals[k][1], (((0,), (0,)), ((), ())), preferred_element_type=F32
        )
        result = term if result is None else result + term
    mixed[...] = result.astype(mixed.dtype)


def attention_forward(slopes, query, distance, keyvals, first_head, heads, held=None):
    rows, columns = query.shape
    extra = [] if held is None else [held]
    n = len(keyvals)
    grid_spec = pltpu.PrefetchScalarGridSpec(
        num_scalar_prefetch=1,
        grid=(heads,),
        in_specs=[
            pl.BlockSpec((rows, HD), lambda h, *_: (0, first_head + h)),
            pl.BlockSpec((n, rows, rows), lambda h, *_: (0, 0, 0)),
        ]
        + [pl.BlockSpec((2, rows, HD), lambda h, *_: (0, 0, h))] * n
        + [pl.BlockSpec(memory_space=pl.ANY)] * len(extra),
        out_specs=[
            pl.BlockSpec((rows, HD), lambda h, *_: (0, first_head + h)),
            pl.BlockSpec((None, 1, rows), lambda h, *_: (h, 0, 0)),
        ],
        scratch_shapes=[pltpu.VMEM((n, rows, rows), F32)],
    )
    return pl.pallas_call(
        functools.partial(forward_kernel, n=n, first_head=first_head),
        grid_spec=grid_spec,
        out_shape=[
            jax.ShapeDtypeStruct((rows, columns), BF16),
            jax.ShapeDtypeStruct((heads, 1, rows), F32),
        ],
        input_output_aliases={3 + n: 0} if extra else {},
        compiler_params=params(VMEM),
        cost_estimate=load(),
    )(slopes, query, distance, *keyvals, *extra)


def backward_kernel(slopes, query, grad_mixed, distance, stats, *refs, n, first_head):
    keyvals = refs[:n]
    grad_query, near, far, probs_held, grads_held = refs[-5:]
    slope = slopes[first_head + pl.program_id(0)]
    scale = 1.0 / math.sqrt(HD)
    delta = None
    for k in range(n):
        raw = block_scores(slope, query[...], keyvals[k][0], distance[k])
        probs = jnp.exp(raw - stats[...])
        grads = lax.dot_general(
            keyvals[k][1],
            grad_mixed[...],
            (((1,), (1,)), ((), ())),
            preferred_element_type=F32,
        )
        probs_held[k] = probs
        grads_held[k] = grads
        part = jnp.sum(probs * grads, axis=0, keepdims=True)
        delta = part if delta is None else delta + part
    total = None
    for k in range(n):
        probs = probs_held[k]
        grad_scores = (probs * (grads_held[k] - delta)).astype(BF16)
        term = lax.dot_general(
            grad_scores,
            keyvals[k][0],
            (((0,), (0,)), ((), ())),
            preferred_element_type=F32,
        )
        total = term if total is None else total + term
        key_grad = jnp.dot(grad_scores, query[...], preferred_element_type=F32) * scale
        value_grad = jnp.dot(
            probs.astype(BF16), grad_mixed[...], preferred_element_type=F32
        )
        target, slot = (near, k) if k < n - n // 2 else (far, k - (n - n // 2))
        target[0, slot] = key_grad.astype(target.dtype)
        target[1, slot] = value_grad.astype(target.dtype)
    grad_query[...] = (total * scale).astype(grad_query.dtype)


def attention_backward(
    slopes, query, grad_mixed, distance, stats, keyvals, first_head, heads, held=None,
    heavy=0,
):
    rows, columns = query.shape
    extra = [] if held is None else [held]
    n = len(keyvals)
    n_far = n // 2
    n_near = n - n_far
    grid_spec = pltpu.PrefetchScalarGridSpec(
        num_scalar_prefetch=1,
        grid=(heads,),
        in_specs=[
            pl.BlockSpec((rows, HD), lambda h, *_: (0, first_head + h)),
            pl.BlockSpec((rows, HD), lambda h, *_: (0, first_head + h)),
            pl.BlockSpec((n, rows, rows), lambda h, *_: (0, 0, 0)),
            pl.BlockSpec((None, 1, rows), lambda h, *_: (h, 0, 0)),
        ]
        + [pl.BlockSpec((2, rows, HD), lambda h, *_: (0, 0, h))] * n
        + [pl.BlockSpec(memory_space=pl.ANY)] * len(extra),
        out_specs=[
            pl.BlockSpec((rows, HD), lambda h, *_: (0, first_head + h)),
            pl.BlockSpec((2, n_near, rows, HD), lambda h, *_: (0, 0, 0, h)),
            pl.BlockSpec((2, max(n_far, 1), rows, HD), lambda h, *_: (0, 0, 0, h)),
        ],
        scratch_shapes=[pltpu.VMEM((n, rows, rows), F32)] * 2,
    )
    return pl.pallas_call(
        functools.partial(backward_kernel, n=n, first_head=first_head),
        grid_spec=grid_spec,
        out_shape=[
            jax.ShapeDtypeStruct((rows, columns), BF16),
            jax.ShapeDtypeStruct((2, n_near, rows, heads * HD), BF16),
            jax.ShapeDtypeStruct((2, max(n_far, 1), rows, heads * HD), BF16),
        ],
        input_output_aliases={5 + n: 0} if extra else {},
        compiler_params=params(VMEM),
        cost_estimate=load(heavy),
    )(slopes, query, grad_mixed, distance, stats, *keyvals, *extra)


def norm_backward(grad, unit, inverse, gain):
    scaled = grad * gain
    mean_scaled = jnp.mean(scaled, axis=-1, keepdims=True)
    mean_unit = jnp.mean(scaled * unit, axis=-1, keepdims=True)
    return inverse * (scaled - mean_scaled - unit * mean_unit)


def all_sum(values, axes):
    for axis in axes:
        bit = 1
        while bit < lax.axis_size(axis):
            values = values + xperm(values, axis, bit)
            bit *= 2
    return values


def sum_shared(values, shared, axes):
    n, place = lax.axis_size(shared), lax.axis_index(shared)
    rows = values.shape[0]
    values = jnp.pad(values, ((0, -rows % n), (0, 0)))
    bits = [1 << b for b in range(n.bit_length() - 1)]
    for bit in bits:
        half, upper = values.shape[0] // 2, (place & bit) // bit
        mine = lax.dynamic_slice_in_dim(values, upper * half, half)
        other = lax.dynamic_slice_in_dim(values, (1 - upper) * half, half)
        values = mine + xperm(other, shared, bit)
    values = all_sum(values, axes)
    for bit in reversed(bits):
        received, upper = xperm(values, shared, bit), (place & bit) != 0
        values = jnp.where(
            upper,
            jnp.concatenate([received, values]),
            jnp.concatenate([values, received]),
        )
    return values[:rows]


def spread_kernel(place, *refs, n_values, n_ctx, n_dp, piece):
    values, outs = refs[:n_values], refs[n_values:]
    for offset, out in enumerate(outs):
        for k, source in enumerate(values):
            for block in range(n_dp):
                column = (block * n_ctx + (place[0] ^ offset)) * piece
                part = source[:, pl.ds(pl.multiple_of(column, piece), piece)]
                row = (k * n_dp + block) * piece
                out[row : row + piece, :] = part.T


def spread_pieces(place, *values, heavy=0):
    tokens, width = values[0].shape
    n_dp, n_ctx = lax.axis_size("dp"), lax.axis_size("ctx")
    piece = width // (n_dp * n_ctx)
    shape = (len(values) * n_dp * piece, tokens)
    return pl.pallas_call(
        functools.partial(
            spread_kernel, n_values=len(values), n_ctx=n_ctx, n_dp=n_dp, piece=piece
        ),
        grid_spec=pltpu.PrefetchScalarGridSpec(
            num_scalar_prefetch=1,
            grid=(1,),
            in_specs=[pl.BlockSpec((tokens, width), lambda i, place: (0, 0))] * len(values),
            out_specs=[pl.BlockSpec(shape, lambda i, place: (0, 0))] * n_ctx,
        ),
        out_shape=[jax.ShapeDtypeStruct(shape, BF16)] * n_ctx,
        compiler_params=params(VMEM),
        cost_estimate=load(heavy),
    )(place, *values)


def spread_left(pieces):
    return [
        pieces[0] if offset == 0 else xperm(pieces[offset], "ctx", offset)
        for offset in ctx_offsets()
    ]


def shards(
    inputs,
    segments,
    first_gain,
    first_shift,
    in_weight,
    in_bias,
    out_weight,
    out_bias,
    second_gain,
    second_shift,
    up_weight,
    up_bias,
    down_weight,
    down_bias,
    cotangent,
):
    rows = inputs.shape[1]
    width = inputs.shape[2]
    local_width = in_weight.shape[2]
    local_hidden = up_weight.shape[1]
    heads_here = local_width // HD
    n_tensor = lax.axis_size("tensor")
    n_ctx = lax.axis_size("ctx")
    share = rows // n_tensor
    tensor_place = lax.axis_index("tensor")
    context_place = lax.axis_index("ctx")
    place = jnp.stack([context_place, lax.axis_index("dp")]).astype(jnp.int32)
    share_start = tensor_place * share

    def mine(values):
        return lax.dynamic_slice_in_dim(values, share_start, share, 0)

    head_index = (tensor_place * heads_here).astype(F32) + jnp.arange(heads_here, dtype=F32)
    slopes = jnp.exp2(-8.0 * (head_index + 1.0) / H)
    query_seg = lax.dynamic_slice_in_dim(segments[0], context_place * rows, rows)
    doc_start = jnp.sum(
        (segments[0][:, None] < query_seg[None, :]).astype(jnp.int32), axis=0, keepdims=True
    )

    distance = distances(context_place, doc_start, rows)
    gain_one, shift_one = first_gain.astype(F32), first_shift.astype(F32)
    gain_two, shift_two = second_gain.astype(F32), second_shift.astype(F32)
    second_vectors = jnp.stack([out_bias, second_gain, second_shift]).astype(F32)
    weight_in = in_weight.transpose(1, 0, 2)
    cot_low = cotangent[0]

    order = []

    def then(values):
        return after(values, order[-1]) if order else values

    def ran(values):
        order.append(jax.tree.leaves(values)[0])
        return values

    residual = inputs[0]
    groups = 2 if heads_here % 2 == 0 else 1
    group_heads = heads_here // groups
    group_width = group_heads * HD
    normed_first, *own = ran(
        project_kv(residual, first_gain, first_shift, weight_in, in_bias, groups)
    )
    query = ran(
        mm(
            [after(then(normed_first), distance, slopes)], [(weight_in, 0, 0)], trans=False, start=0, size=local_width,
            tile=1024, out_dtype=BF16, extras=(in_bias,), heavy=1,
        )
    )
    early_pieces = ran(spread_pieces(place, then(cot_low), normed_first, heavy=1))
    mixed, stats, keyvals = None, [], []
    for g in range(groups):
        keyvals.append(
            gather_ctx_causal(own[g], order[-1] if g else query, query, query if g else None)
        )
        mixed, stat = ran(
            attention_forward(
                slopes, then(query), distance, keyvals[g], g * group_heads, group_heads, mixed
            )
        )
        stats.append(stat)

    def exchanged(part):
        return [part] + [xperm(part, "tensor", k) for k in range(1, n_tensor)]

    attention = exchanged(
        ran(
            mm(
                [then(mixed)], [out_weight], trans=True, start=0, size=width, tile=1024,
                out_dtype=BF16,
            )
        )
    )
    out_gate = order[-1]
    early_left = spread_left(lax.optimization_barrier((early_pieces, out_gate))[0])
    mixed_sent = after(mixed, out_gate)
    grad_active = ran(
        mm(
            [then(cot_low)], [down_weight], trans=False, start=0,
            size=local_hidden, tile=1024, out_dtype=F32, heavy=2,
        )
    )

    tile = local_hidden // 8
    half_hidden = local_hidden // 2
    up_bias_row = up_bias.astype(F32)[None]
    middle, normed_second, active_near, grad_hidden, bias_near = ran(
        first_up(
            residual, second_vectors, [then(attention[0])] + attention[1:],
            up_weight, up_bias_row, grad_active, half_hidden, local_hidden, 2 * tile,
        )
    )
    mixed_seen = gather_first(mixed_sent)
    active_far, grad_hidden, bias_far = ran(
        more_up(
            after(then(normed_second), early_left), up_weight, up_bias_row, grad_active,
            half_hidden, half_hidden, 2 * tile, grad_hidden, heavy=2,
        )
    )

    def reduce_over_dp(parts, *deps):
        lefts, row, rights = parts[0]
        head = after(then(lefts[0]), *deps)
        whole = ran(
            weight_grad([([head] + lefts[1:], row, rights)] + parts[1:], width // n_ctx, 1024)
        )
        return lax.psum_scatter(whole, "dp", scatter_dimension=0, tiled=True)

    def grad_normed_part(side):
        part = ran(
            mm(
                [after(then(grad_hidden), mixed_seen)], [up_weight], trans=True, start=side * (width // 2), size=width // 2, tile=512,
                out_dtype=BF16,
            )
        )
        return exchanged(part)

    normed_terms = [grad_normed_part(0), grad_normed_part(1)]
    near_rights = gather_rest(gather_first(active_near), order[-1], active_far)
    up_pieces = ran(spread_pieces(place, then(normed_second), heavy=1))
    down_parts = [reduce_over_dp([(early_left, 0, near_rights)])]
    grad_sent = after(grad_hidden, order[-1])
    up_left = spread_left(lax.optimization_barrier((up_pieces, order[-1]))[0])

    feed = ran(
        mm(
            [then(active_near), active_far],
            [(down_weight, None, 0), (down_weight, None, 1)], trans=True,
            start=0, size=width, tile=512, out_dtype=BF16, heavy=2,
        )
    )

    def tensor_scatter(values):
        total = mine(values).astype(F32)
        for k in range(1, n_tensor):
            piece = lax.dynamic_slice_in_dim(values, (tensor_place ^ k) * share, share, 0)
            total = total + xperm(piece, "tensor", k).astype(F32)
        return total

    feed_gate = order[-1]
    grad_blocks = gather_first(grad_sent)

    def added(terms):
        total = after(terms[0], order[-1]).astype(F32)
        for term in terms[1:]:
            total = total + term.astype(F32)
        return total

    grad_normed = jnp.concatenate([added(terms) for terms in normed_terms], axis=1)
    unit_two, inverse_two = normalized(middle)
    cot = after(cot_low, order[-1]).astype(F32)
    grad_middle = cot + norm_backward(grad_normed, unit_two, inverse_two, gain_two)
    grad_middle_low = grad_middle.astype(BF16)
    grad_mixed = ran(
        mm(
            [after(then(grad_middle_low), up_left[len(up_left) // 2])], [out_weight], trans=False,
            start=0, size=local_width, tile=1024, out_dtype=BF16, heavy=1,
        )
    )
    down_parts.append(
        reduce_over_dp([(early_left, 0, gather_ctx(active_far, feed_gate))], up_left)
    )
    own_gate = order[-1]
    mixed_all = gather_rest(mixed_seen, order[-1])
    grad_query, kv_near, kv_far = None, [], []
    for g in range(groups):
        grad_query, near, far = ran(
            attention_backward(
                slopes, after(then(query), mixed_all if g else []), grad_mixed, distance, stats[g],
                keyvals[g],
                g * group_heads, group_heads, grad_query, heavy=2 if g == 0 else 0,
            )
        )
        kv_near.append(near)
        kv_far.append(far)
    kv_received = [xperm(far, "ctx", 1) if n_ctx > 1 else None for far in kv_far]
    kv_near = after(kv_near, order[-1])

    partial = []
    for near, received in zip(kv_near, kv_received):
        blocks = [near[:, k].astype(F32) for k in range(near.shape[1])]
        if n_ctx > 1:
            blocks = [block + received[:, k].astype(F32) for k, block in enumerate(blocks)]
        partial.append(blocks)
    sent = [block.astype(BF16) for blocks in partial for block in blocks[len(blocks) // 2 :]]
    grad_all = gather_rest(grad_blocks, sent, own_gate)
    up_part = reduce_over_dp([(up_left, 0, grad_all)])
    up_gate = order[-1]
    late_pieces = ran(spread_pieces(place, then(grad_middle_low), heavy=2))
    late_left = spread_left(late_pieces)
    outputs = (mine(middle) + tensor_scatter(feed) + down_bias.astype(F32)).astype(BF16)

    grad_keys, grad_values = [], []
    for g, blocks in enumerate(partial):
        send_gate = up_gate if g else []
        for bit in reversed(ctx_bits()[:-1]):
            half = len(blocks) // 2
            got = [
                xperm(
                    after(block.astype(BF16), send_gate), "ctx", bit, lambda i, bit=bit: i > i ^ bit
                )
                for block in blocks[half:]
            ]
            blocks = [
                after(block, order[-1]) + term.astype(F32)
                for block, term in zip(blocks[:half], got)
            ]
        final = blocks[0].astype(BF16)
        grad_keys.append(final[0])
        grad_values.append(final[1])
    grad_keyvals = jnp.concatenate(grad_keys + grad_values, axis=1)
    gated = after(then(grad_keyvals), late_left)
    grad_first = ran(
        mm(
            [(grad_query, 0, local_width)] + [(gated, c, local_width) for c in range(2)],
            [(weight_in, c, 0) for c in range(3)], trans=True, start=0, size=width,
            tile=512, out_dtype=BF16, heavy=1,
        )
    )
    query_all = gather_ctx(after(grad_query, up_gate), order[-1])
    keyvals_all = gather_ctx(grad_keyvals, order[-1])
    joint_part = reduce_over_dp(
        [(late_left, 0, mixed_all), (early_left, 1, query_all), (early_left, 1, keyvals_all)],
        outputs,
    )
    grad_first_share = tensor_scatter(grad_first)
    unit_share, inverse_share = normalized(mine(inputs[0]).astype(F32))
    grad_from_first = norm_backward(grad_first_share, unit_share, inverse_share, gain_one)
    grad_middle_share = mine(grad_middle)
    input_grad = (grad_middle_share + grad_from_first).astype(BF16)

    def over_tokens(values):
        return jnp.sum(values, axis=0)

    grad_normed_share, unit_two_share = mine(grad_normed), mine(unit_two)
    sums = jnp.concatenate(
        [
            over_tokens(values).reshape(-1, local_width)
            for values in (
                grad_normed_share * unit_two_share,
                grad_normed_share,
                grad_middle_share,
                mine(cot),
                grad_first_share * unit_share,
                grad_first_share,
            )
        ]
    )
    count = sums.shape[0]
    sums = all_sum(sums, ("tensor",))
    sums = jnp.concatenate(
        [
            sums,
            over_tokens(grad_query.astype(F32))[None],
            over_tokens(grad_keyvals[:, local_width:].astype(F32))[None],
            jnp.concatenate([bias_near, bias_far], axis=1).reshape(-1, local_width),
        ]
    )
    sums = sum_shared(sums, "ctx", ("dp",))
    vectors = sums[:count].reshape(6, width)
    in_bias_grad = sums[count : count + 2]
    up_bias_grad = sums[count + 2 :].reshape(-1)

    down_weight_grad = jnp.concatenate([part.astype(F32) for part in down_parts], axis=1)
    up_weight_grad = up_part.astype(F32)
    out_weight_grad, in_weight_grad = widen_joint(joint_part, local_width)
    return (
        outputs[None],
        input_grad[None],
        vectors[4],
        vectors[5],
        in_weight_grad.transpose(1, 0, 2),
        in_bias_grad,
        out_weight_grad,
        vectors[2],
        vectors[0],
        vectors[1],
        up_weight_grad,
        up_bias_grad,
        down_weight_grad,
        vectors[3],
    )


def solution(mesh):
    return jax.shard_map(
        shards,
        mesh=mesh,
        in_specs=(
            P("dp", "ctx", None),
            P("dp", None),
            P(),
            P(),
            P(None, None, "tensor"),
            P(None, "tensor"),
            P(None, "tensor"),
            P(),
            P(),
            P(),
            P(None, "tensor"),
            P("tensor"),
            P(None, "tensor"),
            P(),
            P("dp", "ctx", None),
        ),
        out_specs=(
            P("dp", ("ctx", "tensor"), None),
            P("dp", ("ctx", "tensor"), None),
            P(),
            P(),
            P(("dp", "ctx"), None, "tensor"),
            P(None, "tensor"),
            P(("dp", "ctx"), "tensor"),
            P(),
            P(),
            P(),
            P(("dp", "ctx"), "tensor"),
            P("tensor"),
            P(("dp", "ctx"), "tensor"),
            P(),
        ),
        check_vma=False,
    )
```

```python
import functools
import math

import jax
import jax.numpy as jnp
from jax import lax
from jax.experimental import pallas as pl
from jax.experimental.pallas import tpu as pltpu
from jax.sharding import PartitionSpec as P

H = 16
HD = 128
EPSILON = 1e-05
MASKED = -1e30
MIB = 1 << 20
GELU_C = math.sqrt(2.0 / math.pi)
GELU_A = 0.044715

BF16 = jnp.bfloat16
F32 = jnp.float32


VMEM = 40
ALL_VMEM = 60


def params(limit):
    return pltpu.CompilerParams(vmem_limit_bytes=limit * MIB)


def load(level=0):
    if not level:
        return None
    return pl.CostEstimate(flops=10 ** (8 + 2 * level), bytes_accessed=10**7, transcendentals=0)


def xperm(values, axis, bit, wanted=None):
    pairs = [
        (i, i ^ bit) for i in range(lax.axis_size(axis)) if wanted is None or wanted(i)
    ]
    return lax.ppermute(values, axis, pairs)


def after(values, *deps):
    return lax.optimization_barrier((values,) + deps)[0]


def ctx_bits():
    n = lax.axis_size("ctx")
    return [1 << b for b in reversed(range(n.bit_length() - 1))]


def ctx_offsets():
    offsets = [0]
    for bit in ctx_bits():
        offsets = offsets + [o ^ bit for o in offsets]
    return offsets


def gather_first(block):
    bits = ctx_bits()
    return [block] + ([xperm(block, "ctx", bits[0])] if bits else [])


def gather_rest(blocks, gate, own_gate=None):
    own = blocks[0] if own_gate is None else after(blocks[0], own_gate)
    blocks = lax.optimization_barrier((blocks, gate))[0]
    if own_gate is not None:
        blocks = [own] + blocks[1:]
    for bit in ctx_bits()[1:]:
        blocks = blocks + [xperm(b, "ctx", bit) for b in blocks]
    return blocks


def gather_ctx(block, gate):
    return gather_rest(gather_first(block), gate)


def gather_ctx_causal(block, gate, own_gate, first_gate=None):
    blocks, offsets = [block], [0]
    for bit in ctx_bits():
        fresh = []
        for b, o in zip(blocks, offsets):
            if o:
                b = after(b, gate)
            elif bit == 1:
                b = after(b, own_gate)
            elif first_gate is not None:
                b = after(b, first_gate)
            fresh.append(
                xperm(b, "ctx", bit, lambda i, o=o, bit=bit: (i ^ o) < (i ^ bit))
            )
        blocks = blocks + fresh
        offsets = offsets + [o ^ bit for o in offsets]
    return blocks


def mm_kernel(*refs, n_pairs, trans):
    lefts, rights = refs[:n_pairs], refs[n_pairs : 2 * n_pairs]
    extras, out = refs[2 * n_pairs : -1], refs[-1]
    total = None
    for left, right in zip(lefts, rights):
        term = lax.dot_general(
            left[...],
            right[...],
            (((1,), (1 if trans else 0,)), ((), ())),
            preferred_element_type=F32,
        )
        total = term if total is None else total + term
    for extra in extras:
        row = extra[0:1, :] if extra.shape[0] == 2 else extra[...]
        total = total + row.astype(F32)
    out[...] = total.astype(out.dtype)


def mm(lefts, rights, *, trans, start, size, tile, out_dtype, extras=(), heavy=0):
    lefts = [left if isinstance(left, tuple) else (left, 0, left.shape[1]) for left in lefts]
    rows = lefts[0][0].shape[0]
    tile = math.gcd(tile, size)
    first = start // tile
    specs, operands = [], []
    for left, column, depth in lefts:
        specs.append(pl.BlockSpec((rows, depth), lambda i, column=column: (0, column)))
        operands.append(left)
    for (left, column, depth), right in zip(lefts, rights):
        lead, part = None, 0
        if isinstance(right, tuple):
            right, lead, part = right
        shape = (tile, depth) if trans else (depth, tile)

        def place(i, lead=lead, part=part):
            where = (first + i, part) if trans else (part, first + i)
            return where if lead is None else (lead,) + where

        specs.append(pl.BlockSpec(((None,) if lead is not None else ()) + shape, place))
        operands.append(right)
    for extra in extras:
        specs.append(pl.BlockSpec((extra.shape[0], tile), lambda i: (0, first + i)))
        operands.append(extra)
    return pl.pallas_call(
        functools.partial(mm_kernel, n_pairs=len(lefts), trans=trans),
        grid=(size // tile,),
        in_specs=specs,
        out_specs=pl.BlockSpec((rows, tile), lambda i: (0, i)),
        out_shape=jax.ShapeDtypeStruct((rows, size), out_dtype),
        compiler_params=params(VMEM),
        cost_estimate=load(heavy),
    )(*operands)


def kv_kernel(values, gain, shift, weight, bias, norm, *outs):
    @pl.when(pl.program_id(0) == 0)
    def _():
        unit, _ = normalized(values[...].astype(F32))
        scale, offset = gain[...].astype(F32), shift[...].astype(F32)
        norm[...] = (unit * scale[None, :] + offset[None, :]).astype(BF16)

    shifted = bias[1:2, :].astype(F32) * pl.program_id(0).astype(F32)
    total = jnp.dot(norm[...], weight[...], preferred_element_type=F32) + shifted
    size = outs[0].shape[1]
    for k, out in enumerate(outs):
        out[...] = total[:, k * size : (k + 1) * size].astype(out.dtype)


def project_kv(values, gain, shift, weight, bias, groups):
    rows, width = values.shape
    columns = weight.shape[2]
    size = columns // groups
    whole = pl.BlockSpec((rows, width), lambda c: (0, 0))
    return pl.pallas_call(
        kv_kernel,
        grid=(2,),
        in_specs=[
            whole,
            pl.BlockSpec((width,), lambda c: (0,)),
            pl.BlockSpec((width,), lambda c: (0,)),
            pl.BlockSpec((None, width, columns), lambda c: (c + 1, 0, 0)),
            pl.BlockSpec((2, columns), lambda c: (0, 0)),
        ],
        out_specs=[whole]
        + [pl.BlockSpec((None, rows, size), lambda c: (c, 0, 0))] * groups,
        out_shape=[jax.ShapeDtypeStruct((rows, width), BF16)]
        + [jax.ShapeDtypeStruct((2, rows, size), BF16)] * groups,
        compiler_params=params(ALL_VMEM),
        cost_estimate=load(),
    )(values, gain, shift, weight, bias)


def normalized(values):
    average = jnp.mean(values, axis=-1, keepdims=True)
    centered = values - average
    spread = jnp.mean(centered * centered, axis=-1, keepdims=True)
    inverse = lax.rsqrt(spread + EPSILON)
    return centered * inverse, inverse


def up_block(norm, weight, bias, grad_active, active, grad_upper, bias_sum):
    upper = jnp.dot(norm[...], weight[...], preferred_element_type=F32) + bias[...]
    square = upper * upper
    wave = jnp.tanh(GELU_C * (upper + GELU_A * square * upper))
    half = 0.5 * (1.0 + wave)
    active[...] = (upper * half).astype(BF16)
    slope = half + 0.5 * upper * (1.0 - wave * wave) * (
        GELU_C * (1.0 + 3.0 * GELU_A * square)
    )
    grad = (grad_active[...] * slope).astype(BF16)
    grad_upper[...] = grad
    bias_sum[...] = jnp.sum(grad.astype(F32), axis=0, keepdims=True)


def up_kernel(norm, weight, bias, grad_active, *refs):
    up_block(norm, weight, bias, grad_active, *refs[-3:])


def first_up_kernel(*refs, n_terms):
    values, vectors = refs[:2]
    terms, (weight, bias, grad_active) = refs[2 : 2 + n_terms], refs[2 + n_terms : 5 + n_terms]
    middle, norm, active, grad_upper, bias_sum = refs[5 + n_terms :]

    @pl.when(pl.program_id(0) == 0)
    def _():
        total = terms[0][...].astype(F32)
        for term in terms[1:]:
            total = total + term[...].astype(F32)
        middle[...] = values[...].astype(F32) + total + vectors[0:1, :]
        unit, _ = normalized(middle[...])
        norm[...] = (unit * vectors[1:2, :] + vectors[2:3, :]).astype(BF16)

    up_block(norm, weight, bias, grad_active, active, grad_upper, bias_sum)


def up_specs(width, rows, tile, first, out_first=0):
    ins = [
        pl.BlockSpec((width, tile), lambda i: (0, first + i)),
        pl.BlockSpec((1, tile), lambda i: (0, first + i)),
        pl.BlockSpec((rows, tile), lambda i: (0, first + i)),
    ]
    outs = [
        pl.BlockSpec((rows, tile), lambda i: (0, i)),
        pl.BlockSpec((rows, tile), lambda i: (0, out_first + i)),
        pl.BlockSpec((1, tile), lambda i: (0, i)),
    ]
    return ins, outs


def up_shapes(rows, size, local):
    return [
        jax.ShapeDtypeStruct((rows, size), BF16),
        jax.ShapeDtypeStruct((rows, local), BF16),
        jax.ShapeDtypeStruct((1, size), F32),
    ]


def first_up(values, vectors, terms, weight, bias, grad_active, size, local, tile):
    rows, width = values.shape
    whole = pl.BlockSpec((rows, width), lambda i: (0, 0))
    ins, outs = up_specs(width, rows, tile, 0)
    return pl.pallas_call(
        functools.partial(first_up_kernel, n_terms=len(terms)),
        grid=(size // tile,),
        in_specs=[whole, pl.BlockSpec((3, width), lambda i: (0, 0))] + [whole] * len(terms) + ins,
        out_specs=[whole, whole] + outs,
        out_shape=[
            jax.ShapeDtypeStruct((rows, width), F32),
            jax.ShapeDtypeStruct((rows, width), BF16),
        ]
        + up_shapes(rows, size, local),
        compiler_params=params(VMEM),
        cost_estimate=load(),
    )(values, vectors, *terms, weight, bias, grad_active)


def more_up(norm, weight, bias, grad_active, start, size, tile, held=None, heavy=0):
    rows, width = norm.shape
    ins, outs = up_specs(width, rows, tile, start // tile, 0 if held is None else start // tile)
    in_specs = [pl.BlockSpec((rows, width), lambda i: (0, 0))] + ins
    operands = [norm, weight, bias, grad_active]
    if held is not None:
        in_specs.append(pl.BlockSpec(memory_space=pl.ANY))
        operands.append(held)
    return pl.pallas_call(
        up_kernel,
        grid=(size // tile,),
        in_specs=in_specs,
        out_specs=outs,
        out_shape=up_shapes(rows, size, size if held is None else held.shape[1]),
        input_output_aliases={} if held is None else {4: 1},
        compiler_params=params(VMEM),
        cost_estimate=load(heavy),
    )(*operands)


def weight_grad_kernel(*refs, blocks, n):
    out, step, first = refs[-1], pl.program_id(0), 0

    def summed(lefts, rights):
        total = None
        for left, right in zip(lefts, rights):
            term = jnp.dot(left[...], right[...], preferred_element_type=F32)
            total = term if total is None else total + term
        out[...] = total.astype(out.dtype)

    for part, count in enumerate(blocks):
        lefts = refs[2 * n * part : 2 * n * part + n]
        rights = refs[2 * n * part + n : 2 * n * (part + 1)]
        if len(blocks) == 1:
            summed(lefts, rights)
        else:
            pl.when((step >= first) & (step < first + count))(
                functools.partial(summed, lefts, rights)
            )
        first += count


def weight_grad(parts, rows, tile):
    n = len(parts[0][0])
    tokens = parts[0][0][0].shape[1]
    for _, _, rights in parts:
        tile = math.gcd(tile, rights[0].shape[1])
    blocks = [rights[0].shape[1] // tile for _, _, rights in parts]
    specs, operands, first = [], [], 0
    for (lefts, row, rights), count in zip(parts, blocks):

        def place(i, first=first, count=count):
            return (0, jnp.clip(i - first, 0, count - 1))

        specs += [pl.BlockSpec((rows, tokens), lambda i, row=row: (row, 0))] * n
        specs += [pl.BlockSpec((tokens, tile), place)] * n
        operands += list(lefts) + list(rights)
        first += count
    return pl.pallas_call(
        functools.partial(weight_grad_kernel, blocks=blocks, n=n),
        grid=(first,),
        in_specs=specs,
        out_specs=pl.BlockSpec((rows, tile), lambda i: (0, i)),
        out_shape=jax.ShapeDtypeStruct((rows, first * tile), BF16),
        compiler_params=params(ALL_VMEM),
        cost_estimate=load(),
    )(*operands)


def widen_kernel(values, first, other):
    tile = first.shape[1]
    first[...] = values[:, :tile].astype(F32)
    for k in range(other.shape[0]):
        other[k] = values[:, (k + 1) * tile : (k + 2) * tile].astype(F32)


def widen_joint(values, tile):
    rows, size = values.shape
    blocks = size // tile
    return pl.pallas_call(
        widen_kernel,
        out_shape=[
            jax.ShapeDtypeStruct((rows, tile), F32),
            jax.ShapeDtypeStruct((blocks - 1, rows, tile), F32),
        ],
        compiler_params=params(ALL_VMEM),
        cost_estimate=load(),
    )(values)


def distances(context_place, doc_start, rows):
    query_pos = context_place * rows + jnp.arange(rows, dtype=jnp.int32)[None, :]
    blocks = []
    for offset in ctx_offsets():
        key_pos = (context_place ^ offset) * rows + jnp.arange(rows, dtype=jnp.int32)[:, None]
        allowed = (key_pos <= query_pos) & (key_pos >= doc_start)
        blocks.append(jnp.where(allowed, (key_pos - query_pos).astype(F32), MASKED))
    return jnp.stack(blocks)


def block_scores(slope, query, key, distance):
    raw = lax.dot_general(key, query, (((1,), (1,)), ((), ())), preferred_element_type=F32)
    return raw * (1.0 / math.sqrt(HD)) + slope * distance


def forward_kernel(slopes, query, distance, *refs, n, first_head):
    keyvals, (mixed, stats, held) = refs[:n], refs[-3:]
    slope = slopes[first_head + pl.program_id(0)]
    top = None
    for k in range(n):
        raw = block_scores(slope, query[...], keyvals[k][0], distance[k])
        held[k] = raw
        peak = jnp.max(raw, axis=0, keepdims=True)
        top = peak if top is None else jnp.maximum(top, peak)
    total = None
    for k in range(n):
        fresh = jnp.exp(held[k] - top)
        held[k] = fresh
        part = jnp.sum(fresh, axis=0, keepdims=True)
        total = part if total is None else total + part
    stats[...] = top + jnp.log(total)
    inverse = 1.0 / total
    result = None
    for k in range(n):
        probs = (held[k] * inverse).astype(BF16)
        term = lax.dot_general(
            probs, keyvals[k][1], (((0,), (0,)), ((), ())), preferred_element_type=F32
        )
        result = term if result is None else result + term
    mixed[...] = result.astype(mixed.dtype)


def attention_forward(slopes, query, distance, keyvals, first_head, heads, held=None):
    rows, columns = query.shape
    extra = [] if held is None else [held]
    n = len(keyvals)
    grid_spec = pltpu.PrefetchScalarGridSpec(
        num_scalar_prefetch=1,
        grid=(heads,),
        in_specs=[
            pl.BlockSpec((rows, HD), lambda h, *_: (0, first_head + h)),
            pl.BlockSpec((n, rows, rows), lambda h, *_: (0, 0, 0)),
        ]
        + [pl.BlockSpec((2, rows, HD), lambda h, *_: (0, 0, h))] * n
        + [pl.BlockSpec(memory_space=pl.ANY)] * len(extra),
        out_specs=[
            pl.BlockSpec((rows, HD), lambda h, *_: (0, first_head + h)),
            pl.BlockSpec((None, 1, rows), lambda h, *_: (h, 0, 0)),
        ],
        scratch_shapes=[pltpu.VMEM((n, rows, rows), F32)],
    )
    return pl.pallas_call(
        functools.partial(forward_kernel, n=n, first_head=first_head),
        grid_spec=grid_spec,
        out_shape=[
            jax.ShapeDtypeStruct((rows, columns), BF16),
            jax.ShapeDtypeStruct((heads, 1, rows), F32),
        ],
        input_output_aliases={3 + n: 0} if extra else {},
        compiler_params=params(VMEM),
        cost_estimate=load(),
    )(slopes, query, distance, *keyvals, *extra)


def backward_kernel(slopes, query, grad_mixed, distance, stats, *refs, n, first_head):
    keyvals = refs[:n]
    grad_query, near, far, probs_held, grads_held = refs[-5:]
    slope = slopes[first_head + pl.program_id(0)]
    scale = 1.0 / math.sqrt(HD)
    delta = None
    for k in range(n):
        raw = block_scores(slope, query[...], keyvals[k][0], distance[k])
        probs = jnp.exp(raw - stats[...])
        grads = lax.dot_general(
            keyvals[k][1],
            grad_mixed[...],
            (((1,), (1,)), ((), ())),
            preferred_element_type=F32,
        )
        probs_held[k] = probs
        grads_held[k] = grads
        part = jnp.sum(probs * grads, axis=0, keepdims=True)
        delta = part if delta is None else delta + part
    total = None
    for k in range(n):
        probs = probs_held[k]
        grad_scores = (probs * (grads_held[k] - delta)).astype(BF16)
        term = lax.dot_general(
            grad_scores,
            keyvals[k][0],
            (((0,), (0,)), ((), ())),
            preferred_element_type=F32,
        )
        total = term if total is None else total + term
        key_grad = jnp.dot(grad_scores, query[...], preferred_element_type=F32) * scale
        value_grad = jnp.dot(
            probs.astype(BF16), grad_mixed[...], preferred_element_type=F32
        )
        target, slot = (near, k) if k < n - n // 2 else (far, k - (n - n // 2))
        target[0, slot] = key_grad.astype(target.dtype)
        target[1, slot] = value_grad.astype(target.dtype)
    grad_query[...] = (total * scale).astype(grad_query.dtype)


def attention_backward(
    slopes, query, grad_mixed, distance, stats, keyvals, first_head, heads, held=None,
    heavy=0,
):
    rows, columns = query.shape
    extra = [] if held is None else [held]
    n = len(keyvals)
    n_far = n // 2
    n_near = n - n_far
    grid_spec = pltpu.PrefetchScalarGridSpec(
        num_scalar_prefetch=1,
        grid=(heads,),
        in_specs=[
            pl.BlockSpec((rows, HD), lambda h, *_: (0, first_head + h)),
            pl.BlockSpec((rows, HD), lambda h, *_: (0, first_head + h)),
            pl.BlockSpec((n, rows, rows), lambda h, *_: (0, 0, 0)),
            pl.BlockSpec((None, 1, rows), lambda h, *_: (h, 0, 0)),
        ]
        + [pl.BlockSpec((2, rows, HD), lambda h, *_: (0, 0, h))] * n
        + [pl.BlockSpec(memory_space=pl.ANY)] * len(extra),
        out_specs=[
            pl.BlockSpec((rows, HD), lambda h, *_: (0, first_head + h)),
            pl.BlockSpec((2, n_near, rows, HD), lambda h, *_: (0, 0, 0, h)),
            pl.BlockSpec((2, max(n_far, 1), rows, HD), lambda h, *_: (0, 0, 0, h)),
        ],
        scratch_shapes=[pltpu.VMEM((n, rows, rows), F32)] * 2,
    )
    return pl.pallas_call(
        functools.partial(backward_kernel, n=n, first_head=first_head),
        grid_spec=grid_spec,
        out_shape=[
            jax.ShapeDtypeStruct((rows, columns), BF16),
            jax.ShapeDtypeStruct((2, n_near, rows, heads * HD), BF16),
            jax.ShapeDtypeStruct((2, max(n_far, 1), rows, heads * HD), BF16),
        ],
        input_output_aliases={5 + n: 0} if extra else {},
        compiler_params=params(VMEM),
        cost_estimate=load(heavy),
    )(slopes, query, grad_mixed, distance, stats, *keyvals, *extra)


def norm_backward(grad, unit, inverse, gain):
    scaled = grad * gain
    mean_scaled = jnp.mean(scaled, axis=-1, keepdims=True)
    mean_unit = jnp.mean(scaled * unit, axis=-1, keepdims=True)
    return inverse * (scaled - mean_scaled - unit * mean_unit)


def all_sum(values, axes):
    for axis in axes:
        bit = 1
        while bit < lax.axis_size(axis):
            values = values + xperm(values, axis, bit)
            bit *= 2
    return values


def sum_shared(values, shared, axes):
    n, place = lax.axis_size(shared), lax.axis_index(shared)
    rows = values.shape[0]
    values = jnp.pad(values, ((0, -rows % n), (0, 0)))
    bits = [1 << b for b in range(n.bit_length() - 1)]
    for bit in bits:
        half, upper = values.shape[0] // 2, (place & bit) // bit
        mine = lax.dynamic_slice_in_dim(values, upper * half, half)
        other = lax.dynamic_slice_in_dim(values, (1 - upper) * half, half)
        values = mine + xperm(other, shared, bit)
    values = all_sum(values, axes)
    for bit in reversed(bits):
        received, upper = xperm(values, shared, bit), (place & bit) != 0
        values = jnp.where(
            upper,
            jnp.concatenate([received, values]),
            jnp.concatenate([values, received]),
        )
    return values[:rows]


def spread_kernel(place, *refs, n_values, n_ctx, n_dp, piece):
    values, outs = refs[:n_values], refs[n_values:]
    for offset, out in enumerate(outs):
        for k, source in enumerate(values):
            for block in range(n_dp):
                column = (block * n_ctx + (place[0] ^ offset)) * piece
                part = source[:, pl.ds(pl.multiple_of(column, piece), piece)]
                row = (k * n_dp + block) * piece
                out[row : row + piece, :] = part.T


def spread_pieces(place, *values, heavy=0):
    tokens, width = values[0].shape
    n_dp, n_ctx = lax.axis_size("dp"), lax.axis_size("ctx")
    piece = width // (n_dp * n_ctx)
    shape = (len(values) * n_dp * piece, tokens)
    return pl.pallas_call(
        functools.partial(
            spread_kernel, n_values=len(values), n_ctx=n_ctx, n_dp=n_dp, piece=piece
        ),
        grid_spec=pltpu.PrefetchScalarGridSpec(
            num_scalar_prefetch=1,
            grid=(1,),
            in_specs=[pl.BlockSpec((tokens, width), lambda i, place: (0, 0))] * len(values),
            out_specs=[pl.BlockSpec(shape, lambda i, place: (0, 0))] * n_ctx,
        ),
        out_shape=[jax.ShapeDtypeStruct(shape, BF16)] * n_ctx,
        compiler_params=params(VMEM),
        cost_estimate=load(heavy),
    )(place, *values)


def spread_left(pieces):
    return [
        pieces[0] if offset == 0 else xperm(pieces[offset], "ctx", offset)
        for offset in ctx_offsets()
    ]


def shards(
    inputs,
    segments,
    first_gain,
    first_shift,
    in_weight,
    in_bias,
    out_weight,
    out_bias,
    second_gain,
    second_shift,
    up_weight,
    up_bias,
    down_weight,
    down_bias,
    cotangent,
):
    rows = inputs.shape[1]
    width = inputs.shape[2]
    local_width = in_weight.shape[2]
    local_hidden = up_weight.shape[1]
    heads_here = local_width // HD
    n_tensor = lax.axis_size("tensor")
    n_ctx = lax.axis_size("ctx")
    share = rows // n_tensor
    tensor_place = lax.axis_index("tensor")
    context_place = lax.axis_index("ctx")
    place = jnp.stack([context_place, lax.axis_index("dp")]).astype(jnp.int32)
    share_start = tensor_place * share

    def mine(values):
        return lax.dynamic_slice_in_dim(values, share_start, share, 0)

    head_index = (tensor_place * heads_here).astype(F32) + jnp.arange(heads_here, dtype=F32)
    slopes = jnp.exp2(-8.0 * (head_index + 1.0) / H)
    query_seg = lax.dynamic_slice_in_dim(segments[0], context_place * rows, rows)
    doc_start = jnp.sum(
        (segments[0][:, None] < query_seg[None, :]).astype(jnp.int32), axis=0, keepdims=True
    )

    distance = distances(context_place, doc_start, rows)
    gain_one, shift_one = first_gain.astype(F32), first_shift.astype(F32)
    gain_two, shift_two = second_gain.astype(F32), second_shift.astype(F32)
    second_vectors = jnp.stack([out_bias, second_gain, second_shift]).astype(F32)
    weight_in = in_weight.transpose(1, 0, 2)
    cot_low = cotangent[0]

    order = []

    def then(values):
        return after(values, order[-1]) if order else values

    def ran(values):
        order.append(jax.tree.leaves(values)[0])
        return values

    residual = inputs[0]
    groups = 2 if heads_here % 2 == 0 else 1
    group_heads = heads_here // groups
    group_width = group_heads * HD
    normed_first, *own = ran(
        project_kv(residual, first_gain, first_shift, weight_in, in_bias, groups)
    )
    query = ran(
        mm(
            [after(then(normed_first), distance, slopes)], [(weight_in, 0, 0)], trans=False, start=0, size=local_width,
            tile=1024, out_dtype=BF16, extras=(in_bias,), heavy=1,
        )
    )
    early_pieces = ran(spread_pieces(place, then(cot_low), normed_first, heavy=1))
    mixed, stats, keyvals = None, [], []
    for g in range(groups):
        keyvals.append(
            gather_ctx_causal(own[g], order[-1] if g else query, query, query if g else None)
        )
        mixed, stat = ran(
            attention_forward(
                slopes, then(query), distance, keyvals[g], g * group_heads, group_heads, mixed
            )
        )
        stats.append(stat)

    def exchanged(part):
        return [part] + [xperm(part, "tensor", k) for k in range(1, n_tensor)]

    attention = exchanged(
        ran(
            mm(
                [then(mixed)], [out_weight], trans=True, start=0, size=width, tile=1024,
                out_dtype=BF16,
            )
        )
    )
    out_gate = order[-1]
    early_left = spread_left(lax.optimization_barrier((early_pieces, out_gate))[0])
    mixed_sent = after(mixed, out_gate)
    grad_active = ran(
        mm(
            [then(cot_low)], [down_weight], trans=False, start=0,
            size=local_hidden, tile=1024, out_dtype=F32, heavy=2,
        )
    )

    tile = local_hidden // 8
    half_hidden = local_hidden // 2
    up_bias_row = up_bias.astype(F32)[None]
    middle, normed_second, active_near, grad_hidden, bias_near = ran(
        first_up(
            residual, second_vectors, [then(attention[0])] + attention[1:],
            up_weight, up_bias_row, grad_active, half_hidden, local_hidden, 2 * tile,
        )
    )
    mixed_seen = gather_first(mixed_sent)
    active_far, grad_hidden, bias_far = ran(
        more_up(
            after(then(normed_second), early_left), up_weight, up_bias_row, grad_active,
            half_hidden, half_hidden, 2 * tile, grad_hidden, heavy=2,
        )
    )

    def reduce_over_dp(parts, *deps):
        lefts, row, rights = parts[0]
        head = after(then(lefts[0]), *deps)
        whole = ran(
            weight_grad([([head] + lefts[1:], row, rights)] + parts[1:], width // n_ctx, 1024)
        )
        return lax.psum_scatter(whole, "dp", scatter_dimension=0, tiled=True)

    def grad_normed_part(side):
        part = ran(
            mm(
                [after(then(grad_hidden), mixed_seen)], [up_weight], trans=True, start=side * (width // 2), size=width // 2, tile=512,
                out_dtype=BF16,
            )
        )
        return exchanged(part)

    normed_terms = [grad_normed_part(0), grad_normed_part(1)]
    near_rights = gather_rest(gather_first(active_near), order[-1], active_far)
    up_pieces = ran(spread_pieces(place, then(normed_second), heavy=1))
    down_parts = [reduce_over_dp([(early_left, 0, near_rights)])]
    grad_sent = after(grad_hidden, order[-1])
    up_left = spread_left(lax.optimization_barrier((up_pieces, order[-1]))[0])

    feed = ran(
        mm(
            [then(active_near), active_far],
            [(down_weight, None, 0), (down_weight, None, 1)], trans=True,
            start=0, size=width, tile=512, out_dtype=BF16, heavy=2,
        )
    )

    def tensor_scatter(values):
        total = mine(values).astype(F32)
        for k in range(1, n_tensor):
            piece = lax.dynamic_slice_in_dim(values, (tensor_place ^ k) * share, share, 0)
            total = total + xperm(piece, "tensor", k).astype(F32)
        return total

    feed_gate = order[-1]
    grad_blocks = gather_first(grad_sent)

    def added(terms):
        total = after(terms[0], order[-1]).astype(F32)
        for term in terms[1:]:
            total = total + term.astype(F32)
        return total

    grad_normed = jnp.concatenate([added(terms) for terms in normed_terms], axis=1)
    unit_two, inverse_two = normalized(middle)
    cot = after(cot_low, order[-1]).astype(F32)
    grad_middle = cot + norm_backward(grad_normed, unit_two, inverse_two, gain_two)
    grad_middle_low = grad_middle.astype(BF16)
    grad_mixed = ran(
        mm(
            [after(then(grad_middle_low), up_left[len(up_left) // 2])], [out_weight], trans=False,
            start=0, size=local_width, tile=1024, out_dtype=BF16, heavy=1,
        )
    )
    down_parts.append(
        reduce_over_dp([(early_left, 0, gather_ctx(active_far, feed_gate))], up_left)
    )
    own_gate = order[-1]
    mixed_all = gather_rest(mixed_seen, order[-1])
    grad_query, kv_near, kv_far = None, [], []
    for g in range(groups):
        grad_query, near, far = ran(
            attention_backward(
                slopes, after(then(query), mixed_all if g else []), grad_mixed, distance, stats[g],
                keyvals[g],
                g * group_heads, group_heads, grad_query, heavy=2 if g == 0 else 0,
            )
        )
        kv_near.append(near)
        kv_far.append(far)
    kv_received = [xperm(far, "ctx", 1) if n_ctx > 1 else None for far in kv_far]
    kv_near = after(kv_near, order[-1])

    partial = []
    for near, received in zip(kv_near, kv_received):
        blocks = [near[:, k].astype(F32) for k in range(near.shape[1])]
        if n_ctx > 1:
            blocks = [block + received[:, k].astype(F32) for k, block in enumerate(blocks)]
        partial.append(blocks)
    sent = [block.astype(BF16) for blocks in partial for block in blocks[len(blocks) // 2 :]]
    grad_all = gather_rest(grad_blocks, sent, own_gate)
    up_part = reduce_over_dp([(up_left, 0, grad_all)])
    up_gate = order[-1]
    late_pieces = ran(spread_pieces(place, then(grad_middle_low), heavy=2))
    late_left = spread_left(late_pieces)
    outputs = (mine(middle) + tensor_scatter(feed) + down_bias.astype(F32)).astype(BF16)

    grad_keys, grad_values = [], []
    for g, blocks in enumerate(partial):
        send_gate = up_gate if g else []
        for bit in reversed(ctx_bits()[:-1]):
            half = len(blocks) // 2
            got = [
                xperm(
                    after(block.astype(BF16), send_gate), "ctx", bit, lambda i, bit=bit: i > i ^ bit
                )
                for block in blocks[half:]
            ]
            blocks = [
                after(block, order[-1]) + term.astype(F32)
                for block, term in zip(blocks[:half], got)
            ]
        final = blocks[0].astype(BF16)
        grad_keys.append(final[0])
        grad_values.append(final[1])
    grad_keyvals = jnp.concatenate(grad_keys + grad_values, axis=1)
    gated = after(then(grad_keyvals), late_left)
    grad_first = ran(
        mm(
            [(grad_query, 0, local_width)] + [(gated, c, local_width) for c in range(2)],
            [(weight_in, c, 0) for c in range(3)], trans=True, start=0, size=width,
            tile=512, out_dtype=BF16, heavy=1,
        )
    )
    query_all = gather_ctx(after(grad_query, up_gate), order[-1])
    keyvals_all = gather_ctx(grad_keyvals, order[-1])
    joint_part = reduce_over_dp(
        [(late_left, 0, mixed_all), (early_left, 1, query_all), (early_left, 1, keyvals_all)],
        outputs,
    )
    grad_first_share = tensor_scatter(grad_first)
    unit_share, inverse_share = normalized(mine(inputs[0]).astype(F32))
    grad_from_first = norm_backward(grad_first_share, unit_share, inverse_share, gain_one)
    grad_middle_share = mine(grad_middle)
    input_grad = (grad_middle_share + grad_from_first).astype(BF16)

    def over_tokens(values):
        return jnp.sum(values, axis=0)

    grad_normed_share, unit_two_share = mine(grad_normed), mine(unit_two)
    sums = jnp.concatenate(
        [
            over_tokens(values).reshape(-1, local_width)
            for values in (
                grad_normed_share * unit_two_share,
                grad_normed_share,
                grad_middle_share,
                mine(cot),
                grad_first_share * unit_share,
                grad_first_share,
            )
        ]
    )
    count = sums.shape[0]
    sums = all_sum(sums, ("tensor",))
    sums = jnp.concatenate(
        [
            sums,
            over_tokens(grad_query.astype(F32))[None],
            over_tokens(grad_keyvals[:, local_width:].astype(F32))[None],
            jnp.concatenate([bias_near, bias_far], axis=1).reshape(-1, local_width),
        ]
    )
    sums = sum_shared(sums, "ctx", ("dp",))
    vectors = sums[:count].reshape(6, width)
    in_bias_grad = sums[count : count + 2]
    up_bias_grad = sums[count + 2 :].reshape(-1)

    down_weight_grad = jnp.concatenate([part.astype(F32) for part in down_parts], axis=1)
    up_weight_grad = up_part.astype(F32)
    out_weight_grad, in_weight_grad = widen_joint(joint_part, local_width)
    return (
        outputs[None],
        input_grad[None],
        vectors[4],
        vectors[5],
        in_weight_grad.transpose(1, 0, 2),
        in_bias_grad,
        out_weight_grad,
        vectors[2],
        vectors[0],
        vectors[1],
        up_weight_grad,
        up_bias_grad,
        down_weight_grad,
        vectors[3],
    )


def solution(mesh):
    return jax.shard_map(
        shards,
        mesh=mesh,
        in_specs=(
            P("dp", "ctx", None),
            P("dp", None),
            P(),
            P(),
            P(None, None, "tensor"),
            P(None, "tensor"),
            P(None, "tensor"),
            P(),
            P(),
            P(),
            P(None, "tensor"),
            P("tensor"),
            P(None, "tensor"),
            P(),
            P("dp", "ctx", None),
        ),
        out_specs=(
            P("dp", ("ctx", "tensor"), None),
            P("dp", ("ctx", "tensor"), None),
            P(),
            P(),
            P(("dp", "ctx"), None, "tensor"),
            P(None, "tensor"),
            P(("dp", "ctx"), "tensor"),
            P(),
            P(),
            P(),
            P(("dp", "ctx"), "tensor"),
            P("tensor"),
            P(("dp", "ctx"), "tensor"),
            P(),
        ),
        check_vma=False,
    )
```
